32 devices in a mesh: cohort: 4 (over y, core), cell: 8 (over z, x).
Axes of the slice: x: 2, y: 2, z: 4, core: 2. Of those that a mesh axis runs over, the one named last changes fastest.
Arguments:
- cohort_features: bfloat16 [2048, 128], P('cohort'), may hold values from -6 to 6
- cell_features: bfloat16 [4096, 128], P('cell'), may hold values from -6 to 6
- cohort_region: int32 [2048], P('cohort'), may hold values from 0 to 31
- cell_region: int32 [4096], P('cell'), may hold values from 0 to 31
- penalty: float32 [32, 32], replicated, may hold values from 0 to 2
- cohort_mass: float32 [2048], P('cohort'), may hold values from 0.5 to 2
- cell_mass: float32 [4096], P('cell'), may hold values from 0.25 to 1
- cohort_segment: int32 [2048], P('cohort'), may hold values from 0 to 31
- spend_merchant: int32 [2048, 1024], P('cohort', 'cell'), may hold values from 0 to 127
- spend_day: int32 [2048, 1024], P('cohort', 'cell'), may hold values from 0 to 63
- spend_amount: float32 [2048, 1024], P('cohort', 'cell'), may hold values from 0.05 to 0.5
Outputs:
- weights: float32 [2048], P('cohort')
- cell_scale: float32 [4096], P('cell')
- trend: float32 [64, 32, 1024], P('cohort', None, 'cell')
The draws below stay inside these ranges and needn't reach their ends.
All inputs are finite; a program needn't handle non-finite values.
Results may differ from the reference program's by a relative error of at most 0.0003.
Values sent between devices are 32-bit elements; how exact they have to be, the bound alone decides.
No kernel may reach another device: no remote copies, remote signals or barrier semaphores. Data moves between devices by JAX's collectives and lax.ppermute only.
A program may use at most 64 MiB of HBM per device.

```python
import math
import jax
import jax.numpy as jnp
import numpy as np
from jax import lax

COH_DEV = 512
FEAT = 128
REGIONS = 32
ITERS = 2
SEG = 32
MERCH_DEV = 128
DAYS = 64
TXN_COH = 128
COHORTS = 2048
CELLS = 4096
MERCHANTS = 1024
RECORDS = 1024
N_COHORT = 4


def plant(array, stream_key, low, top_value):
    longest = array.shape.index(max(array.shape))
    spots = []
    for shift in (0, 1):
        where = [jax.random.randint(jax.random.fold_in(stream_key, axis), (), 0, length) for axis, length in enumerate(array.shape)]
        where[longest] = (where[longest] + shift) % array.shape[longest]
        spots.append(tuple(where))
    return array.at[spots[0]].set(low).at[spots[1]].set(top_value)


def level_of(stream_key, dims, pieces, least, largest):
    def one(dim, blocks):
        steps = jax.random.uniform(jax.random.fold_in(jax.random.fold_in(stream_key, 6), dim), (blocks,), jnp.float32, least / len(pieces), largest / len(pieces))
        return jnp.repeat(jnp.exp(steps), dims[dim] // blocks).reshape((-1,) + (1,) * (len(dims) - dim - 1))

    factor_of = one(*pieces[0])
    for cut in pieces[1:]:
        factor_of = factor_of * one(*cut)
    return factor_of


def gaussian(own_key, extent, spread, limit, split=(), dtype=jnp.bfloat16):
    values = spread * jax.random.normal(own_key, extent, jnp.float32)
    if split:
        values = values * level_of(own_key, extent, split, -0.22, 0.18)
    return jnp.clip(values, -limit, limit).astype(dtype)


def setup_inputs(seed: int = 0) -> dict:
    key_list = jax.random.split(jax.random.key(seed), 12)
    return {
        "cohort_features": gaussian(key_list[0], (COHORTS, FEAT), 1.0, 6.0, ((0, 4),)),
        "cell_features": gaussian(key_list[1], (CELLS, FEAT), 1.0, 6.0, ((0, 8),)),
        "cohort_region": plant(jax.random.randint(key_list[2], (COHORTS,), 0, REGIONS), jax.random.fold_in(key_list[2], 1), 0, REGIONS - 1).astype(jnp.int32),
        "cell_region": plant(jax.random.randint(key_list[3], (CELLS,), 0, REGIONS), jax.random.fold_in(key_list[3], 1), 0, REGIONS - 1).astype(jnp.int32),
        "penalty": jnp.clip(jax.random.uniform(key_list[4], (REGIONS, REGIONS), jnp.float32, 0.0, 2.0), 0.0, 2.0),
        "cohort_mass": jnp.clip(jnp.exp(math.log(2.0) - 1.3862944 * jax.random.uniform(key_list[5], (COHORTS,), jnp.float32) ** level_of(key_list[5], (COHORTS,), ((0, 4),), -0.2, 0.2)), 0.5, 2.0),
        "cell_mass": jnp.clip(jnp.exp(math.log(1.0) - 1.3862944 * jax.random.uniform(key_list[6], (CELLS,), jnp.float32) ** level_of(key_list[6], (CELLS,), ((0, 8),), -0.2, 0.2)), 0.25, 1.0),
        "cohort_segment": plant(jax.random.randint(key_list[7], (COHORTS,), 0, SEG), jax.random.fold_in(key_list[7], 1), 0, SEG - 1).astype(jnp.int32),
        "spend_merchant": plant(jax.random.randint(key_list[8], (COHORTS, RECORDS), 0, MERCH_DEV), jax.random.fold_in(key_list[8], 1), 0, MERCH_DEV - 1).astype(jnp.int32),
        "spend_day": plant(jax.random.randint(key_list[9], (COHORTS, RECORDS), 0, DAYS), jax.random.fold_in(key_list[9], 1), 0, DAYS - 1).astype(jnp.int32),
        "spend_amount": jnp.clip(jnp.exp(math.log(0.5) - 2.3025851 * jax.random.uniform(key_list[10], (COHORTS, RECORDS), jnp.float32) ** level_of(key_list[10], (COHORTS, RECORDS), ((0, 4), (1, 8)), -0.2, 0.2)), 0.05, 0.5),
    }


half_span = 11

def filter_table(day_count):
    outer = 13.0
    coeffs = []
    for offset_days in range(-half_span, half_span + 1):
        sq = float(offset_days * offset_days)
        top = 315.0 * ((outer - 1) ** 2 - sq) * (outer ** 2 - sq) * ((outer + 1) ** 2 - sq) * (3 * outer ** 2 - 16 - 11 * sq)
        bottom = 8 * outer * (outer ** 2 - 1) * (4 * outer ** 2 - 1) * (4 * outer ** 2 - 9) * (4 * outer ** 2 - 25)
        coeffs.append(top / bottom)
    matrix = np.zeros((day_count, day_count))
    for row_day in range(day_count):
        for offset_days in range(-half_span, half_span + 1):
            col_day = row_day + offset_days
            if 0 <= col_day < day_count:
                matrix[row_day, col_day] = coeffs[offset_days + half_span]
        matrix[row_day] = matrix[row_day] / matrix[row_day].sum()
    return matrix

def penalty_block(row_regions, col_regions, penalty):
    region_count = penalty.shape[0]
    row_onehot = (row_regions[:, None] == jnp.arange(region_count)[None, :]).astype(jnp.float32)
    col_onehot = (jnp.arange(region_count)[:, None] == col_regions[None, :]).astype(jnp.float32)
    rowpen = jnp.dot(row_onehot, penalty, precision=lax.Precision.HIGHEST)
    return jnp.dot(rowpen, col_onehot, precision=lax.Precision.HIGHEST)

def gibbs(row_feats, col_feats, pen_block):
    inv_root = 1.0 / math.sqrt(row_feats.shape[1])
    inner = jnp.dot(row_feats, col_feats.T, preferred_element_type=jnp.float32)
    return jnp.exp(inner * inv_root - pen_block)

def reference(cohort_features, cell_features, cohort_region, cell_region, penalty, cohort_mass, cell_mass, cohort_segment, spend_merchant, spend_day, spend_amount):
    feat_blocks = cohort_features.reshape(N_COHORT, COH_DEV, FEAT)
    region_blocks = cohort_region.reshape(N_COHORT, COH_DEV)

    def block_kernel(feats, regions):
        return gibbs(feats, cell_features, penalty_block(regions, cell_region, penalty))

    def rows_apply(cell_scale):

        def one_block(item):
            return jnp.dot(block_kernel(item[0], item[1]), cell_scale, precision=lax.Precision.HIGHEST)
        return lax.map(one_block, (feat_blocks, region_blocks)).reshape(-1)

    def cols_apply(cohort_scale):
        scale_blocks = cohort_scale.reshape(N_COHORT, COH_DEV)

        def one_block(running, item):
            kernel = block_kernel(item[0], item[1])
            return (running + jnp.dot(item[2], kernel, precision=lax.Precision.HIGHEST), None)
        running, _ = lax.scan(one_block, jnp.zeros((CELLS,), jnp.float32), (feat_blocks, region_blocks, scale_blocks))
        return running
    cell_scale = jnp.ones((CELLS,), jnp.float32)
    cohort_scale = cohort_mass
    for iteration in range(ITERS):
        cohort_scale = cohort_mass / rows_apply(cell_scale)
        cell_scale = cell_mass / cols_apply(cohort_scale)
    weights = cohort_scale * rows_apply(cell_scale)
    column_block = (jnp.arange(RECORDS) // TXN_COH).astype(jnp.int32)
    bin_total = DAYS * SEG * MERCHANTS

    def spend_block(running, item):
        block_weights, merchants, days, amounts, segment_of = item
        merchant_global = column_block[None, :] * MERCH_DEV + merchants
        bin_index = (days * SEG + segment_of[:, None]) * MERCHANTS + merchant_global
        values = block_weights[:, None] * amounts
        return (running + jax.ops.segment_sum(values.reshape(-1), bin_index.reshape(-1), num_segments=bin_total), None)
    spend_bins, _ = lax.scan(spend_block, jnp.zeros((bin_total,), jnp.float32), (weights.reshape(N_COHORT, COH_DEV), spend_merchant.reshape(N_COHORT, COH_DEV, RECORDS), spend_day.reshape(N_COHORT, COH_DEV, RECORDS), spend_amount.reshape(N_COHORT, COH_DEV, RECORDS), cohort_segment.reshape(N_COHORT, COH_DEV)))
    henderson = jnp.asarray(filter_table(DAYS), jnp.float32)
    trend = jnp.dot(henderson, spend_bins.reshape(DAYS, -1), precision=lax.Precision.HIGHEST).reshape(DAYS, SEG, MERCHANTS)
    return (weights, cell_scale, trend)
```

```python
import functools
import math

import jax
import jax.numpy as jnp
import numpy as np
from jax import lax
from jax.experimental import pallas as pl
from jax.experimental.pallas import tpu as pltpu
from jax.sharding import PartitionSpec as P

ITERS = 2
SEG = 32
MERCH_DEV = 128
DAYS = 64
LANES = 128
GROUP = 16

half_span = 11

f32 = jnp.float32
bf16 = jnp.bfloat16
VMEM = pl.BlockSpec(memory_space=pltpu.VMEM)
ANY = pl.BlockSpec(memory_space=pl.ANY)
PARAMS = pltpu.CompilerParams(vmem_limit_bytes=20 * 2**20)


def filter_table(day_count):
    outer = 13.0
    coeffs = []
    for offset_days in range(-half_span, half_span + 1):
        sq = float(offset_days * offset_days)
        top = (
            315.0
            * ((outer - 1) ** 2 - sq)
            * (outer**2 - sq)
            * ((outer + 1) ** 2 - sq)
            * (3 * outer**2 - 16 - 11 * sq)
        )
        bottom = (
            8
            * outer
            * (outer**2 - 1)
            * (4 * outer**2 - 1)
            * (4 * outer**2 - 9)
            * (4 * outer**2 - 25)
        )
        coeffs.append(top / bottom)
    matrix = np.zeros((day_count, day_count))
    for row_day in range(day_count):
        for offset_days in range(-half_span, half_span + 1):
            col_day = row_day + offset_days
            if 0 <= col_day < day_count:
                matrix[row_day, col_day] = coeffs[offset_days + half_span]
        matrix[row_day] = matrix[row_day] / matrix[row_day].sum()
    return matrix


def split2(x):
    hi = x.astype(bf16)
    return hi, (x - hi.astype(f32)).astype(bf16)


def split_rows(x):
    hi = x.astype(bf16)
    rest = x - hi.astype(f32)
    mid = rest.astype(bf16)
    low = (rest - mid.astype(f32)).astype(bf16)
    return jnp.concatenate([hi, mid, low, jnp.zeros((5, x.shape[1]), bf16)], 0)


def cols_of(u, khi_ref, klo_ref):
    rows = split_rows(u)
    out = jnp.dot(rows, khi_ref[...], preferred_element_type=f32)
    out = out + jnp.dot(rows, klo_ref[...], preferred_element_type=f32)
    return jnp.sum(out, axis=0, keepdims=True)


def rows_of(v, khi_ref, klo_ref):
    rows = split_rows(v)
    dims = (((1,), (1,)), ((), ()))
    out = lax.dot_general(rows, khi_ref[...], dims, preferred_element_type=f32)
    out = out + lax.dot_general(rows, klo_ref[...], dims, preferred_element_type=f32)
    return jnp.sum(out, axis=0, keepdims=True)


def gibbs_body(x_ref, y_ref, rr_ref, cr_ref, pen_ref, khi_ref, klo_ref, r_ref):
    n, m = x_ref.shape[0], y_ref.shape[0]
    regions = pen_ref.shape[0]
    inv_root = 1.0 / math.sqrt(x_ref.shape[1])
    dims = (((1,), (1,)), ((), ()))
    inner = lax.dot_general(x_ref[...], y_ref[...], dims, preferred_element_type=f32)
    row_hot = (lax.broadcasted_iota(jnp.int32, (regions, n), 0) == rr_ref[...]).astype(f32).astype(bf16)
    col_hot = (lax.broadcasted_iota(jnp.int32, (regions, m), 0) == cr_ref[...]).astype(f32).astype(bf16)
    phi, plo = split2(pen_ref[...])
    qhi = jnp.dot(phi, col_hot, preferred_element_type=f32).astype(bf16)
    qlo = jnp.dot(plo, col_hot, preferred_element_type=f32).astype(bf16)
    pen = lax.dot_general(
        jnp.concatenate([row_hot, row_hot], 0),
        jnp.concatenate([qhi, qlo], 0),
        (((0,), (0,)), ((), ())),
        preferred_element_type=f32,
    )
    hi, lo = split2(jnp.exp(inner * inv_root - pen))
    khi_ref[...] = hi
    klo_ref[...] = lo
    r_ref[...] = rows_of(jnp.ones((1, m), f32), khi_ref, klo_ref)


def gibbs_call(x, y, rr, cr, penalty):
    n, m = x.shape[0], y.shape[0]
    return pl.pallas_call(
        gibbs_body,
        in_specs=[VMEM] * 5,
        out_specs=[VMEM] * 3,
        out_shape=[pltpu.VMEM((n, m), bf16), pltpu.VMEM((n, m), bf16), pltpu.VMEM((1, n), f32)],
        compiler_params=PARAMS,
        name="gibbs",
    )(x, y, rr, cr, penalty)


def step_body(apply, parts, mass_ref, khi_ref, klo_ref, *refs):
    part_refs, out_refs = refs[:parts], refs[-2:]
    total = part_refs[0][...]
    for ref in part_refs[1:]:
        total = total + ref[...]
    scale = mass_ref[...] / total
    out_refs[0][...] = scale
    out_refs[1][...] = apply(scale, khi_ref, klo_ref)


def step_call(apply, name, mass, khi, klo, partials, tokens):
    out = khi.shape[1] if apply is cols_of else khi.shape[0]
    return pl.pallas_call(
        functools.partial(step_body, apply, len(partials)),
        in_specs=[VMEM] * (3 + len(partials)) + [ANY] * len(tokens),
        out_specs=[VMEM] * 2,
        out_shape=[pltpu.VMEM(mass.shape, f32), pltpu.VMEM((1, out), f32)],
        compiler_params=PARAMS,
        name=name,
    )(mass, khi, klo, *partials, *tokens)


def table_body(first, count, f_ref, m_ref, d_ref, a_ref, after_ref, hi_ref, lo_ref, tok_ref):
    t_count = f_ref.shape[0]
    filt = f_ref[...]
    merch_iota = lax.broadcasted_iota(jnp.int32, (MERCH_DEV, LANES), 0).astype(f32).astype(bf16)
    one, zero = jnp.ones((MERCH_DEV, LANES), bf16), jnp.zeros((MERCH_DEV, LANES), bf16)

    def group(step, carry):
        start = pl.multiple_of(step * GROUP, GROUP)
        rows_in = pl.ds(first + start, GROUP)
        merch = m_ref[rows_in, :].astype(f32).astype(bf16)
        days = d_ref[rows_in, :]
        amounts = a_ref[rows_in, :]
        tables = []
        for i in range(GROUP):
            day = jnp.broadcast_to(days[i : i + 1, :], (t_count, LANES))
            coef = jnp.take_along_axis(filt, day, axis=1, mode="promise_in_bounds")
            chi, clo = split2(coef * amounts[i : i + 1, :])
            hot = jnp.where(merch_iota == merch[i : i + 1, :], one, zero)
            both = lax.dot_general(
                jnp.concatenate([chi, clo], 0), hot, (((1,), (1,)), ((), ())), preferred_element_type=f32
            )
            tables.append(both[:t_count] + both[t_count:])
        hi, lo = split2(jnp.swapaxes(jnp.stack(tables, 0), 0, 1))
        hi_ref[:, pl.ds(start, GROUP), :] = hi
        lo_ref[:, pl.ds(start, GROUP), :] = lo
        return carry

    lax.fori_loop(0, count // GROUP, group, 0)
    tok_ref[...] = jnp.zeros_like(tok_ref)


def table_call(filt, merchants, days, amounts, first, count, after):
    t_count = filt.shape[0]
    hi, lo, token = pl.pallas_call(
        functools.partial(table_body, first, count),
        in_specs=[VMEM] * 4 + [ANY],
        out_specs=[VMEM] * 3,
        out_shape=[pltpu.VMEM((t_count, count, LANES), bf16)] * 2 + [pltpu.VMEM((8, LANES), f32)],
        compiler_params=PARAMS,
        cost_estimate=pl.CostEstimate(
            flops=4 * count * t_count * 128 * 128, transcendentals=0, bytes_accessed=count * 100000
        ),
        name="tables",
    )(filt, merchants, days, amounts, after)
    return (hi, lo), token


def spread_body(t_first, t_count, counts, parts, seg_ref, u_ref, *refs):
    part_refs = refs[:parts]
    pair_refs = refs[parts : parts + 2 * len(counts)]
    o_ref, w_ref = refs[-2:]
    total = part_refs[0][...]
    for ref in part_refs[1:]:
        total = total + ref[...]
    w = u_ref[...] * total
    w_ref[...] = w
    n = w.shape[1]
    hot = lax.broadcasted_iota(jnp.int32, (SEG, n), 0) == seg_ref[...]
    whi, wlo = split2(jnp.where(hot, w, 0.0))
    both = jnp.concatenate([whi, wlo], 0)
    for t in range(t_first, t_first + t_count, 2):
        hi = jnp.concatenate(
            [jnp.concatenate([pair_refs[2 * k][t + q] for k in range(len(counts))], 0) for q in range(2)], 1
        )
        lo = jnp.concatenate(
            [jnp.concatenate([pair_refs[2 * k + 1][t + q] for k in range(len(counts))], 0) for q in range(2)], 1
        )
        p = jnp.dot(both, hi, preferred_element_type=f32)
        q = jnp.dot(whi, lo, preferred_element_type=f32)
        out = p[:SEG] + p[SEG:] + q
        o_ref[t - t_first] = out[:, :LANES]
        o_ref[t - t_first + 1] = out[:, LANES:]


def spread_call(seg, u, partials, pairs, t_first, t_count, tokens):
    counts = [hi.shape[1] for hi, _ in pairs]
    flat = [ref for pair in pairs for ref in pair]
    return pl.pallas_call(
        functools.partial(spread_body, t_first, t_count, counts, len(partials)),
        in_specs=[VMEM] * (2 + len(partials) + len(flat)) + [ANY] * len(tokens),
        out_specs=[VMEM] * 2,
        out_shape=[
            pltpu.VMEM((t_count, SEG, LANES), f32),
            jax.ShapeDtypeStruct(u.shape, f32),
        ],
        compiler_params=PARAMS,
        name="spread",
    )(seg, u, *partials, *flat, *tokens)


def swap(x, axis, size, mask):
    return lax.ppermute(x, axis, [(i, i ^ mask) for i in range(size)])


def shift(x, axis, size, pair, step):
    blocks = size // pair
    return lax.ppermute(
        x, axis, [(b * pair + r, ((b + step) % blocks) * pair + r) for b in range(blocks) for r in range(pair)]
    )


def per_device(
    n_cohort,
    n_cell,
    cohort_features,
    cell_features,
    cohort_region,
    cell_region,
    penalty,
    cohort_mass,
    cell_mass,
    cohort_segment,
    spend_merchant,
    spend_day,
    spend_amount,
):
    n = cohort_features.shape[0]
    row = lambda x: x.reshape(1, -1)
    t_dev = DAYS // n_cohort
    n_y = n_cohort // 2
    table = np.zeros((n_cohort, DAYS, LANES), np.float32)
    henderson = filter_table(DAYS)
    for me in range(n_cohort):
        y, c = divmod(me, 2)
        rows = []
        for core in (1 - c, c):
            for step in range(1, n_y + 1):
                dest = ((y + step) % n_y) * 2 + core
                rows.extend(range(dest * t_dev, (dest + 1) * t_dev))
        table[me, :, :DAYS] = henderson[rows]
    filt = lax.dynamic_index_in_dim(jnp.asarray(table), lax.axis_index("cohort"), 0, keepdims=False)

    windows = 3 * ITERS + 2
    state = {"first": 0, "left": windows}
    pairs = []

    def fill(after, weight):
        state["left"] -= 1
        first = state["first"]
        count = n - first if state["left"] == 0 else min(n - first, weight * GROUP * n // 512)
        if count <= 0:
            return []
        state["first"] = first + count
        pair, token = table_call(filt, spend_merchant, spend_day, spend_amount, first, count, after)
        pairs.append(pair)
        return [token]

    def over_cell(partial):
        other = swap(partial, "cell", n_cell, 1)
        tokens = fill(partial, 3)
        if tokens:
            partial, other, _ = lax.optimization_barrier((partial, other, tokens[0]))
        partial = partial + other
        others = [shift(partial, "cell", n_cell, 2, k) for k in range(1, n_cell // 2)]
        return [partial] + others, fill(partial, 5)

    def over_cohort(partial):
        others = [shift(partial, "cohort", n_cohort, 1, k) for k in range(1, n_cohort)]
        return [partial] + others, fill(partial, 4)

    khi, klo, partial = gibbs_call(cohort_features, cell_features, row(cohort_region), row(cell_region), penalty)
    for _ in range(ITERS):
        partials, tokens = over_cell(partial)
        cohort_scale, partial = step_call(cols_of, "cols", row(cohort_mass), khi, klo, partials, tokens)
        partials, tokens = over_cohort(partial)
        cell_scale, partial = step_call(rows_of, "rows", row(cell_mass), khi, klo, partials, tokens)
    partials, tokens = over_cell(partial)
    half = DAYS // 2
    seg = row(cohort_segment)
    away, weights = spread_call(seg, cohort_scale, partials, pairs, 0, half, tokens)
    came = swap(away, "cohort", n_cohort, 1)
    mine, _ = spread_call(seg, cohort_scale, partials, pairs, half, half, tokens)
    mine = mine + came
    out = mine[(n_y - 1) * t_dev :]
    for step in range(1, n_y):
        out = out + shift(mine[(step - 1) * t_dev : step * t_dev], "cohort", n_cohort, 2, step)
    return (weights.reshape(-1), cell_scale.reshape(-1), out)


def solution(mesh):
    return jax.shard_map(
        functools.partial(per_device, mesh.shape["cohort"], mesh.shape["cell"]),
        mesh=mesh,
        in_specs=(
            P("cohort", None),
            P("cell", None),
            P("cohort"),
            P("cell"),
            P(),
            P("cohort"),
            P("cell"),
            P("cohort"),
            P("cohort", "cell"),
            P("cohort", "cell"),
            P("cohort", "cell"),
        ),
        out_specs=(P("cohort"), P("cell"), P("cohort", None, "cell")),
        check_vma=False,
    )
```

```python
import functools
import math

import jax
import jax.numpy as jnp
import numpy as np
from jax import lax
from jax.experimental import pallas as pl
from jax.experimental.pallas import tpu as pltpu
from jax.sharding import PartitionSpec as P

ITERS = 2
SEG = 32
MERCH_DEV = 128
DAYS = 64
LANES = 128
GROUP = 16
UNROLL = 64

half_span = 11

f32 = jnp.float32
bf16 = jnp.bfloat16
VMEM = pl.BlockSpec(memory_space=pltpu.VMEM)
ANY = pl.BlockSpec(memory_space=pl.ANY)
PARAMS = pltpu.CompilerParams(vmem_limit_bytes=20 * 2**20)


def filter_table(day_count):
    outer = 13.0
    coeffs = []
    for offset_days in range(-half_span, half_span + 1):
        sq = float(offset_days * offset_days)
        top = (
            315.0
            * ((outer - 1) ** 2 - sq)
            * (outer**2 - sq)
            * ((outer + 1) ** 2 - sq)
            * (3 * outer**2 - 16 - 11 * sq)
        )
        bottom = (
            8
            * outer
            * (outer**2 - 1)
            * (4 * outer**2 - 1)
            * (4 * outer**2 - 9)
            * (4 * outer**2 - 25)
        )
        coeffs.append(top / bottom)
    matrix = np.zeros((day_count, day_count))
    for row_day in range(day_count):
        for offset_days in range(-half_span, half_span + 1):
            col_day = row_day + offset_days
            if 0 <= col_day < day_count:
                matrix[row_day, col_day] = coeffs[offset_days + half_span]
        matrix[row_day] = matrix[row_day] / matrix[row_day].sum()
    return matrix


def split2(x):
    hi = x.astype(bf16)
    return hi, (x - hi.astype(f32)).astype(bf16)


def split_rows(x):
    hi = x.astype(bf16)
    rest = x - hi.astype(f32)
    mid = rest.astype(bf16)
    low = (rest - mid.astype(f32)).astype(bf16)
    return jnp.concatenate([hi, mid, low, jnp.zeros((5, x.shape[1]), bf16)], 0)


def cols_of(u, khi_ref, klo_ref):
    rows = split_rows(u)
    out = jnp.dot(rows, khi_ref[...], preferred_element_type=f32)
    out = out + jnp.dot(rows, klo_ref[...], preferred_element_type=f32)
    return jnp.sum(out, axis=0, keepdims=True)


def rows_of(v, khi_ref, klo_ref):
    rows = split_rows(v)
    dims = (((1,), (1,)), ((), ()))
    out = lax.dot_general(rows, khi_ref[...], dims, preferred_element_type=f32)
    out = out + lax.dot_general(rows, klo_ref[...], dims, preferred_element_type=f32)
    return jnp.sum(out, axis=0, keepdims=True)


def gibbs_body(x_hbm, y_hbm, rr_hbm, cr_hbm, pen_hbm, f_hbm, m_hbm, d_hbm, a_hbm, *refs):
    khi_ref, klo_ref, r_ref, f_ref, m_ref, d_ref, a_ref = refs[:7]
    x_ref, y_ref, rr_ref, cr_ref, pen_ref, sems = refs[7:]
    me = lax.axis_index("cohort")
    copies = [
        pltpu.make_async_copy(src, dst, sems.at[k])
        for k, (src, dst) in enumerate(
            (
                (x_hbm, x_ref),
                (y_hbm, y_ref),
                (rr_hbm, rr_ref),
                (cr_hbm, cr_ref),
                (pen_hbm, pen_ref),
                (f_hbm.at[me], f_ref),
                (m_hbm, m_ref),
                (d_hbm, d_ref),
                (a_hbm, a_ref),
            )
        )
    ]
    for copy in copies:
        copy.start()
    for copy in copies[:5]:
        copy.wait()
    n, m = x_ref.shape[0], y_ref.shape[0]
    regions = pen_ref.shape[0]
    inv_root = 1.0 / math.sqrt(x_ref.shape[1])
    dims = (((1,), (1,)), ((), ()))
    inner = lax.dot_general(x_ref[...], y_ref[...], dims, preferred_element_type=f32)
    row_hot = (lax.broadcasted_iota(jnp.int32, (regions, n), 0) == rr_ref[...]).astype(f32).astype(bf16)
    col_hot = (lax.broadcasted_iota(jnp.int32, (regions, m), 0) == cr_ref[...]).astype(f32).astype(bf16)
    phi, plo = split2(pen_ref[...])
    qhi = jnp.dot(phi, col_hot, preferred_element_type=f32).astype(bf16)
    qlo = jnp.dot(plo, col_hot, preferred_element_type=f32).astype(bf16)
    pen = lax.dot_general(
        jnp.concatenate([row_hot, row_hot], 0),
        jnp.concatenate([qhi, qlo], 0),
        (((0,), (0,)), ((), ())),
        preferred_element_type=f32,
    )
    hi, lo = split2(jnp.exp(inner * inv_root - pen))
    khi_ref[...] = hi
    klo_ref[...] = lo
    r_ref[...] = rows_of(jnp.ones((1, m), f32), khi_ref, klo_ref)
    for copy in copies[5:]:
        copy.wait()


def gibbs_call(x, y, rr, cr, penalty, table, merchants, days, amounts):
    n, m = x.shape[0], y.shape[0]
    args = (x, y, rr, cr, penalty)
    records = (merchants, days, amounts)
    return pl.pallas_call(
        gibbs_body,
        in_specs=[ANY] * 9,
        out_specs=[VMEM] * 7,
        out_shape=[pltpu.VMEM((n, m), bf16), pltpu.VMEM((n, m), bf16), pltpu.VMEM((1, n), f32)]
        + [pltpu.VMEM(table.shape[1:], f32)]
        + [pltpu.VMEM(r.shape, r.dtype) for r in records],
        scratch_shapes=[pltpu.VMEM(r.shape, r.dtype) for r in args] + [pltpu.SemaphoreType.DMA((9,))],
        compiler_params=PARAMS,
        name="gibbs",
    )(*args, table, *records)


def step_body(apply, parts, mass_ref, khi_ref, klo_ref, *refs):
    part_refs, out_refs = refs[:parts], refs[-2:]
    total = part_refs[0][...]
    for ref in part_refs[1:]:
        total = total + ref[...]
    scale = mass_ref[...] / total
    out_refs[0][...] = scale
    out_refs[1][...] = apply(scale, khi_ref, klo_ref)


def step_call(apply, name, mass, khi, klo, partials, tokens):
    out = khi.shape[1] if apply is cols_of else khi.shape[0]
    return pl.pallas_call(
        functools.partial(step_body, apply, len(partials)),
        in_specs=[VMEM] * (3 + len(partials)) + [ANY] * len(tokens),
        out_specs=[VMEM] * 2,
        out_shape=[pltpu.VMEM(mass.shape, f32), pltpu.VMEM((1, out), f32)],
        compiler_params=PARAMS,
        name=name,
    )(mass, khi, klo, *partials, *tokens)


def table_body(first, count, f_ref, m_ref, d_ref, a_ref, after_ref, hi_ref, lo_ref, tok_ref):
    t_count = f_ref.shape[0]
    filt = f_ref[...]
    merch_iota = lax.broadcasted_iota(jnp.int32, (MERCH_DEV, LANES), 0).astype(f32).astype(bf16)
    one, zero = jnp.ones((MERCH_DEV, LANES), bf16), jnp.zeros((MERCH_DEV, LANES), bf16)

    size = math.gcd(count, UNROLL)

    def group(step, carry):
        start = pl.multiple_of(step * size, size)
        rows_in = pl.ds(first + start, size)
        merch = m_ref[rows_in, :].astype(f32).astype(bf16)
        days = d_ref[rows_in, :]
        amounts = a_ref[rows_in, :]
        tables = []
        for i in range(size):
            day = jnp.broadcast_to(days[i : i + 1, :], (t_count, LANES))
            coef = jnp.take_along_axis(filt, day, axis=1, mode="promise_in_bounds")
            chi, clo = split2(coef * amounts[i : i + 1, :])
            hot = jnp.where(merch_iota == merch[i : i + 1, :], one, zero)
            both = lax.dot_general(
                jnp.concatenate([chi, clo], 0), hot, (((1,), (1,)), ((), ())), preferred_element_type=f32
            )
            tables.append(both[:t_count] + both[t_count:])
        hi, lo = split2(jnp.swapaxes(jnp.stack(tables, 0), 0, 1))
        hi_ref[:, pl.ds(start, size), :] = hi
        lo_ref[:, pl.ds(start, size), :] = lo
        return carry

    lax.fori_loop(0, count // size, group, 0)
    tok_ref[...] = jnp.zeros_like(tok_ref)


def table_call(filt, merchants, days, amounts, first, count, after):
    t_count = filt.shape[0]
    hi, lo, token = pl.pallas_call(
        functools.partial(table_body, first, count),
        in_specs=[VMEM] * 4 + [ANY],
        out_specs=[VMEM] * 3,
        out_shape=[pltpu.VMEM((t_count, count, LANES), bf16)] * 2 + [pltpu.VMEM((8, LANES), f32)],
        compiler_params=PARAMS,
        cost_estimate=pl.CostEstimate(
            flops=4 * count * t_count * 128 * 128, transcendentals=0, bytes_accessed=count * 100000
        ),
        name="tables",
    )(filt, merchants, days, amounts, after)
    return (hi, lo), token


def spread_body(t_first, t_count, counts, parts, seg_ref, u_ref, *refs):
    part_refs = refs[:parts]
    pair_refs = refs[parts : parts + 2 * len(counts)]
    o_ref, w_ref = refs[-2:]
    total = part_refs[0][...]
    for ref in part_refs[1:]:
        total = total + ref[...]
    w = u_ref[...] * total
    w_ref[...] = w
    n = w.shape[1]
    hot = lax.broadcasted_iota(jnp.int32, (SEG, n), 0) == seg_ref[...]
    whi, wlo = split2(jnp.where(hot, w, 0.0))
    both = jnp.concatenate([whi, wlo], 0)
    for t in range(t_first, t_first + t_count, 2):
        hi = jnp.concatenate(
            [jnp.concatenate([pair_refs[2 * k][t + q] for k in range(len(counts))], 0) for q in range(2)], 1
        )
        lo = jnp.concatenate(
            [jnp.concatenate([pair_refs[2 * k + 1][t + q] for k in range(len(counts))], 0) for q in range(2)], 1
        )
        p = jnp.dot(both, hi, preferred_element_type=f32)
        q = jnp.dot(whi, lo, preferred_element_type=f32)
        out = p[:SEG] + p[SEG:] + q
        o_ref[t - t_first] = out[:, :LANES]
        o_ref[t - t_first + 1] = out[:, LANES:]


def spread_call(seg, u, partials, pairs, t_first, t_count, tokens):
    counts = [hi.shape[1] for hi, _ in pairs]
    flat = [ref for pair in pairs for ref in pair]
    return pl.pallas_call(
        functools.partial(spread_body, t_first, t_count, counts, len(partials)),
        in_specs=[VMEM] * (2 + len(partials) + len(flat)) + [ANY] * len(tokens),
        out_specs=[VMEM] * 2,
        out_shape=[
            pltpu.VMEM((t_count, SEG, LANES), f32),
            jax.ShapeDtypeStruct(u.shape, f32),
        ],
        compiler_params=PARAMS,
        name="spread",
    )(seg, u, *partials, *flat, *tokens)


def swap(x, axis, size, mask):
    return lax.ppermute(x, axis, [(i, i ^ mask) for i in range(size)])


def shift(x, axis, size, pair, step):
    blocks = size // pair
    return lax.ppermute(
        x, axis, [(b * pair + r, ((b + step) % blocks) * pair + r) for b in range(blocks) for r in range(pair)]
    )


def per_device(
    n_cohort,
    n_cell,
    cohort_features,
    cell_features,
    cohort_region,
    cell_region,
    penalty,
    cohort_mass,
    cell_mass,
    cohort_segment,
    spend_merchant,
    spend_day,
    spend_amount,
):
    n = cohort_features.shape[0]
    row = lambda x: x.reshape(1, -1)
    t_dev = DAYS // n_cohort
    n_y = n_cohort // 2
    table = np.zeros((n_cohort, DAYS, LANES), np.float32)
    henderson = filter_table(DAYS)
    for me in range(n_cohort):
        y, c = divmod(me, 2)
        rows = []
        for core in (1 - c, c):
            for step in range(1, n_y + 1):
                dest = ((y + step) % n_y) * 2 + core
                rows.extend(range(dest * t_dev, (dest + 1) * t_dev))
        table[me, :, :DAYS] = henderson[rows]

    windows = 3 * ITERS + 2
    state = {"first": 0, "left": windows}
    pairs = []

    def fill(after, weight):
        state["left"] -= 1
        first = state["first"]
        count = n - first if state["left"] == 0 else min(n - first, weight * GROUP * n // 512)
        if count <= 0:
            return []
        state["first"] = first + count
        pair, token = table_call(filt, spend_merchant, spend_day, spend_amount, first, count, after)
        pairs.append(pair)
        return [token]

    def over_cell(partial):
        other = swap(partial, "cell", n_cell, 1)
        tokens = fill(partial, 4)
        if tokens:
            partial, other, _ = lax.optimization_barrier((partial, other, tokens[0]))
        partial = partial + other
        others = [shift(partial, "cell", n_cell, 2, k) for k in range(1, n_cell // 2)]
        return [partial] + others, fill(partial, 4)

    def over_cohort(partial):
        others = [shift(partial, "cohort", n_cohort, 1, k) for k in range(1, n_cohort)]
        return [partial] + others, fill(partial, 4)

    khi, klo, partial, filt, spend_merchant, spend_day, spend_amount = gibbs_call(
        cohort_features,
        cell_features,
        row(cohort_region),
        row(cell_region),
        penalty,
        jnp.asarray(table),
        spend_merchant,
        spend_day,
        spend_amount,
    )
    for _ in range(ITERS):
        partials, tokens = over_cell(partial)
        cohort_scale, partial = step_call(cols_of, "cols", row(cohort_mass), khi, klo, partials, tokens)
        partials, tokens = over_cohort(partial)
        cell_scale, partial = step_call(rows_of, "rows", row(cell_mass), khi, klo, partials, tokens)
    partials, tokens = over_cell(partial)
    half = DAYS // 2
    seg = row(cohort_segment)
    away, weights = spread_call(seg, cohort_scale, partials, pairs, 0, half, tokens)
    came = swap(away, "cohort", n_cohort, 1)
    mine, _ = spread_call(seg, cohort_scale, partials, pairs, half, half, tokens)
    mine = mine + came
    out = mine[(n_y - 1) * t_dev :]
    for step in range(1, n_y):
        out = out + shift(mine[(step - 1) * t_dev : step * t_dev], "cohort", n_cohort, 2, step)
    return (weights.reshape(-1), cell_scale.reshape(-1), out)


def solution(mesh):
    return jax.shard_map(
        functools.partial(per_device, mesh.shape["cohort"], mesh.shape["cell"]),
        mesh=mesh,
        in_specs=(
            P("cohort", None),
            P("cell", None),
            P("cohort"),
            P("cell"),
            P(),
            P("cohort"),
            P("cell"),
            P("cohort"),
            P("cohort", "cell"),
            P("cohort", "cell"),
            P("cohort", "cell"),
        ),
        out_specs=(P("cohort"), P("cell"), P("cohort", None, "cell")),
        check_vma=False,
    )
```

```python
import functools
import math

import jax
import jax.numpy as jnp
import numpy as np
from jax import lax
from jax.experimental import pallas as pl
from jax.experimental.pallas import tpu as pltpu
from jax.sharding import PartitionSpec as P

ITERS = 2
SEG = 32
MERCH_DEV = 128
DAYS = 64
LANES = 128
CHUNKS = 4
UNROLL = 64

half_span = 11

f32 = jnp.float32
bf16 = jnp.bfloat16
VMEM = pl.BlockSpec(memory_space=pltpu.VMEM)
ANY = pl.BlockSpec(memory_space=pl.ANY)
HBM = pl.BlockSpec(memory_space=pltpu.HBM)
PARAMS = pltpu.CompilerParams(vmem_limit_bytes=20 * 2**20)


def filter_table(day_count):
    outer = 13.0
    coeffs = []
    for offset_days in range(-half_span, half_span + 1):
        sq = float(offset_days * offset_days)
        top = (
            315.0
            * ((outer - 1) ** 2 - sq)
            * (outer**2 - sq)
            * ((outer + 1) ** 2 - sq)
            * (3 * outer**2 - 16 - 11 * sq)
        )
        bottom = (
            8
            * outer
            * (outer**2 - 1)
            * (4 * outer**2 - 1)
            * (4 * outer**2 - 9)
            * (4 * outer**2 - 25)
        )
        coeffs.append(top / bottom)
    matrix = np.zeros((day_count, day_count))
    for row_day in range(day_count):
        for offset_days in range(-half_span, half_span + 1):
            col_day = row_day + offset_days
            if 0 <= col_day < day_count:
                matrix[row_day, col_day] = coeffs[offset_days + half_span]
        matrix[row_day] = matrix[row_day] / matrix[row_day].sum()
    return matrix


def split2(x):
    hi = x.astype(bf16)
    return hi, (x - hi.astype(f32)).astype(bf16)


def split_rows(x):
    hi = x.astype(bf16)
    rest = x - hi.astype(f32)
    mid = rest.astype(bf16)
    low = (rest - mid.astype(f32)).astype(bf16)
    return jnp.concatenate([hi, mid, low, jnp.zeros((5, x.shape[1]), bf16)], 0)


def dot_rows(rows, k, dims):
    return lax.dot_general(rows, k, (dims, ((), ())), preferred_element_type=f32)


def cols_of(us, blocks):
    out = 0.0
    for u, (khi, klo) in zip(us, blocks):
        rows = split_rows(u)
        out = out + dot_rows(rows, khi[...], ((1,), (0,))) + dot_rows(rows, klo[...], ((1,), (0,)))
    return jnp.sum(out, axis=0, keepdims=True)


def rows_of(vs, blocks):
    out = 0.0
    for v, (khi, klo) in zip(vs, blocks):
        rows = split_rows(v)
        out = out + dot_rows(rows, khi[...], ((1,), (1,))) + dot_rows(rows, klo[...], ((1,), (1,)))
    return jnp.sum(out, axis=0, keepdims=True)


def kernel_block(x, y, row_region, col_region, penalty):
    n, m = x.shape[0], y.shape[0]
    regions = penalty.shape[0]
    inv_root = 1.0 / math.sqrt(x.shape[1])
    inner = dot_rows(x, y, ((1,), (1,)))
    row_hot = (lax.broadcasted_iota(jnp.int32, (regions, n), 0) == row_region).astype(f32).astype(bf16)
    col_hot = (lax.broadcasted_iota(jnp.int32, (regions, m), 0) == col_region).astype(f32).astype(bf16)
    phi, plo = split2(penalty)
    qhi = jnp.dot(phi, col_hot, preferred_element_type=f32).astype(bf16)
    qlo = jnp.dot(plo, col_hot, preferred_element_type=f32).astype(bf16)
    pen = dot_rows(jnp.concatenate([row_hot, row_hot], 0), jnp.concatenate([qhi, qlo], 0), ((0,), (0,)))
    return split2(jnp.exp(inner * inv_root - pen))


def run_copies(pairs, sems):
    copies = [pltpu.make_async_copy(src, dst, sems.at[k]) for k, (src, dst) in enumerate(pairs)]
    for copy in copies:
        copy.start()
    return copies


def first_body(
    x_hbm, y_hbm, rr_hbm, cr_hbm, pen_hbm, rr4_hbm, seg4_hbm, mass4_hbm, cr4_hbm, cm4_hbm, f_hbm, m_hbm, d_hbm, a_hbm,
    khi_ref, klo_ref, r_ref, xpack_ref, ypack_ref, seg_ref, mass_ref, cm_ref, pen_ref, cr_ref, rr_ref, xb_ref, yb_ref,
    f_ref, m_ref, d_ref, a_ref, rr4_ref, seg4_ref, cr4_ref, sems,
):
    me = lax.axis_index("cohort")
    n, m = xb_ref.shape[0], yb_ref.shape[0]
    p, q = n // LANES, m // LANES
    copies = run_copies(
        (
            (x_hbm, xb_ref),
            (y_hbm, yb_ref),
            (rr_hbm, rr_ref),
            (cr_hbm, cr_ref),
            (pen_hbm, pen_ref),
            (rr4_hbm, rr4_ref),
            (seg4_hbm, seg4_ref),
            (mass4_hbm, xpack_ref.at[pl.ds(n + 2 * p, p), :]),
            (cr4_hbm, cr4_ref),
            (cm4_hbm, ypack_ref.at[pl.ds(m + q, q), :]),
            (mass4_hbm, mass_ref),
            (cm4_hbm, cm_ref),
            (seg4_hbm, seg_ref),
            (f_hbm.at[me], f_ref),
            (m_hbm, m_ref),
            (d_hbm, d_ref),
            (a_hbm, a_ref),
        ),
        sems,
    )
    for copy in copies[:5]:
        copy.wait()
    hi, lo = kernel_block(xb_ref[...], yb_ref[...], rr_ref[...], cr_ref[...], pen_ref[...])
    khi_ref[...] = hi
    klo_ref[...] = lo
    r_ref[...] = rows_of([jnp.ones((1, m), f32)], [(khi_ref, klo_ref)])
    xpack_ref[0:n, :] = xb_ref[...].astype(f32)
    ypack_ref[0:m, :] = yb_ref[...].astype(f32)
    for copy in copies[5:]:
        copy.wait()
    xpack_ref[n : n + p, :] = rr4_ref[...].astype(f32)
    xpack_ref[n + p : n + 2 * p, :] = seg4_ref[...].astype(f32)
    ypack_ref[m : m + q, :] = cr4_ref[...].astype(f32)


def first_call(x, y, rr, cr, penalty, mass, cm, seg, table, records):
    n, m = x.shape[0], y.shape[0]
    p, q = n // LANES, m // LANES
    row = lambda v: v.reshape(1, -1)
    block = lambda v: v.reshape(-1, LANES)
    i32 = jnp.int32
    out = [
        ((n, m), bf16),
        ((n, m), bf16),
        ((1, n), f32),
        ((n + 3 * p, LANES), f32),
        ((m + 2 * q, LANES), f32),
        ((p, LANES), i32),
        ((p, LANES), f32),
        ((q, LANES), f32),
        (penalty.shape, f32),
        ((1, m), i32),
        ((1, n), i32),
        (x.shape, bf16),
        (y.shape, bf16),
        (table.shape[1:], f32),
    ] + [(r.shape, r.dtype) for r in records]
    return pl.pallas_call(
        first_body,
        in_specs=[HBM] * 14,
        out_specs=[VMEM] * len(out),
        out_shape=[pltpu.VMEM(shape, dtype) for shape, dtype in out],
        scratch_shapes=[
            pltpu.VMEM((p, LANES), i32),
            pltpu.VMEM((p, LANES), i32),
            pltpu.VMEM((q, LANES), i32),
            pltpu.SemaphoreType.DMA((17,)),
        ],
        compiler_params=PARAMS,
        name="first",
    )(x, y, row(rr), row(cr), penalty, block(rr), block(seg), block(mass), block(cr), block(cm), table, *records)


def flat(block):
    return jnp.concatenate([block[k : k + 1, :] for k in range(block.shape[0])], 1)


def rest_body(counts, x_ref, y_ref, rr_ref, cr_ref, pen_ref, *refs):
    n_x, n_y = counts
    xpacks, ypacks = refs[:n_x], refs[n_x : n_x + n_y]
    outs = refs[n_x + n_y :]
    n, m = x_ref.shape[0], y_ref.shape[0]
    p, q = n // LANES, m // LANES
    xs = [(x_ref[...], rr_ref[...])]
    for pack in xpacks:
        xs.append((pack[0:n, :].astype(bf16), flat(pack[n : n + p, :]).astype(jnp.int32)))
    ys = [(y_ref[...], cr_ref[...])]
    for pack in ypacks:
        ys.append((pack[0:m, :].astype(bf16), flat(pack[m : m + q, :]).astype(jnp.int32)))
    pen = pen_ref[...]
    k = 0
    for i, (x, rr) in enumerate(xs):
        for j, (y, cr) in enumerate(ys):
            if i or j:
                outs[k][...], outs[k + 1][...] = kernel_block(x, y, rr, cr, pen)
                k += 2


def rest_call(x, y, rr, cr, penalty, xpacks, ypacks, after):
    n, m = x.shape[0], y.shape[0]
    blocks = (1 + len(xpacks)) * (1 + len(ypacks)) - 1
    out = pl.pallas_call(
        lambda *refs: rest_body(
            (len(xpacks), len(ypacks)), *refs[: 5 + len(xpacks) + len(ypacks)], *refs[-2 * blocks :]
        ),
        in_specs=[VMEM] * (5 + len(xpacks) + len(ypacks)) + [ANY] * len(after),
        out_specs=[VMEM] * (2 * blocks),
        out_shape=[pltpu.VMEM((n, m), bf16)] * (2 * blocks),
        compiler_params=PARAMS,
        cost_estimate=pl.CostEstimate(
            flops=2 * blocks * n * m * LANES, transcendentals=blocks * n * m, bytes_accessed=blocks * n * m * 4
        ),
        name="rest",
    )(x, y, rr, cr, penalty, *xpacks, *ypacks, *after)
    return [(out[2 * k], out[2 * k + 1]) for k in range(blocks)]


def total_of(refs):
    total = refs[0][...]
    for ref in refs[1:]:
        total = total + ref[...]
    return total


def cols_body(n, groups, packs, block_count, mass_ref, *refs):
    p = n // LANES
    at = 0
    sums = []
    for count in groups:
        sums.append(total_of(refs[at : at + count]))
        at += count
    pack_refs = refs[at : at + packs]
    blocks = [(refs[at + packs + 2 * k], refs[at + packs + 2 * k + 1]) for k in range(block_count)]
    u_ref, c_ref = refs[-2:]
    masses = [flat(mass_ref[...])] + [flat(pack[n + 2 * p : n + 3 * p, :]) for pack in pack_refs]
    if len(groups) == 1:
        sums = [sums[0][:, k * n : (k + 1) * n] for k in range(len(masses))]
    us = [mass / part for mass, part in zip(masses, sums)]
    u_ref[...] = jnp.concatenate(us, 1)
    width = block_count // len(masses)
    c_ref[...] = jnp.concatenate(
        [cols_of(us, [blocks[i * width + j] for i in range(len(masses))]) for j in range(width)], 1
    )


def cols_call(mass, n, partial_groups, packs, blocks, after):
    partials = [part for group in partial_groups for part in group]
    parts = 1 + len(packs)
    m = blocks[0][0].shape[1]
    width = len(blocks) // parts
    args = [mass, *partials, *packs, *[ref for block in blocks for ref in block]]
    return pl.pallas_call(
        lambda *refs: cols_body(
            n, [len(group) for group in partial_groups], len(packs), len(blocks), *refs[: len(args)], *refs[-2:]
        ),
        in_specs=[VMEM] * len(args) + [ANY] * len(after),
        out_specs=[VMEM] * 2,
        out_shape=[pltpu.VMEM((1, parts * n), f32), pltpu.VMEM((1, width * m), f32)],
        compiler_params=PARAMS,
        name="cols",
    )(*args, *after)


def rows_body(m, packs, parts, block_count, mass_ref, *refs):
    q = m // LANES
    total = total_of(refs[:parts])
    pack_refs = refs[parts : parts + packs]
    blocks = [(refs[parts + packs + 2 * k], refs[parts + packs + 2 * k + 1]) for k in range(block_count)]
    v_ref, r_ref = refs[-2:]
    masses = [flat(mass_ref[...])] + [flat(pack[m + q : m + 2 * q, :]) for pack in pack_refs]
    vs = [mass / total[:, k * m : (k + 1) * m] for k, mass in enumerate(masses)]
    v_ref[...] = vs[0]
    width = len(masses)
    r_ref[...] = jnp.concatenate(
        [rows_of(vs, blocks[i * width : (i + 1) * width]) for i in range(block_count // width)], 1
    )


def rows_call(mass, partials, packs, blocks, after):
    n, m = blocks[0][0].shape
    width = 1 + len(packs)
    args = [mass, *partials, *packs, *[ref for block in blocks for ref in block]]
    return pl.pallas_call(
        lambda *refs: rows_body(m, len(packs), len(partials), len(blocks), *refs[: len(args)], *refs[-2:]),
        in_specs=[VMEM] * len(args) + [ANY] * len(after),
        out_specs=[VMEM] * 2,
        out_shape=[
            jax.ShapeDtypeStruct((1, m), f32),
            pltpu.VMEM((1, len(blocks) // width * n), f32),
        ],
        compiler_params=PARAMS,
        name="rows",
    )(*args, *after)


def table_body(count, filt, read, hi_ref, lo_ref):
    t_count = filt.shape[0]
    merch_iota = lax.broadcasted_iota(jnp.int32, (MERCH_DEV, LANES), 0).astype(f32).astype(bf16)
    one, zero = jnp.ones((MERCH_DEV, LANES), bf16), jnp.zeros((MERCH_DEV, LANES), bf16)
    size = math.gcd(count, UNROLL)

    def group(step, carry):
        start = pl.multiple_of(step * size, size)
        merch, days, amounts = read(start, size)
        merch = merch.astype(f32).astype(bf16)
        days = days.astype(jnp.int32)
        tables = []
        for i in range(size):
            day = jnp.broadcast_to(days[i : i + 1, :], (t_count, LANES))
            coef = jnp.take_along_axis(filt, day, axis=1, mode="promise_in_bounds")
            chi, clo = split2(coef * amounts[i : i + 1, :])
            hot = jnp.where(merch_iota == merch[i : i + 1, :], one, zero)
            both = dot_rows(jnp.concatenate([chi, clo], 0), hot, ((1,), (1,)))
            tables.append(both[:t_count] + both[t_count:])
        hi, lo = split2(jnp.swapaxes(jnp.stack(tables, 0), 0, 1))
        hi_ref[:, pl.ds(start, size), :] = hi
        lo_ref[:, pl.ds(start, size), :] = lo
        return carry

    lax.fori_loop(0, count // size, group, 0)


def own_body(first, count, f_ref, m_ref, d_ref, a_ref, hi_ref, lo_ref, pack_ref):
    rows = pl.ds(first, count)
    pack_ref[0:count, :] = m_ref[rows, :].astype(f32)
    pack_ref[count : 2 * count, :] = d_ref[rows, :].astype(f32)
    pack_ref[2 * count : 3 * count, :] = a_ref[rows, :]

    def read(start, size):
        at = pl.ds(first + start, size)
        return m_ref[at, :], d_ref[at, :], a_ref[at, :]

    table_body(count, f_ref[...], read, hi_ref, lo_ref)


def other_body(count, f_ref, pack_ref, hi_ref, lo_ref, token_ref):
    def read(start, size):
        return tuple(pack_ref[pl.ds(k * count + start, size), :] for k in range(3))

    table_body(count, f_ref[...], read, hi_ref, lo_ref)
    token_ref[...] = jnp.zeros_like(token_ref)


def table_call(body, filt, args, count, extra, after):
    t_count = filt.shape[0]
    hi, lo, pack = pl.pallas_call(
        lambda *refs: body(*refs[: 1 + len(args)], *refs[-3:]),
        in_specs=[VMEM] * (1 + len(args)) + [ANY] * len(after),
        out_specs=[VMEM] * 3,
        out_shape=[pltpu.VMEM((t_count, count, LANES), bf16)] * 2 + [pltpu.VMEM((extra, LANES), f32)],
        compiler_params=PARAMS,
        cost_estimate=pl.CostEstimate(
            flops=4 * count * t_count * LANES * LANES, transcendentals=0, bytes_accessed=count * 80000
        ),
        name="tables",
    )(filt, *args, *after)
    return (hi, lo), pack


def spread_body(n, t_first, t_count, parts, packs, count, seg_ref, u_ref, *refs):
    p = n // LANES
    w = u_ref[...] * total_of(refs[:parts])
    pack_refs = refs[parts : parts + packs]
    pair_refs = refs[parts + packs : parts + packs + 2 * count]
    o_ref, w_ref = refs[-2:]
    w_ref[...] = w[:, :n]
    seg = jnp.concatenate(
        [flat(seg_ref[...])] + [flat(pack[n + p : n + 2 * p, :]).astype(jnp.int32) for pack in pack_refs], 1
    )
    hot = lax.broadcasted_iota(jnp.int32, (SEG, w.shape[1]), 0) == seg
    whi, wlo = split2(jnp.where(hot, w, 0.0))
    both = jnp.concatenate([whi, wlo], 0)

    def take(part, t):
        return jnp.concatenate(
            [jnp.concatenate([pair_refs[2 * k + part][t + q] for k in range(count)], 0) for q in range(2)], 1
        )

    for t in range(t_first, t_first + t_count, 2):
        two = jnp.dot(both, take(0, t), preferred_element_type=f32)
        out = two[:SEG] + two[SEG:] + jnp.dot(whi, take(1, t), preferred_element_type=f32)
        o_ref[t - t_first] = out[:, :LANES]
        o_ref[t - t_first + 1] = out[:, LANES:]


def spread_call(n, seg, u, partials, packs, pairs, t_first, t_count, after):
    refs = [ref for pair in pairs for ref in pair]
    args = [seg, u, *partials, *packs, *refs]
    return pl.pallas_call(
        lambda *refs: spread_body(
            n, t_first, t_count, len(partials), len(packs), len(pairs), *refs[: len(args)], *refs[-2:]
        ),
        in_specs=[VMEM] * len(args) + [ANY] * len(after),
        out_specs=[VMEM] * 2,
        out_shape=[pltpu.VMEM((t_count, SEG, LANES), f32), jax.ShapeDtypeStruct((1, n), f32)],
        compiler_params=PARAMS,
        name="spread",
    )(*args, *after)


def move(x, axis, size, pair, step, flip):
    blocks = size // pair
    return lax.ppermute(
        x,
        axis,
        [(b * pair + r, ((b + step) % blocks) * pair + (r ^ flip)) for b in range(blocks) for r in range(pair)],
    )


def gate(x, *after):
    return lax.optimization_barrier((x, *after))[0]


def per_device(
    n_cohort,
    n_cell,
    cohort_features,
    cell_features,
    cohort_region,
    cell_region,
    penalty,
    cohort_mass,
    cell_mass,
    cohort_segment,
    spend_merchant,
    spend_day,
    spend_amount,
):
    n = cohort_features.shape[0]
    t_dev = DAYS // n_cohort
    n_y, n_z = n_cohort // 2, n_cell // 2
    table = np.zeros((n_cohort, 2 * t_dev, LANES), np.float32)
    henderson = filter_table(DAYS)
    for me in range(n_cohort):
        for k, dest in enumerate((me ^ 1, me)):
            table[me, k * t_dev : (k + 1) * t_dev, :DAYS] = henderson[dest * t_dev : (dest + 1) * t_dev]

    over_y = lambda x, step: move(x, "cohort", n_cohort, 2, step, 0)
    core = lambda x: move(x, "cohort", n_cohort, 2, 0, 1)
    along_z = lambda x: [x] + [move(x, "cell", n_cell, 2, step, 0) for step in range(1, n_z)]

    (
        khi, klo, partial, xpack, ypack, seg, mass, cmass, pen, creg, rreg, xb, yb, filt, *records
    ) = first_call(
        cohort_features, cell_features, cohort_region, cell_region, penalty, cohort_mass, cell_mass, cohort_segment,
        jnp.asarray(table), (spend_merchant, spend_day, spend_amount),
    )
    count = n // CHUNKS
    own, sends = [], []

    def own_tables(after):
        first = len(own) * count
        pair, pack = table_call(functools.partial(own_body, first, count), filt, records, count, 3 * count, after)
        own.append(pair)
        sends.append(pack)
        return pack

    lines = along_z(partial)
    xpacks = [over_y(xpack, step) for step in range(1, n_y)]
    ypacks = [move(ypack, "cell", n_cell, 2, 0, 1)]
    token = own_tables([partial])
    token = own_tables([token])
    part = gate(sum(lines), token)
    whole = [part, move(part, "cell", n_cell, 2, 0, 1)]
    groups = [whole]
    for step in range(1, n_y):
        groups.append([both_axes(part, n_cohort, n_cell, step, flip) for flip in range(2)])
    token = own_tables([part])
    token = own_tables([token])
    blocks = [(khi, klo)] + rest_call(xb, yb, rreg, creg, pen, xpacks, ypacks, [token])
    cohort_scale, column = cols_call(mass, n, groups, xpacks, blocks, [token])
    others = []
    gated = column
    waiting = [(step, chunk) for chunk in range(CHUNKS) for step in range(1, n_y)]
    arrived = [over_y(gate(sends[chunk], gated), step) for step, chunk in waiting]
    per_window = -(-len(arrived) // 2)
    token = None
    for iteration in range(ITERS):
        after = [] if token is None else [token]
        cell_scale, partial = rows_call(cmass, [column, core(column)], ypacks, blocks, after)
        lines = along_z(partial)
        token = partial
        for pack in arrived[iteration * per_window : (iteration + 1) * per_window]:
            pair, token = table_call(functools.partial(other_body, count), filt, [pack], count, 8, [token])
            others.append(pair)
        if iteration < ITERS - 1:
            cohort_scale, column = cols_call(mass, n, [lines], xpacks, blocks, [token])
            token = None
    pairs = own + [others[k] for step in range(1, n_y) for k in range(len(waiting)) if waiting[k][0] == step]
    away, weights = spread_call(n, seg, cohort_scale, lines, xpacks, pairs, 0, t_dev, [token])
    mine, _ = spread_call(n, seg, cohort_scale, lines, xpacks, pairs, t_dev, t_dev, [token])
    out = mine + core(away)
    return (weights.reshape(-1), cell_scale.reshape(-1), out)


def both_axes(x, n_cohort, n_cell, step, flip):
    pairs = []
    blocks = n_cohort // 2
    for b in range(blocks):
        for c in range(2):
            for cell in range(n_cell):
                source = (b * 2 + c) * n_cell + cell
                target = (((b + step) % blocks) * 2 + c) * n_cell + (cell ^ flip)
                pairs.append((source, target))
    return lax.ppermute(x, ("cohort", "cell"), pairs)


def solution(mesh):
    return jax.shard_map(
        functools.partial(per_device, mesh.shape["cohort"], mesh.shape["cell"]),
        mesh=mesh,
        in_specs=(
            P("cohort", None),
            P("cell", None),
            P("cohort"),
            P("cell"),
            P(),
            P("cohort"),
            P("cell"),
            P("cohort"),
            P("cohort", "cell"),
            P("cohort", "cell"),
            P("cohort", "cell"),
        ),
        out_specs=(P("cohort"), P("cell"), P("cohort", None, "cell")),
        check_vma=False,
    )
```

```python
import functools
import math

import jax
import jax.numpy as jnp
import numpy as np
from jax import lax
from jax.experimental import pallas as pl
from jax.experimental.pallas import tpu as pltpu
from jax.sharding import PartitionSpec as P

ITERS = 2
SEG = 32
MERCH_DEV = 128
DAYS = 64
LANES = 128
CHUNKS = 4
UNROLL = 64

half_span = 11

f32 = jnp.float32
bf16 = jnp.bfloat16
VMEM = pl.BlockSpec(memory_space=pltpu.VMEM)
ANY = pl.BlockSpec(memory_space=pl.ANY)
HBM = pl.BlockSpec(memory_space=pltpu.HBM)
PARAMS = pltpu.CompilerParams(vmem_limit_bytes=20 * 2**20)


def filter_table(day_count):
    outer = 13.0
    coeffs = []
    for offset_days in range(-half_span, half_span + 1):
        sq = float(offset_days * offset_days)
        top = (
            315.0
            * ((outer - 1) ** 2 - sq)
            * (outer**2 - sq)
            * ((outer + 1) ** 2 - sq)
            * (3 * outer**2 - 16 - 11 * sq)
        )
        bottom = (
            8
            * outer
            * (outer**2 - 1)
            * (4 * outer**2 - 1)
            * (4 * outer**2 - 9)
            * (4 * outer**2 - 25)
        )
        coeffs.append(top / bottom)
    matrix = np.zeros((day_count, day_count))
    for row_day in range(day_count):
        for offset_days in range(-half_span, half_span + 1):
            col_day = row_day + offset_days
            if 0 <= col_day < day_count:
                matrix[row_day, col_day] = coeffs[offset_days + half_span]
        matrix[row_day] = matrix[row_day] / matrix[row_day].sum()
    return matrix


def split2(x):
    hi = x.astype(bf16)
    return hi, (x - hi.astype(f32)).astype(bf16)


def split_rows(x):
    hi = x.astype(bf16)
    rest = x - hi.astype(f32)
    mid = rest.astype(bf16)
    low = (rest - mid.astype(f32)).astype(bf16)
    return jnp.concatenate([hi, mid, low, jnp.zeros((5, x.shape[1]), bf16)], 0)


def dot_rows(rows, k, dims):
    return lax.dot_general(rows, k, (dims, ((), ())), preferred_element_type=f32)


def cols_of(us, blocks):
    out = 0.0
    for u, (khi, klo) in zip(us, blocks):
        rows = split_rows(u)
        out = out + dot_rows(rows, khi[...], ((1,), (0,))) + dot_rows(rows, klo[...], ((1,), (0,)))
    return jnp.sum(out, axis=0, keepdims=True)


def rows_of(vs, blocks):
    out = 0.0
    for v, (khi, klo) in zip(vs, blocks):
        rows = split_rows(v)
        out = out + dot_rows(rows, khi[...], ((1,), (1,))) + dot_rows(rows, klo[...], ((1,), (1,)))
    return jnp.sum(out, axis=0, keepdims=True)


def kernel_block(x, y, row_region, col_region, penalty):
    n, m = x.shape[0], y.shape[0]
    regions = penalty.shape[0]
    inv_root = 1.0 / math.sqrt(x.shape[1])
    inner = dot_rows(x, y, ((1,), (1,)))
    row_hot = (lax.broadcasted_iota(jnp.int32, (regions, n), 0) == row_region).astype(f32).astype(bf16)
    col_hot = (lax.broadcasted_iota(jnp.int32, (regions, m), 0) == col_region).astype(f32).astype(bf16)
    phi, plo = split2(penalty)
    qhi = jnp.dot(phi, col_hot, preferred_element_type=f32).astype(bf16)
    qlo = jnp.dot(plo, col_hot, preferred_element_type=f32).astype(bf16)
    pen = dot_rows(jnp.concatenate([row_hot, row_hot], 0), jnp.concatenate([qhi, qlo], 0), ((0,), (0,)))
    return split2(jnp.exp(inner * inv_root - pen))


def run_copies(pairs, sems):
    copies = [pltpu.make_async_copy(src, dst, sems.at[k]) for k, (src, dst) in enumerate(pairs)]
    for copy in copies:
        copy.start()
    return copies


def first_body(
    x_hbm, y_hbm, rr_hbm, cr_hbm, pen_hbm, rr4_hbm, seg4_hbm, mass4_hbm, cr4_hbm, cm4_hbm, f_hbm, m_hbm, d_hbm, a_hbm,
    khi_ref, klo_ref, r_ref, xpack_ref, ypack_ref, seg_ref, mass_ref, cm_ref, pen_ref, cr_ref, rr_ref, xb_ref, yb_ref,
    f_ref, m_ref, d_ref, a_ref, rr4_ref, seg4_ref, cr4_ref, sems,
):
    me = lax.axis_index("cohort")
    n, m = xb_ref.shape[0], yb_ref.shape[0]
    p, q = n // LANES, m // LANES
    copies = run_copies(
        (
            (x_hbm, xb_ref),
            (y_hbm, yb_ref),
            (rr_hbm, rr_ref),
            (cr_hbm, cr_ref),
            (pen_hbm, pen_ref),
            (rr4_hbm, rr4_ref),
            (seg4_hbm, seg4_ref),
            (mass4_hbm, xpack_ref.at[pl.ds(n + 2 * p, p), :]),
            (cr4_hbm, cr4_ref),
            (cm4_hbm, ypack_ref.at[pl.ds(m + q, q), :]),
            (mass4_hbm, mass_ref),
            (cm4_hbm, cm_ref),
            (seg4_hbm, seg_ref),
            (f_hbm.at[me], f_ref),
            (m_hbm, m_ref),
            (d_hbm, d_ref),
            (a_hbm, a_ref),
        ),
        sems,
    )
    for copy in copies[:5]:
        copy.wait()
    hi, lo = kernel_block(xb_ref[...], yb_ref[...], rr_ref[...], cr_ref[...], pen_ref[...])
    khi_ref[...] = hi
    klo_ref[...] = lo
    r_ref[...] = rows_of([jnp.ones((1, m), f32)], [(khi_ref, klo_ref)])
    xpack_ref[0:n, :] = xb_ref[...].astype(f32)
    ypack_ref[0:m, :] = yb_ref[...].astype(f32)
    for copy in copies[5:]:
        copy.wait()
    xpack_ref[n : n + p, :] = rr4_ref[...].astype(f32)
    xpack_ref[n + p : n + 2 * p, :] = seg4_ref[...].astype(f32)
    ypack_ref[m : m + q, :] = cr4_ref[...].astype(f32)


def first_call(x, y, rr, cr, penalty, mass, cm, seg, table, records):
    n, m = x.shape[0], y.shape[0]
    p, q = n // LANES, m // LANES
    row = lambda v: v.reshape(1, -1)
    block = lambda v: v.reshape(-1, LANES)
    i32 = jnp.int32
    out = [
        ((n, m), bf16),
        ((n, m), bf16),
        ((1, n), f32),
        ((n + 3 * p, LANES), f32),
        ((m + 2 * q, LANES), f32),
        ((p, LANES), i32),
        ((p, LANES), f32),
        ((q, LANES), f32),
        (penalty.shape, f32),
        ((1, m), i32),
        ((1, n), i32),
        (x.shape, bf16),
        (y.shape, bf16),
        (table.shape[1:], f32),
    ] + [(r.shape, r.dtype) for r in records]
    return pl.pallas_call(
        first_body,
        in_specs=[HBM] * 14,
        out_specs=[VMEM] * len(out),
        out_shape=[pltpu.VMEM(shape, dtype) for shape, dtype in out],
        scratch_shapes=[
            pltpu.VMEM((p, LANES), i32),
            pltpu.VMEM((p, LANES), i32),
            pltpu.VMEM((q, LANES), i32),
            pltpu.SemaphoreType.DMA((17,)),
        ],
        compiler_params=PARAMS,
        name="first",
    )(
        *[
            pltpu.with_memory_space_constraint(arg, pltpu.HBM)
            for arg in (
                x, y, row(rr), row(cr), penalty, block(rr), block(seg), block(mass), block(cr), block(cm), table, *records
            )
        ]
    )


def flat(block):
    return jnp.concatenate([block[k : k + 1, :] for k in range(block.shape[0])], 1)


def rest_body(counts, x_ref, y_ref, rr_ref, cr_ref, pen_ref, *refs):
    n_x, n_y = counts
    xpacks, ypacks = refs[:n_x], refs[n_x : n_x + n_y]
    outs = refs[n_x + n_y :]
    n, m = x_ref.shape[0], y_ref.shape[0]
    p, q = n // LANES, m // LANES
    xs = [(x_ref[...], rr_ref[...])]
    for pack in xpacks:
        xs.append((pack[0:n, :].astype(bf16), flat(pack[n : n + p, :]).astype(jnp.int32)))
    ys = [(y_ref[...], cr_ref[...])]
    for pack in ypacks:
        ys.append((pack[0:m, :].astype(bf16), flat(pack[m : m + q, :]).astype(jnp.int32)))
    pen = pen_ref[...]
    k = 0
    for i, (x, rr) in enumerate(xs):
        for j, (y, cr) in enumerate(ys):
            if i or j:
                outs[k][...], outs[k + 1][...] = kernel_block(x, y, rr, cr, pen)
                k += 2


def rest_call(x, y, rr, cr, penalty, xpacks, ypacks, after):
    n, m = x.shape[0], y.shape[0]
    blocks = (1 + len(xpacks)) * (1 + len(ypacks)) - 1
    out = pl.pallas_call(
        lambda *refs: rest_body(
            (len(xpacks), len(ypacks)), *refs[: 5 + len(xpacks) + len(ypacks)], *refs[-2 * blocks :]
        ),
        in_specs=[VMEM] * (5 + len(xpacks) + len(ypacks)) + [ANY] * len(after),
        out_specs=[VMEM] * (2 * blocks),
        out_shape=[pltpu.VMEM((n, m), bf16)] * (2 * blocks),
        compiler_params=PARAMS,
        cost_estimate=pl.CostEstimate(
            flops=2 * blocks * n * m * LANES, transcendentals=blocks * n * m, bytes_accessed=blocks * n * m * 4
        ),
        name="rest",
    )(x, y, rr, cr, penalty, *xpacks, *ypacks, *after)
    return [(out[2 * k], out[2 * k + 1]) for k in range(blocks)]


def total_of(refs):
    total = refs[0][...]
    for ref in refs[1:]:
        total = total + ref[...]
    return total


def cols_body(n, groups, packs, block_count, mass_ref, *refs):
    p = n // LANES
    at = 0
    sums = []
    for count in groups:
        sums.append(total_of(refs[at : at + count]))
        at += count
    pack_refs = refs[at : at + packs]
    blocks = [(refs[at + packs + 2 * k], refs[at + packs + 2 * k + 1]) for k in range(block_count)]
    u_ref, c_ref = refs[-2:]
    masses = [flat(mass_ref[...])] + [flat(pack[n + 2 * p : n + 3 * p, :]) for pack in pack_refs]
    if len(groups) == 1:
        sums = [sums[0][:, k * n : (k + 1) * n] for k in range(len(masses))]
    us = [mass / part for mass, part in zip(masses, sums)]
    u_ref[...] = jnp.concatenate(us, 1)
    width = block_count // len(masses)
    c_ref[...] = jnp.concatenate(
        [cols_of(us, [blocks[i * width + j] for i in range(len(masses))]) for j in range(width)], 1
    )


def cols_call(mass, n, partial_groups, packs, blocks, after):
    partials = [part for group in partial_groups for part in group]
    parts = 1 + len(packs)
    m = blocks[0][0].shape[1]
    width = len(blocks) // parts
    args = [mass, *partials, *packs, *[ref for block in blocks for ref in block]]
    return pl.pallas_call(
        lambda *refs: cols_body(
            n, [len(group) for group in partial_groups], len(packs), len(blocks), *refs[: len(args)], *refs[-2:]
        ),
        in_specs=[VMEM] * len(args) + [ANY] * len(after),
        out_specs=[VMEM] * 2,
        out_shape=[pltpu.VMEM((1, parts * n), f32), pltpu.VMEM((1, width * m), f32)],
        compiler_params=PARAMS,
        name="cols",
    )(*args, *after)


def rows_body(m, packs, parts, block_count, mass_ref, *refs):
    q = m // LANES
    total = total_of(refs[:parts])
    pack_refs = refs[parts : parts + packs]
    blocks = [(refs[parts + packs + 2 * k], refs[parts + packs + 2 * k + 1]) for k in range(block_count)]
    v_ref, r_ref = refs[-2:]
    masses = [flat(mass_ref[...])] + [flat(pack[m + q : m + 2 * q, :]) for pack in pack_refs]
    vs = [mass / total[:, k * m : (k + 1) * m] for k, mass in enumerate(masses)]
    v_ref[...] = vs[0]
    width = len(masses)
    r_ref[...] = jnp.concatenate(
        [rows_of(vs, blocks[i * width : (i + 1) * width]) for i in range(block_count // width)], 1
    )


def rows_call(mass, partials, packs, blocks, after):
    n, m = blocks[0][0].shape
    width = 1 + len(packs)
    args = [mass, *partials, *packs, *[ref for block in blocks for ref in block]]
    return pl.pallas_call(
        lambda *refs: rows_body(m, len(packs), len(partials), len(blocks), *refs[: len(args)], *refs[-2:]),
        in_specs=[VMEM] * len(args) + [ANY] * len(after),
        out_specs=[VMEM] * 2,
        out_shape=[
            jax.ShapeDtypeStruct((1, m), f32),
            pltpu.VMEM((1, len(blocks) // width * n), f32),
        ],
        compiler_params=PARAMS,
        name="rows",
    )(*args, *after)


def table_body(count, filt, read, hi_ref, lo_ref):
    t_count = filt.shape[0]
    merch_iota = lax.broadcasted_iota(jnp.int32, (MERCH_DEV, LANES), 0).astype(f32).astype(bf16)
    one, zero = jnp.ones((MERCH_DEV, LANES), bf16), jnp.zeros((MERCH_DEV, LANES), bf16)
    size = math.gcd(count, UNROLL)

    def group(step, carry):
        start = pl.multiple_of(step * size, size)
        merch, days, amounts = read(start, size)
        merch = merch.astype(f32).astype(bf16)
        days = days.astype(jnp.int32)
        tables = []
        for i in range(size):
            day = jnp.broadcast_to(days[i : i + 1, :], (t_count, LANES))
            coef = jnp.take_along_axis(filt, day, axis=1, mode="promise_in_bounds")
            chi, clo = split2(coef * amounts[i : i + 1, :])
            hot = jnp.where(merch_iota == merch[i : i + 1, :], one, zero)
            both = dot_rows(jnp.concatenate([chi, clo], 0), hot, ((1,), (1,)))
            tables.append(both[:t_count] + both[t_count:])
        hi, lo = split2(jnp.swapaxes(jnp.stack(tables, 0), 0, 1))
        hi_ref[:, pl.ds(start, size), :] = hi
        lo_ref[:, pl.ds(start, size), :] = lo
        return carry

    lax.fori_loop(0, count // size, group, 0)


def own_body(first, count, f_ref, m_ref, d_ref, a_ref, hi_ref, lo_ref, pack_ref):
    rows = pl.ds(first, count)
    pack_ref[0:count, :] = m_ref[rows, :].astype(f32)
    pack_ref[count : 2 * count, :] = d_ref[rows, :].astype(f32)
    pack_ref[2 * count : 3 * count, :] = a_ref[rows, :]

    def read(start, size):
        at = pl.ds(first + start, size)
        return m_ref[at, :], d_ref[at, :], a_ref[at, :]

    table_body(count, f_ref[...], read, hi_ref, lo_ref)


def other_body(count, f_ref, pack_ref, hi_ref, lo_ref, token_ref):
    def read(start, size):
        return tuple(pack_ref[pl.ds(k * count + start, size), :] for k in range(3))

    table_body(count, f_ref[...], read, hi_ref, lo_ref)
    token_ref[...] = jnp.zeros_like(token_ref)


def table_call(body, filt, args, count, extra, after):
    t_count = filt.shape[0]
    hi, lo, pack = pl.pallas_call(
        lambda *refs: body(*refs[: 1 + len(args)], *refs[-3:]),
        in_specs=[VMEM] * (1 + len(args)) + [ANY] * len(after),
        out_specs=[VMEM] * 3,
        out_shape=[pltpu.VMEM((t_count, count, LANES), bf16)] * 2 + [pltpu.VMEM((extra, LANES), f32)],
        compiler_params=PARAMS,
        cost_estimate=pl.CostEstimate(
            flops=4 * count * t_count * LANES * LANES, transcendentals=0, bytes_accessed=count * 80000
        ),
        name="tables",
    )(filt, *args, *after)
    return (hi, lo), pack


def spread_body(n, t_first, t_count, parts, packs, count, seg_ref, u_ref, *refs):
    p = n // LANES
    w = u_ref[...] * total_of(refs[:parts])
    pack_refs = refs[parts : parts + packs]
    pair_refs = refs[parts + packs : parts + packs + 2 * count]
    o_ref, w_ref = refs[-2:]
    w_ref[...] = w[:, :n]
    seg = jnp.concatenate(
        [flat(seg_ref[...])] + [flat(pack[n + p : n + 2 * p, :]).astype(jnp.int32) for pack in pack_refs], 1
    )
    hot = lax.broadcasted_iota(jnp.int32, (SEG, w.shape[1]), 0) == seg
    whi, wlo = split2(jnp.where(hot, w, 0.0))
    both = jnp.concatenate([whi, wlo], 0)

    def take(part, t):
        return jnp.concatenate(
            [jnp.concatenate([pair_refs[2 * k + part][t + q] for k in range(count)], 0) for q in range(2)], 1
        )

    for t in range(t_first, t_first + t_count, 2):
        two = jnp.dot(both, take(0, t), preferred_element_type=f32)
        out = two[:SEG] + two[SEG:] + jnp.dot(whi, take(1, t), preferred_element_type=f32)
        o_ref[t - t_first] = out[:, :LANES]
        o_ref[t - t_first + 1] = out[:, LANES:]


def spread_call(n, seg, u, partials, packs, pairs, t_first, t_count, after):
    refs = [ref for pair in pairs for ref in pair]
    args = [seg, u, *partials, *packs, *refs]
    return pl.pallas_call(
        lambda *refs: spread_body(
            n, t_first, t_count, len(partials), len(packs), len(pairs), *refs[: len(args)], *refs[-2:]
        ),
        in_specs=[VMEM] * len(args) + [ANY] * len(after),
        out_specs=[VMEM] * 2,
        out_shape=[pltpu.VMEM((t_count, SEG, LANES), f32), jax.ShapeDtypeStruct((1, n), f32)],
        compiler_params=PARAMS,
        name="spread",
    )(*args, *after)


def move(x, axis, size, pair, step, flip):
    blocks = size // pair
    return lax.ppermute(
        x,
        axis,
        [(b * pair + r, ((b + step) % blocks) * pair + (r ^ flip)) for b in range(blocks) for r in range(pair)],
    )


def gate(x, *after):
    return lax.optimization_barrier((x, *after))[0]


def per_device(
    n_cohort,
    n_cell,
    cohort_features,
    cell_features,
    cohort_region,
    cell_region,
    penalty,
    cohort_mass,
    cell_mass,
    cohort_segment,
    spend_merchant,
    spend_day,
    spend_amount,
):
    n = cohort_features.shape[0]
    t_dev = DAYS // n_cohort
    n_y, n_z = n_cohort // 2, n_cell // 2
    table = np.zeros((n_cohort, 2 * t_dev, LANES), np.float32)
    henderson = filter_table(DAYS)
    for me in range(n_cohort):
        for k, dest in enumerate((me ^ 1, me)):
            table[me, k * t_dev : (k + 1) * t_dev, :DAYS] = henderson[dest * t_dev : (dest + 1) * t_dev]

    over_y = lambda x, step: move(x, "cohort", n_cohort, 2, step, 0)
    core = lambda x: move(x, "cohort", n_cohort, 2, 0, 1)
    along_z = lambda x: [x] + [move(x, "cell", n_cell, 2, step, 0) for step in range(1, n_z)]

    (
        khi, klo, partial, xpack, ypack, seg, mass, cmass, pen, creg, rreg, xb, yb, filt, *records
    ) = first_call(
        cohort_features, cell_features, cohort_region, cell_region, penalty, cohort_mass, cell_mass, cohort_segment,
        jnp.asarray(table), (spend_merchant, spend_day, spend_amount),
    )
    count = n // CHUNKS
    own, sends = [], []

    def own_tables(after):
        first = len(own) * count
        pair, pack = table_call(functools.partial(own_body, first, count), filt, records, count, 3 * count, after)
        own.append(pair)
        sends.append(pack)
        return pack

    lines = along_z(partial)
    xpacks = [over_y(xpack, step) for step in range(1, n_y)]
    ypacks = [move(ypack, "cell", n_cell, 2, 0, 1)]
    token = own_tables([partial])
    token = own_tables([token])
    part = gate(sum(lines), token)
    whole = [part, move(part, "cell", n_cell, 2, 0, 1)]
    groups = [whole]
    for step in range(1, n_y):
        groups.append([both_axes(part, n_cohort, n_cell, step, flip) for flip in range(2)])
    token = own_tables([part])
    token = own_tables([token])
    blocks = [(khi, klo)] + rest_call(xb, yb, rreg, creg, pen, xpacks, ypacks, [token])
    cohort_scale, column = cols_call(mass, n, groups, xpacks, blocks, [token])
    others = []
    gated = column
    waiting = [(step, chunk) for chunk in range(CHUNKS) for step in range(1, n_y)]
    arrived = [over_y(gate(sends[chunk], gated), step) for step, chunk in waiting]
    per_window = -(-len(arrived) // 2)
    token = None
    for iteration in range(ITERS):
        after = [] if token is None else [token]
        cell_scale, partial = rows_call(cmass, [column, core(column)], ypacks, blocks, after)
        lines = along_z(partial)
        token = partial
        for pack in arrived[iteration * per_window : (iteration + 1) * per_window]:
            pair, token = table_call(functools.partial(other_body, count), filt, [pack], count, 8, [token])
            others.append(pair)
        if iteration < ITERS - 1:
            cohort_scale, column = cols_call(mass, n, [lines], xpacks, blocks, [token])
            token = None
    pairs = own + [others[k] for step in range(1, n_y) for k in range(len(waiting)) if waiting[k][0] == step]
    away, weights = spread_call(n, seg, cohort_scale, lines, xpacks, pairs, 0, t_dev, [token])
    mine, _ = spread_call(n, seg, cohort_scale, lines, xpacks, pairs, t_dev, t_dev, [token])
    out = mine + core(away)
    return (weights.reshape(-1), cell_scale.reshape(-1), out)


def both_axes(x, n_cohort, n_cell, step, flip):
    pairs = []
    blocks = n_cohort // 2
    for b in range(blocks):
        for c in range(2):
            for cell in range(n_cell):
                source = (b * 2 + c) * n_cell + cell
                target = (((b + step) % blocks) * 2 + c) * n_cell + (cell ^ flip)
                pairs.append((source, target))
    return lax.ppermute(x, ("cohort", "cell"), pairs)


def solution(mesh):
    return jax.shard_map(
        functools.partial(per_device, mesh.shape["cohort"], mesh.shape["cell"]),
        mesh=mesh,
        in_specs=(
            P("cohort", None),
            P("cell", None),
            P("cohort"),
            P("cell"),
            P(),
            P("cohort"),
            P("cell"),
            P("cohort"),
            P("cohort", "cell"),
            P("cohort", "cell"),
            P("cohort", "cell"),
        ),
        out_specs=(P("cohort"), P("cell"), P("cohort", None, "cell")),
        check_vma=False,
    )
```

```python
import functools
import math

import jax
import jax.numpy as jnp
import numpy as np
from jax import lax
from jax.experimental import pallas as pl
from jax.experimental.pallas import tpu as pltpu
from jax.sharding import PartitionSpec as P

ITERS = 2
SEG = 32
MERCH_DEV = 128
DAYS = 64
LANES = 128
UNROLL = 128

half_span = 11

f32 = jnp.float32
bf16 = jnp.bfloat16
VMEM = pl.BlockSpec(memory_space=pltpu.VMEM)
ANY = pl.BlockSpec(memory_space=pl.ANY)
HBM = pl.BlockSpec(memory_space=pltpu.HBM)
PARAMS = pltpu.CompilerParams(vmem_limit_bytes=20 * 2**20)


def filter_table(day_count):
    outer = 13.0
    coeffs = []
    for offset_days in range(-half_span, half_span + 1):
        sq = float(offset_days * offset_days)
        top = (
            315.0
            * ((outer - 1) ** 2 - sq)
            * (outer**2 - sq)
            * ((outer + 1) ** 2 - sq)
            * (3 * outer**2 - 16 - 11 * sq)
        )
        bottom = (
            8
            * outer
            * (outer**2 - 1)
            * (4 * outer**2 - 1)
            * (4 * outer**2 - 9)
            * (4 * outer**2 - 25)
        )
        coeffs.append(top / bottom)
    matrix = np.zeros((day_count, day_count))
    for row_day in range(day_count):
        for offset_days in range(-half_span, half_span + 1):
            col_day = row_day + offset_days
            if 0 <= col_day < day_count:
                matrix[row_day, col_day] = coeffs[offset_days + half_span]
        matrix[row_day] = matrix[row_day] / matrix[row_day].sum()
    return matrix


def split2(x):
    hi = x.astype(bf16)
    return hi, (x - hi.astype(f32)).astype(bf16)


def split_rows(x):
    hi = x.astype(bf16)
    rest = x - hi.astype(f32)
    mid = rest.astype(bf16)
    low = (rest - mid.astype(f32)).astype(bf16)
    return jnp.concatenate([hi, mid, low, jnp.zeros((5, x.shape[1]), bf16)], 0)


def dot_rows(rows, k, dims):
    return lax.dot_general(rows, k, (dims, ((), ())), preferred_element_type=f32)


def cols_of(us, blocks):
    out = 0.0
    for u, (khi, klo) in zip(us, blocks):
        rows = split_rows(u)
        out = out + dot_rows(rows, khi[...], ((1,), (0,))) + dot_rows(rows, klo[...], ((1,), (0,)))
    return jnp.sum(out, axis=0, keepdims=True)


def rows_of(vs, blocks):
    out = 0.0
    for v, (khi, klo) in zip(vs, blocks):
        rows = split_rows(v)
        out = out + dot_rows(rows, khi[...], ((1,), (1,))) + dot_rows(rows, klo[...], ((1,), (1,)))
    return jnp.sum(out, axis=0, keepdims=True)


def kernel_block(x, y, row_region, col_region, penalty):
    n, m = x.shape[0], y.shape[0]
    regions = penalty.shape[0]
    inv_root = 1.0 / math.sqrt(x.shape[1])
    inner = dot_rows(x, y, ((1,), (1,)))
    row_hot = (lax.broadcasted_iota(jnp.int32, (regions, n), 0) == row_region).astype(f32).astype(bf16)
    col_hot = (lax.broadcasted_iota(jnp.int32, (regions, m), 0) == col_region).astype(f32).astype(bf16)
    phi, plo = split2(penalty)
    qhi = jnp.dot(phi, col_hot, preferred_element_type=f32).astype(bf16)
    qlo = jnp.dot(plo, col_hot, preferred_element_type=f32).astype(bf16)
    pen = dot_rows(jnp.concatenate([row_hot, row_hot], 0), jnp.concatenate([qhi, qlo], 0), ((0,), (0,)))
    return split2(jnp.exp(inner * inv_root - pen))


def run_copies(pairs, sems):
    copies = [pltpu.make_async_copy(src, dst, sems.at[k]) for k, (src, dst) in enumerate(pairs)]
    for copy in copies:
        copy.start()
    return copies


def first_body(
    x_hbm, y_hbm, rr_hbm, seg_hbm, mass_hbm, cr_hbm, cm_hbm, f_hbm, m_hbm, d_hbm, a_hbm,
    xpack_ref, ypack_ref, rpack_ref, f_ref, xb_ref, yb_ref, rr_ref, seg_ref, cr_ref, m_ref, d_ref, sems,
):
    me = lax.axis_index("cohort")
    n, m = xb_ref.shape[0], yb_ref.shape[0]
    p, q = n // LANES, m // LANES
    copies = run_copies(
        (
            (x_hbm, xb_ref),
            (rr_hbm, rr_ref),
            (seg_hbm, seg_ref),
            (mass_hbm, xpack_ref.at[pl.ds(n + 2 * p, p), :]),
            (y_hbm, yb_ref),
            (cr_hbm, cr_ref),
            (cm_hbm, ypack_ref.at[pl.ds(m + q, q), :]),
            (m_hbm, m_ref),
            (d_hbm, d_ref),
            (a_hbm, rpack_ref.at[pl.ds(2 * n, n), :]),
            (f_hbm.at[me], f_ref),
        ),
        sems,
    )
    for copy in copies:
        copy.wait()
    xpack_ref[0:n, :] = xb_ref[...].astype(f32)
    xpack_ref[n : n + p, :] = rr_ref[...].astype(f32)
    xpack_ref[n + p : n + 2 * p, :] = seg_ref[...].astype(f32)
    ypack_ref[0:m, :] = yb_ref[...].astype(f32)
    ypack_ref[m : m + q, :] = cr_ref[...].astype(f32)
    rpack_ref[0:n, :] = m_ref[...].astype(f32)
    rpack_ref[n : 2 * n, :] = d_ref[...].astype(f32)


def first_call(x, y, rr, seg, mass, cr, cm, table, records):
    n, m = x.shape[0], y.shape[0]
    p, q = n // LANES, m // LANES
    block = lambda v: v.reshape(-1, LANES)
    i32 = jnp.int32
    out = [(n + 3 * p, LANES), (m + 2 * q, LANES), (3 * n, LANES), table.shape[1:]]
    args = (x, y, block(rr), block(seg), block(mass), block(cr), block(cm), table, *records)
    return pl.pallas_call(
        first_body,
        in_specs=[HBM] * len(args),
        out_specs=[VMEM] * len(out),
        out_shape=[pltpu.VMEM(shape, f32) for shape in out],
        scratch_shapes=[
            pltpu.VMEM(x.shape, bf16),
            pltpu.VMEM(y.shape, bf16),
            pltpu.VMEM((p, LANES), i32),
            pltpu.VMEM((p, LANES), i32),
            pltpu.VMEM((q, LANES), i32),
            pltpu.VMEM((n, LANES), i32),
            pltpu.VMEM((n, LANES), i32),
            pltpu.SemaphoreType.DMA((len(args),)),
        ],
        compiler_params=PARAMS,
        name="first",
    )(*[pltpu.with_memory_space_constraint(arg, pltpu.HBM) for arg in args])


def flat(block):
    return jnp.concatenate([block[k : k + 1, :] for k in range(block.shape[0])], 1)


def gibbs_body(n, m, packs_x, packs_y, *refs):
    xpacks, ypacks, pen_ref = refs[:packs_x], refs[packs_x : packs_x + packs_y], refs[packs_x + packs_y]
    outs = refs[packs_x + packs_y + 1 : -1]
    r_ref = refs[-1]
    p, q = n // LANES, m // LANES
    pen = pen_ref[...]
    xs = [(pack[0:n, :].astype(bf16), flat(pack[n : n + p, :]).astype(jnp.int32)) for pack in xpacks]
    ys = [(pack[0:m, :].astype(bf16), flat(pack[m : m + q, :]).astype(jnp.int32)) for pack in ypacks]
    k = 0
    sums = []
    for x, rr in xs:
        blocks = []
        for y, cr in ys:
            outs[k][...], outs[k + 1][...] = kernel_block(x, y, rr, cr, pen)
            blocks.append((outs[k], outs[k + 1]))
            k += 2
        sums.append(rows_of([jnp.ones((1, m), f32)] * len(ys), blocks))
    r_ref[...] = jnp.concatenate(sums, 1)


def gibbs_call(n, m, xpacks, ypacks, penalty, after):
    blocks = len(xpacks) * len(ypacks)
    args = [*xpacks, *ypacks, penalty]
    *out, sums = pl.pallas_call(
        lambda *refs: gibbs_body(n, m, len(xpacks), len(ypacks), *refs[: len(args)], *refs[-2 * blocks - 1 :]),
        in_specs=[VMEM] * len(args) + [ANY] * len(after),
        out_specs=[VMEM] * (2 * blocks + 1),
        out_shape=[pltpu.VMEM((n, m), bf16)] * (2 * blocks) + [pltpu.VMEM((1, len(xpacks) * n), f32)],
        compiler_params=PARAMS,
        cost_estimate=pl.CostEstimate(
            flops=2 * blocks * n * m * LANES, transcendentals=blocks * n * m, bytes_accessed=blocks * n * m * 4
        ),
        name="gibbs",
    )(*args, *after)
    return [(out[2 * k], out[2 * k + 1]) for k in range(blocks)], sums


def total_of(refs):
    total = refs[0][...]
    for ref in refs[1:]:
        total = total + ref[...]
    return total


def cols_body(n, parts, packs, block_count, *refs):
    p = n // LANES
    total = total_of(refs[:parts])
    pack_refs = refs[parts : parts + packs]
    rest = refs[parts + packs :]
    blocks = [(rest[2 * k], rest[2 * k + 1]) for k in range(block_count)]
    u_ref, c_ref = refs[-2:]
    us = [flat(pack[n + 2 * p : n + 3 * p, :]) / total[:, k * n : (k + 1) * n] for k, pack in enumerate(pack_refs)]
    u_ref[...] = jnp.concatenate(us, 1)
    width = block_count // packs
    c_ref[...] = jnp.concatenate([cols_of(us, blocks[j::width]) for j in range(width)], 1)


def rows_body(m, parts, packs, block_count, *refs):
    q = m // LANES
    total = total_of(refs[:parts])
    pack_refs = refs[parts : parts + packs]
    rest = refs[parts + packs :]
    blocks = [(rest[2 * k], rest[2 * k + 1]) for k in range(block_count)]
    v_ref, r_ref = refs[-2:]
    vs = [flat(pack[m + q : m + 2 * q, :]) / total[:, k * m : (k + 1) * m] for k, pack in enumerate(pack_refs)]
    v_ref[...] = vs[0]
    r_ref[...] = jnp.concatenate([rows_of(vs, blocks[i : i + packs]) for i in range(0, block_count, packs)], 1)


def half_step(body, name, size, partials, packs, blocks, outs, after):
    args = [*partials, *packs, *[ref for block in blocks for ref in block]]
    return pl.pallas_call(
        lambda *refs: body(size, len(partials), len(packs), len(blocks), *refs[: len(args)], *refs[-2:]),
        in_specs=[VMEM] * len(args) + [ANY] * len(after),
        out_specs=[VMEM] * 2,
        out_shape=outs,
        compiler_params=PARAMS,
        name=name,
    )(*args, *after)


def table_body(n, first, count, f_ref, pack_ref, hi_ref, lo_ref, token_ref):
    filt = f_ref[...]
    t_count = filt.shape[0]
    merch_rows = lax.broadcasted_iota(jnp.int32, (MERCH_DEV, LANES), 0).astype(f32).astype(bf16)
    merch_cols = lax.broadcasted_iota(jnp.int32, (LANES, MERCH_DEV), 1).astype(f32).astype(bf16)
    one, zero = jnp.ones((MERCH_DEV, LANES), bf16), jnp.zeros((MERCH_DEV, LANES), bf16)
    size = math.gcd(count, UNROLL)

    def group(step, carry):
        start = pl.multiple_of(step * size, size)
        merch = pack_ref[pl.ds(first + start, size), :]
        days = pack_ref[pl.ds(n + first + start, size), :].astype(jnp.int32)
        amounts = pack_ref[pl.ds(2 * n + first + start, size), :]
        turned = jnp.transpose(merch).astype(bf16)
        merch = merch.astype(bf16)
        tables = []
        for i in range(size):
            day = jnp.broadcast_to(days[i : i + 1, :], (t_count, LANES))
            coef = jnp.take_along_axis(filt, day, axis=1, mode="promise_in_bounds")
            both = jnp.concatenate(split2(coef * amounts[i : i + 1, :]), 0)
            if i % 2:
                hot = jnp.where(merch_cols == jnp.broadcast_to(turned[:, i : i + 1], merch_cols.shape), one, zero)
                both = dot_rows(both, hot, ((1,), (0,)))
            else:
                hot = jnp.where(merch_rows == merch[i : i + 1, :], one, zero)
                both = dot_rows(both, hot, ((1,), (1,)))
            tables.append(both[:t_count] + both[t_count:])
        hi, lo = split2(jnp.swapaxes(jnp.stack(tables, 0), 0, 1))
        hi_ref[:, pl.ds(start, size), :] = hi
        lo_ref[:, pl.ds(start, size), :] = lo
        return carry

    lax.fori_loop(0, count // size, group, 0)
    token_ref[...] = jnp.zeros_like(token_ref)


def table_call(filt, pack, n, first, count, after):
    t_count = filt.shape[0]
    hi, lo, token = pl.pallas_call(
        lambda *refs: table_body(n, first, count, *refs[:2], *refs[-3:]),
        in_specs=[VMEM] * 2 + [ANY] * len(after),
        out_specs=[VMEM] * 3,
        out_shape=[pltpu.VMEM((t_count, count, LANES), bf16)] * 2 + [pltpu.VMEM((8, LANES), f32)],
        compiler_params=PARAMS,
        cost_estimate=pl.CostEstimate(
            flops=4 * count * t_count * LANES * LANES, transcendentals=0, bytes_accessed=count * 60000
        ),
        name="tables",
    )(filt, pack, *after)
    return (hi, lo), token


def spread_body(n, t_first, t_count, parts, packs, count, u_ref, *refs):
    p = n // LANES
    w = u_ref[...] * total_of(refs[:parts])
    pack_refs = refs[parts : parts + packs]
    pair_refs = refs[parts + packs : parts + packs + 2 * count]
    o_ref, w_ref = refs[-2:]
    w_ref[...] = w[:, :n]
    seg = jnp.concatenate([flat(pack[n + p : n + 2 * p, :]).astype(jnp.int32) for pack in pack_refs], 1)
    hot = lax.broadcasted_iota(jnp.int32, (SEG, w.shape[1]), 0) == seg
    whi, wlo = split2(jnp.where(hot, w, 0.0))
    both = jnp.concatenate([whi, wlo], 0)

    def take(part, t):
        return jnp.concatenate(
            [jnp.concatenate([pair_refs[2 * k + part][t + q] for k in range(count)], 0) for q in range(2)], 1
        )

    for t in range(t_first, t_first + t_count, 2):
        two = jnp.dot(both, take(0, t), preferred_element_type=f32)
        out = two[:SEG] + two[SEG:] + jnp.dot(whi, take(1, t), preferred_element_type=f32)
        o_ref[t - t_first] = out[:, :LANES]
        o_ref[t - t_first + 1] = out[:, LANES:]


def spread_call(n, u, partials, packs, pairs, t_first, t_count, after):
    refs = [ref for pair in pairs for ref in pair]
    args = [u, *partials, *packs, *refs]
    return pl.pallas_call(
        lambda *refs: spread_body(
            n, t_first, t_count, len(partials), len(packs), len(pairs), *refs[: len(args)], *refs[-2:]
        ),
        in_specs=[VMEM] * len(args) + [ANY] * len(after),
        out_specs=[VMEM] * 2,
        out_shape=[pltpu.VMEM((t_count, SEG, LANES), f32), jax.ShapeDtypeStruct((1, n), f32)],
        compiler_params=PARAMS,
        name="spread",
    )(*args, *after)


def move(x, axis, size, pair, step, flip):
    blocks = size // pair

    def away(b):
        return b ^ step if blocks & (blocks - 1) == 0 else (b + step) % blocks

    return lax.ppermute(
        x, axis, [(b * pair + r, away(b) * pair + (r ^ flip)) for b in range(blocks) for r in range(pair)]
    )


def gate(x, *after):
    return lax.optimization_barrier((x, *after))[0]


def per_device(
    n_cohort,
    n_cell,
    cohort_features,
    cell_features,
    cohort_region,
    cell_region,
    penalty,
    cohort_mass,
    cell_mass,
    cohort_segment,
    spend_merchant,
    spend_day,
    spend_amount,
):
    n, m = cohort_features.shape[0], cell_features.shape[0]
    t_dev = DAYS // n_cohort
    n_y, n_z = n_cohort // 2, n_cell // 2
    table = np.zeros((n_cohort, 2 * t_dev, LANES), np.float32)
    henderson = filter_table(DAYS)
    for me in range(n_cohort):
        for k, dest in enumerate((me ^ 1, me)):
            table[me, k * t_dev : (k + 1) * t_dev, :DAYS] = henderson[dest * t_dev : (dest + 1) * t_dev]

    over_y = lambda x: [move(x, "cohort", n_cohort, 2, step, 0) for step in range(1, n_y)]
    core = lambda x: move(x, "cohort", n_cohort, 2, 0, 1)
    along_z = lambda x: [x] + [move(x, "cell", n_cell, 2, step, 0) for step in range(1, n_z)]

    xpack, ypack, rpack, filt = first_call(
        cohort_features, cell_features, cohort_region, cohort_segment, cohort_mass, cell_region, cell_mass,
        jnp.asarray(table), (spend_merchant, spend_day, spend_amount),
    )
    xpacks = [xpack] + over_y(xpack)
    ypacks = [ypack, move(ypack, "cell", n_cell, 2, 0, 1)]
    rpacks = over_y(rpack)
    pairs = {}

    def tables(source, pack, first, count, token):
        pairs[source, first], token = table_call(filt, pack, n, first, count, [token])
        return token

    early = 3 * n // 4
    token = tables(0, rpack, 0, early, filt)
    blocks, partial = gibbs_call(n, m, xpacks, ypacks, penalty, [token])
    row_sums = lambda: pltpu.VMEM((1, len(xpacks) * n), f32)
    col_sums = lambda: pltpu.VMEM((1, len(ypacks) * m), f32)
    lines = along_z(partial)
    token = tables(0, rpack, early, n - early, partial)
    for iteration in range(ITERS):
        cohort_scale, column = half_step(
            cols_body, "cols", n, lines, xpacks, blocks, [row_sums(), col_sums()], [token]
        )
        cell_scale, partial = half_step(
            rows_body, "rows", m, [column, core(column)], ypacks, blocks,
            [jax.ShapeDtypeStruct((1, m), f32), row_sums()], [],
        )
        lines = along_z(partial)
        token = partial
        part = n // ITERS
        for source, pack in enumerate(rpacks):
            token = tables(1 + source, pack, iteration * part, part, token)
    ordered = [pairs[key] for key in sorted(pairs)]
    away, weights = spread_call(n, cohort_scale, lines, xpacks, ordered, 0, t_dev, [token])
    mine, _ = spread_call(n, cohort_scale, lines, xpacks, ordered, t_dev, t_dev, [token])
    out = mine + core(away)
    return (weights.reshape(-1), cell_scale.reshape(-1), out)


def solution(mesh):
    return jax.shard_map(
        functools.partial(per_device, mesh.shape["cohort"], mesh.shape["cell"]),
        mesh=mesh,
        in_specs=(
            P("cohort", None),
            P("cell", None),
            P("cohort"),
            P("cell"),
            P(),
            P("cohort"),
            P("cell"),
            P("cohort"),
            P("cohort", "cell"),
            P("cohort", "cell"),
            P("cohort", "cell"),
        ),
        out_specs=(P("cohort"), P("cell"), P("cohort", None, "cell")),
        check_vma=False,
    )
```

```python
import functools
import math

import jax
import jax.numpy as jnp
import numpy as np
from jax import lax
from jax.experimental import pallas as pl
from jax.experimental.pallas import tpu as pltpu
from jax.sharding import PartitionSpec as P

ITERS = 2
SEG = 32
MERCH_DEV = 128
DAYS = 64
LANES = 128
UNROLL = 128

half_span = 11

f32 = jnp.float32
bf16 = jnp.bfloat16
VMEM = pl.BlockSpec(memory_space=pltpu.VMEM)
ANY = pl.BlockSpec(memory_space=pl.ANY)
HBM = pl.BlockSpec(memory_space=pltpu.HBM)
PARAMS = pltpu.CompilerParams(vmem_limit_bytes=20 * 2**20)


def filter_table(day_count):
    outer = 13.0
    coeffs = []
    for offset_days in range(-half_span, half_span + 1):
        sq = float(offset_days * offset_days)
        top = (
            315.0
            * ((outer - 1) ** 2 - sq)
            * (outer**2 - sq)
            * ((outer + 1) ** 2 - sq)
            * (3 * outer**2 - 16 - 11 * sq)
        )
        bottom = (
            8
            * outer
            * (outer**2 - 1)
            * (4 * outer**2 - 1)
            * (4 * outer**2 - 9)
            * (4 * outer**2 - 25)
        )
        coeffs.append(top / bottom)
    matrix = np.zeros((day_count, day_count))
    for row_day in range(day_count):
        for offset_days in range(-half_span, half_span + 1):
            col_day = row_day + offset_days
            if 0 <= col_day < day_count:
                matrix[row_day, col_day] = coeffs[offset_days + half_span]
        matrix[row_day] = matrix[row_day] / matrix[row_day].sum()
    return matrix


def split2(x):
    hi = x.astype(bf16)
    return hi, (x - hi.astype(f32)).astype(bf16)


def split_rows(x):
    hi = x.astype(bf16)
    rest = x - hi.astype(f32)
    mid = rest.astype(bf16)
    low = (rest - mid.astype(f32)).astype(bf16)
    return jnp.concatenate([hi, mid, low, jnp.zeros((5, x.shape[1]), bf16)], 0)


def dot_rows(rows, k, dims):
    return lax.dot_general(rows, k, (dims, ((), ())), preferred_element_type=f32)


def cols_of(us, blocks):
    out = 0.0
    for u, (khi, klo) in zip(us, blocks):
        rows = split_rows(u)
        out = out + dot_rows(rows, khi[...], ((1,), (0,))) + dot_rows(rows, klo[...], ((1,), (0,)))
    return jnp.sum(out, axis=0, keepdims=True)


def rows_of(vs, blocks):
    out = 0.0
    for v, (khi, klo) in zip(vs, blocks):
        rows = split_rows(v)
        out = out + dot_rows(rows, khi[...], ((1,), (1,))) + dot_rows(rows, klo[...], ((1,), (1,)))
    return jnp.sum(out, axis=0, keepdims=True)


def kernel_block(x, y, row_region, col_region, penalty):
    n, m = x.shape[0], y.shape[0]
    regions = penalty.shape[0]
    inv_root = 1.0 / math.sqrt(x.shape[1])
    inner = dot_rows(x, y, ((1,), (1,)))
    row_hot = (lax.broadcasted_iota(jnp.int32, (regions, n), 0) == row_region).astype(f32).astype(bf16)
    col_hot = (lax.broadcasted_iota(jnp.int32, (regions, m), 0) == col_region).astype(f32).astype(bf16)
    phi, plo = split2(penalty)
    qhi = jnp.dot(phi, col_hot, preferred_element_type=f32).astype(bf16)
    qlo = jnp.dot(plo, col_hot, preferred_element_type=f32).astype(bf16)
    pen = dot_rows(jnp.concatenate([row_hot, row_hot], 0), jnp.concatenate([qhi, qlo], 0), ((0,), (0,)))
    return split2(jnp.exp(inner * inv_root - pen))


def run_copies(pairs, sems):
    copies = [pltpu.make_async_copy(src, dst, sems.at[k]) for k, (src, dst) in enumerate(pairs)]
    for copy in copies:
        copy.start()
    return copies


def first_body(
    x_hbm, y_hbm, rr_hbm, seg_hbm, mass_hbm, cr_hbm, cm_hbm, f_hbm, m_hbm, d_hbm, a_hbm,
    xpack_ref, ypack_ref, rpack_ref, f_ref, xb_ref, yb_ref, rr_ref, seg_ref, cr_ref, m_ref, d_ref, sems,
):
    me = lax.axis_index("cohort")
    n, m = xb_ref.shape[0], yb_ref.shape[0]
    p, q = n // LANES, m // LANES
    copies = run_copies(
        (
            (x_hbm, xb_ref),
            (rr_hbm, rr_ref),
            (seg_hbm, seg_ref),
            (mass_hbm, xpack_ref.at[pl.ds(n + 2 * p, p), :]),
            (y_hbm, yb_ref),
            (cr_hbm, cr_ref),
            (cm_hbm, ypack_ref.at[pl.ds(m + q, q), :]),
            (m_hbm, m_ref),
            (d_hbm, d_ref),
            (a_hbm, rpack_ref.at[pl.ds(2 * n, n), :]),
            (f_hbm.at[me], f_ref),
        ),
        sems,
    )
    for copy in copies:
        copy.wait()
    xpack_ref[0:n, :] = xb_ref[...].astype(f32)
    xpack_ref[n : n + p, :] = rr_ref[...].astype(f32)
    xpack_ref[n + p : n + 2 * p, :] = seg_ref[...].astype(f32)
    ypack_ref[0:m, :] = yb_ref[...].astype(f32)
    ypack_ref[m : m + q, :] = cr_ref[...].astype(f32)
    rpack_ref[0:n, :] = m_ref[...].astype(f32)
    rpack_ref[n : 2 * n, :] = d_ref[...].astype(f32)


def first_call(x, y, rr, seg, mass, cr, cm, table, records):
    n, m = x.shape[0], y.shape[0]
    p, q = n // LANES, m // LANES
    block = lambda v: v.reshape(-1, LANES)
    i32 = jnp.int32
    out = [(n + 3 * p, LANES), (m + 2 * q, LANES), (3 * n, LANES), table.shape[1:]]
    args = (x, y, block(rr), block(seg), block(mass), block(cr), block(cm), table, *records)
    return pl.pallas_call(
        first_body,
        in_specs=[HBM] * len(args),
        out_specs=[VMEM] * len(out),
        out_shape=[pltpu.VMEM(shape, f32) for shape in out],
        scratch_shapes=[
            pltpu.VMEM(x.shape, bf16),
            pltpu.VMEM(y.shape, bf16),
            pltpu.VMEM((p, LANES), i32),
            pltpu.VMEM((p, LANES), i32),
            pltpu.VMEM((q, LANES), i32),
            pltpu.VMEM((n, LANES), i32),
            pltpu.VMEM((n, LANES), i32),
            pltpu.SemaphoreType.DMA((len(args),)),
        ],
        compiler_params=PARAMS,
        name="first",
    )(*[pltpu.with_memory_space_constraint(arg, pltpu.HBM) for arg in args])


def flat(block):
    return jnp.concatenate([block[k : k + 1, :] for k in range(block.shape[0])], 1)


def gibbs_body(n, m, packs_x, packs_y, *refs):
    xpacks, ypacks, pen_ref = refs[:packs_x], refs[packs_x : packs_x + packs_y], refs[packs_x + packs_y]
    outs = refs[packs_x + packs_y + 1 : -1]
    r_ref = refs[-1]
    p, q = n // LANES, m // LANES
    pen = pen_ref[...]
    xs = [(pack[0:n, :].astype(bf16), flat(pack[n : n + p, :]).astype(jnp.int32)) for pack in xpacks]
    ys = [(pack[0:m, :].astype(bf16), flat(pack[m : m + q, :]).astype(jnp.int32)) for pack in ypacks]
    k = 0
    sums = []
    for x, rr in xs:
        blocks = []
        for y, cr in ys:
            outs[k][...], outs[k + 1][...] = kernel_block(x, y, rr, cr, pen)
            blocks.append((outs[k], outs[k + 1]))
            k += 2
        sums.append(rows_of([jnp.ones((1, m), f32)] * len(ys), blocks))
    r_ref[...] = jnp.concatenate(sums, 1)


def gibbs_call(n, m, xpacks, ypacks, penalty, after):
    blocks = len(xpacks) * len(ypacks)
    args = [*xpacks, *ypacks, penalty]
    *out, sums = pl.pallas_call(
        lambda *refs: gibbs_body(n, m, len(xpacks), len(ypacks), *refs[: len(args)], *refs[-2 * blocks - 1 :]),
        in_specs=[VMEM] * len(args) + [ANY] * len(after),
        out_specs=[VMEM] * (2 * blocks + 1),
        out_shape=[pltpu.VMEM((n, m), bf16)] * (2 * blocks) + [pltpu.VMEM((1, len(xpacks) * n), f32)],
        compiler_params=PARAMS,
        cost_estimate=pl.CostEstimate(
            flops=2 * blocks * n * m * LANES, transcendentals=blocks * n * m, bytes_accessed=blocks * n * m * 4
        ),
        name="gibbs",
    )(*args, *after)
    return [(out[2 * k], out[2 * k + 1]) for k in range(blocks)], sums


def total_of(refs):
    total = refs[0][...]
    for ref in refs[1:]:
        total = total + ref[...]
    return total


def cols_body(n, parts, packs, block_count, *refs):
    p = n // LANES
    total = total_of(refs[:parts])
    pack_refs = refs[parts : parts + packs]
    rest = refs[parts + packs :]
    blocks = [(rest[2 * k], rest[2 * k + 1]) for k in range(block_count)]
    u_ref, c_ref = refs[-2:]
    us = [flat(pack[n + 2 * p : n + 3 * p, :]) / total[:, k * n : (k + 1) * n] for k, pack in enumerate(pack_refs)]
    u_ref[...] = jnp.concatenate(us, 1)
    width = block_count // packs
    c_ref[...] = jnp.concatenate([cols_of(us, blocks[j::width]) for j in range(width)], 1)


def rows_body(m, parts, packs, block_count, *refs):
    q = m // LANES
    total = total_of(refs[:parts])
    pack_refs = refs[parts : parts + packs]
    rest = refs[parts + packs :]
    blocks = [(rest[2 * k], rest[2 * k + 1]) for k in range(block_count)]
    v_ref, r_ref = refs[-2:]
    vs = [flat(pack[m + q : m + 2 * q, :]) / total[:, k * m : (k + 1) * m] for k, pack in enumerate(pack_refs)]
    v_ref[...] = vs[0]
    r_ref[...] = jnp.concatenate([rows_of(vs, blocks[i : i + packs]) for i in range(0, block_count, packs)], 1)


def half_step(body, name, size, partials, packs, blocks, outs, after):
    args = [*partials, *packs, *[ref for block in blocks for ref in block]]
    return pl.pallas_call(
        lambda *refs: body(size, len(partials), len(packs), len(blocks), *refs[: len(args)], *refs[-2:]),
        in_specs=[VMEM] * len(args) + [ANY] * len(after),
        out_specs=[VMEM] * 2,
        out_shape=outs,
        compiler_params=PARAMS,
        name=name,
    )(*args, *after)


def table_body(n, first, count, f_ref, pack_ref, hi_ref, lo_ref, token_ref):
    filt = f_ref[...]
    t_count = filt.shape[0]
    merch_rows = lax.broadcasted_iota(jnp.int32, (MERCH_DEV, LANES), 0).astype(f32).astype(bf16)
    merch_cols = lax.broadcasted_iota(jnp.int32, (LANES, MERCH_DEV), 1).astype(f32).astype(bf16)
    one, zero = jnp.ones((MERCH_DEV, LANES), bf16), jnp.zeros((MERCH_DEV, LANES), bf16)
    size = math.gcd(count, UNROLL)

    def group(step, carry):
        start = pl.multiple_of(step * size, size)
        merch = pack_ref[pl.ds(first + start, size), :]
        days = pack_ref[pl.ds(n + first + start, size), :].astype(jnp.int32)
        amounts = pack_ref[pl.ds(2 * n + first + start, size), :]
        turned = jnp.transpose(merch).astype(bf16)
        merch = merch.astype(bf16)
        tables = []
        for i in range(size):
            day = jnp.broadcast_to(days[i : i + 1, :], (t_count, LANES))
            coef = jnp.take_along_axis(filt, day, axis=1, mode="promise_in_bounds")
            both = jnp.concatenate(split2(coef * amounts[i : i + 1, :]), 0)
            if i % 2:
                hot = jnp.where(merch_cols == jnp.broadcast_to(turned[:, i : i + 1], merch_cols.shape), one, zero)
                both = dot_rows(both, hot, ((1,), (0,)))
            else:
                hot = jnp.where(merch_rows == merch[i : i + 1, :], one, zero)
                both = dot_rows(both, hot, ((1,), (1,)))
            tables.append(both[:t_count] + both[t_count:])
        hi, lo = split2(jnp.swapaxes(jnp.stack(tables, 0), 0, 1))
        hi_ref[:, pl.ds(start, size), :] = hi
        lo_ref[:, pl.ds(start, size), :] = lo
        return carry

    lax.fori_loop(0, count // size, group, 0)
    token_ref[...] = jnp.zeros_like(token_ref)


def table_call(filt, pack, n, first, count, after):
    t_count = filt.shape[0]
    hi, lo, token = pl.pallas_call(
        lambda *refs: table_body(n, first, count, *refs[:2], *refs[-3:]),
        in_specs=[VMEM] * 2 + [ANY] * len(after),
        out_specs=[VMEM] * 3,
        out_shape=[pltpu.VMEM((t_count, count, LANES), bf16)] * 2 + [pltpu.VMEM((8, LANES), f32)],
        compiler_params=PARAMS,
        cost_estimate=pl.CostEstimate(
            flops=4 * count * t_count * LANES * LANES, transcendentals=0, bytes_accessed=count * 60000
        ),
        name="tables",
    )(filt, pack, *after)
    return (hi, lo), token


def spread_body(n, t_first, t_count, parts, packs, count, u_ref, *refs):
    p = n // LANES
    w = u_ref[...] * total_of(refs[:parts])
    pack_refs = refs[parts : parts + packs]
    pair_refs = refs[parts + packs : parts + packs + 2 * count]
    o_ref, w_ref = refs[-2:]
    w_ref[...] = w[:, :n]
    seg = jnp.concatenate([flat(pack[n + p : n + 2 * p, :]).astype(jnp.int32) for pack in pack_refs], 1)
    hot = lax.broadcasted_iota(jnp.int32, (SEG, w.shape[1]), 0) == seg
    whi, wlo = split2(jnp.where(hot, w, 0.0))
    both = jnp.concatenate([whi, wlo], 0)

    def take(part, t):
        return jnp.concatenate(
            [jnp.concatenate([pair_refs[2 * k + part][t + q] for k in range(count)], 0) for q in range(2)], 1
        )

    for t in range(t_first, t_first + t_count, 2):
        two = jnp.dot(both, take(0, t), preferred_element_type=f32)
        out = two[:SEG] + two[SEG:] + jnp.dot(whi, take(1, t), preferred_element_type=f32)
        o_ref[t - t_first] = out[:, :LANES]
        o_ref[t - t_first + 1] = out[:, LANES:]


def spread_call(n, u, partials, packs, pairs, t_first, t_count, after):
    refs = [ref for pair in pairs for ref in pair]
    args = [u, *partials, *packs, *refs]
    return pl.pallas_call(
        lambda *refs: spread_body(
            n, t_first, t_count, len(partials), len(packs), len(pairs), *refs[: len(args)], *refs[-2:]
        ),
        in_specs=[VMEM] * len(args) + [ANY] * len(after),
        out_specs=[VMEM] * 2,
        out_shape=[pltpu.VMEM((t_count, SEG, LANES), f32), jax.ShapeDtypeStruct((1, n), f32)],
        compiler_params=PARAMS,
        name="spread",
    )(*args, *after)


def move(x, axis, size, pair, step, flip):
    blocks = size // pair

    def away(b):
        return b ^ step if blocks & (blocks - 1) == 0 else (b + step) % blocks

    return lax.ppermute(
        x, axis, [(b * pair + r, away(b) * pair + (r ^ flip)) for b in range(blocks) for r in range(pair)]
    )


def gate(x, *after):
    return lax.optimization_barrier((x, *after))[0]


def per_device(
    n_cohort,
    n_cell,
    cohort_features,
    cell_features,
    cohort_region,
    cell_region,
    penalty,
    cohort_mass,
    cell_mass,
    cohort_segment,
    spend_merchant,
    spend_day,
    spend_amount,
):
    n, m = cohort_features.shape[0], cell_features.shape[0]
    t_dev = DAYS // n_cohort
    n_y, n_z = n_cohort // 2, n_cell // 2
    table = np.zeros((n_cohort, 2 * t_dev, LANES), np.float32)
    henderson = filter_table(DAYS)
    for me in range(n_cohort):
        for k, dest in enumerate((me ^ 1, me)):
            table[me, k * t_dev : (k + 1) * t_dev, :DAYS] = henderson[dest * t_dev : (dest + 1) * t_dev]

    over_y = lambda x: [move(x, "cohort", n_cohort, 2, step, 0) for step in range(1, n_y)]
    core = lambda x: move(x, "cohort", n_cohort, 2, 0, 1)
    along_z = lambda x: [x] + [move(x, "cell", n_cell, 2, step, 0) for step in range(1, n_z)]

    xpack, ypack, rpack, filt = first_call(
        cohort_features, cell_features, cohort_region, cohort_segment, cohort_mass, cell_region, cell_mass,
        jnp.asarray(table), (spend_merchant, spend_day, spend_amount),
    )
    xpacks = [xpack] + over_y(xpack)
    ypacks = [ypack, move(ypack, "cell", n_cell, 2, 0, 1)]
    rpacks = over_y(gate(rpack, *xpacks))
    pairs = {}

    def tables(source, pack, first, count, token):
        pairs[source, first], token = table_call(filt, pack, n, first, count, [token])
        return token

    early = 3 * n // 4
    token = tables(0, rpack, 0, early, filt)
    blocks, partial = gibbs_call(n, m, xpacks, ypacks, penalty, [token])
    row_sums = lambda: pltpu.VMEM((1, len(xpacks) * n), f32)
    col_sums = lambda: pltpu.VMEM((1, len(ypacks) * m), f32)
    lines = along_z(partial)
    token = tables(0, rpack, early, n - early, partial)
    for iteration in range(ITERS):
        cohort_scale, column = half_step(
            cols_body, "cols", n, lines, xpacks, blocks, [row_sums(), col_sums()], [token]
        )
        cell_scale, partial = half_step(
            rows_body, "rows", m, [column, core(column)], ypacks, blocks,
            [jax.ShapeDtypeStruct((1, m), f32), row_sums()], [],
        )
        lines = along_z(partial)
        token = partial
        part = n // ITERS
        for source, pack in enumerate(rpacks):
            token = tables(1 + source, pack, iteration * part, part, token)
    ordered = [pairs[key] for key in sorted(pairs)]
    away, weights = spread_call(n, cohort_scale, lines, xpacks, ordered, 0, t_dev, [token])
    mine, _ = spread_call(n, cohort_scale, lines, xpacks, ordered, t_dev, t_dev, [token])
    out = mine + core(away)
    return (weights.reshape(-1), cell_scale.reshape(-1), out)


def solution(mesh):
    return jax.shard_map(
        functools.partial(per_device, mesh.shape["cohort"], mesh.shape["cell"]),
        mesh=mesh,
        in_specs=(
            P("cohort", None),
            P("cell", None),
            P("cohort"),
            P("cell"),
            P(),
            P("cohort"),
            P("cell"),
            P("cohort"),
            P("cohort", "cell"),
            P("cohort", "cell"),
            P("cohort", "cell"),
        ),
        out_specs=(P("cohort"), P("cell"), P("cohort", None, "cell")),
        check_vma=False,
    )
```

```python
import functools
import math

import jax
import jax.numpy as jnp
import numpy as np
from jax import lax
from jax.experimental import pallas as pl
from jax.experimental.pallas import tpu as pltpu
from jax.sharding import PartitionSpec as P

ITERS = 2
SEG = 32
MERCH_DEV = 128
DAYS = 64
LANES = 128
UNROLL = 128

half_span = 11

f32 = jnp.float32
bf16 = jnp.bfloat16
VMEM = pl.BlockSpec(memory_space=pltpu.VMEM)
ANY = pl.BlockSpec(memory_space=pl.ANY)
HBM = pl.BlockSpec(memory_space=pltpu.HBM)
PARAMS = pltpu.CompilerParams(vmem_limit_bytes=20 * 2**20)


def filter_table(day_count):
    outer = 13.0
    coeffs = []
    for offset_days in range(-half_span, half_span + 1):
        sq = float(offset_days * offset_days)
        top = (
            315.0
            * ((outer - 1) ** 2 - sq)
            * (outer**2 - sq)
            * ((outer + 1) ** 2 - sq)
            * (3 * outer**2 - 16 - 11 * sq)
        )
        bottom = (
            8
            * outer
            * (outer**2 - 1)
            * (4 * outer**2 - 1)
            * (4 * outer**2 - 9)
            * (4 * outer**2 - 25)
        )
        coeffs.append(top / bottom)
    matrix = np.zeros((day_count, day_count))
    for row_day in range(day_count):
        for offset_days in range(-half_span, half_span + 1):
            col_day = row_day + offset_days
            if 0 <= col_day < day_count:
                matrix[row_day, col_day] = coeffs[offset_days + half_span]
        matrix[row_day] = matrix[row_day] / matrix[row_day].sum()
    return matrix


def split2(x):
    hi = x.astype(bf16)
    return hi, (x - hi.astype(f32)).astype(bf16)


def split_rows(x):
    hi = x.astype(bf16)
    rest = x - hi.astype(f32)
    mid = rest.astype(bf16)
    low = (rest - mid.astype(f32)).astype(bf16)
    return jnp.concatenate([hi, mid, low, jnp.zeros((5, x.shape[1]), bf16)], 0)


def dot_rows(rows, k, dims):
    return lax.dot_general(rows, k, (dims, ((), ())), preferred_element_type=f32)


def cols_of(us, blocks):
    out = 0.0
    for u, (khi, klo) in zip(us, blocks):
        rows = split_rows(u)
        out = out + dot_rows(rows, khi[...], ((1,), (0,))) + dot_rows(rows, klo[...], ((1,), (0,)))
    return jnp.sum(out, axis=0, keepdims=True)


def rows_of(vs, blocks):
    out = 0.0
    for v, (khi, klo) in zip(vs, blocks):
        rows = split_rows(v)
        out = out + dot_rows(rows, khi[...], ((1,), (1,))) + dot_rows(rows, klo[...], ((1,), (1,)))
    return jnp.sum(out, axis=0, keepdims=True)


def kernel_block(x, y, row_region, col_region, penalty):
    n, m = x.shape[0], y.shape[0]
    regions = penalty.shape[0]
    inv_root = 1.0 / math.sqrt(x.shape[1])
    inner = dot_rows(x, y, ((1,), (1,)))
    row_hot = (lax.broadcasted_iota(jnp.int32, (regions, n), 0) == row_region).astype(f32).astype(bf16)
    col_hot = (lax.broadcasted_iota(jnp.int32, (regions, m), 0) == col_region).astype(f32).astype(bf16)
    phi, plo = split2(penalty)
    qhi = jnp.dot(phi, col_hot, preferred_element_type=f32).astype(bf16)
    qlo = jnp.dot(plo, col_hot, preferred_element_type=f32).astype(bf16)
    pen = dot_rows(jnp.concatenate([row_hot, row_hot], 0), jnp.concatenate([qhi, qlo], 0), ((0,), (0,)))
    return split2(jnp.exp(inner * inv_root - pen))


def run_copies(pairs, sems):
    copies = [pltpu.make_async_copy(src, dst, sems.at[k]) for k, (src, dst) in enumerate(pairs)]
    for copy in copies:
        copy.start()
    return copies


def first_body(
    x_hbm, y_hbm, rr_hbm, seg_hbm, mass_hbm, cr_hbm, cm_hbm, f_hbm, m_hbm, d_hbm, a_hbm,
    xpack_ref, ypack_ref, rpack_ref, f_ref, xb_ref, yb_ref, rr_ref, seg_ref, cr_ref, m_ref, d_ref, sems,
):
    me = lax.axis_index("cohort")
    n, m = xb_ref.shape[0], yb_ref.shape[0]
    p, q = n // LANES, m // LANES
    copies = run_copies(
        (
            (x_hbm, xb_ref),
            (rr_hbm, rr_ref),
            (seg_hbm, seg_ref),
            (mass_hbm, xpack_ref.at[pl.ds(n + 2 * p, p), :]),
            (y_hbm, yb_ref),
            (cr_hbm, cr_ref),
            (cm_hbm, ypack_ref.at[pl.ds(m + q, q), :]),
            (m_hbm, m_ref),
            (d_hbm, d_ref),
            (a_hbm, rpack_ref.at[pl.ds(2 * n, n), :]),
            (f_hbm.at[me], f_ref),
        ),
        sems,
    )
    for copy in copies:
        copy.wait()
    xpack_ref[0:n, :] = xb_ref[...].astype(f32)
    xpack_ref[n : n + p, :] = rr_ref[...].astype(f32)
    xpack_ref[n + p : n + 2 * p, :] = seg_ref[...].astype(f32)
    ypack_ref[0:m, :] = yb_ref[...].astype(f32)
    ypack_ref[m : m + q, :] = cr_ref[...].astype(f32)
    rpack_ref[0:n, :] = m_ref[...].astype(f32)
    rpack_ref[n : 2 * n, :] = d_ref[...].astype(f32)


def first_call(x, y, rr, seg, mass, cr, cm, table, records):
    n, m = x.shape[0], y.shape[0]
    p, q = n // LANES, m // LANES
    block = lambda v: v.reshape(-1, LANES)
    i32 = jnp.int32
    out = [(n + 3 * p, LANES), (m + 2 * q, LANES), (3 * n, LANES), table.shape[1:]]
    args = (x, y, block(rr), block(seg), block(mass), block(cr), block(cm), table, *records)
    return pl.pallas_call(
        first_body,
        in_specs=[HBM] * len(args),
        out_specs=[VMEM] * len(out),
        out_shape=[pltpu.VMEM(shape, f32) for shape in out],
        scratch_shapes=[
            pltpu.VMEM(x.shape, bf16),
            pltpu.VMEM(y.shape, bf16),
            pltpu.VMEM((p, LANES), i32),
            pltpu.VMEM((p, LANES), i32),
            pltpu.VMEM((q, LANES), i32),
            pltpu.VMEM((n, LANES), i32),
            pltpu.VMEM((n, LANES), i32),
            pltpu.SemaphoreType.DMA((len(args),)),
        ],
        compiler_params=PARAMS,
        name="first",
    )(*[pltpu.with_memory_space_constraint(arg, pltpu.HBM) for arg in args])


def flat(block):
    return jnp.concatenate([block[k : k + 1, :] for k in range(block.shape[0])], 1)


def gibbs_body(n, m, packs_x, packs_y, *refs):
    xpacks, ypacks, pen_ref = refs[:packs_x], refs[packs_x : packs_x + packs_y], refs[packs_x + packs_y]
    outs = refs[packs_x + packs_y + 1 : -1]
    r_ref = refs[-1]
    p, q = n // LANES, m // LANES
    pen = pen_ref[...]
    xs = [(pack[0:n, :].astype(bf16), flat(pack[n : n + p, :]).astype(jnp.int32)) for pack in xpacks]
    ys = [(pack[0:m, :].astype(bf16), flat(pack[m : m + q, :]).astype(jnp.int32)) for pack in ypacks]
    k = 0
    sums = []
    for x, rr in xs:
        blocks = []
        for y, cr in ys:
            outs[k][...], outs[k + 1][...] = kernel_block(x, y, rr, cr, pen)
            blocks.append((outs[k], outs[k + 1]))
            k += 2
        sums.append(rows_of([jnp.ones((1, m), f32)] * len(ys), blocks))
    r_ref[...] = jnp.concatenate(sums, 1)


def gibbs_call(n, m, xpacks, ypacks, penalty, after):
    blocks = len(xpacks) * len(ypacks)
    args = [*xpacks, *ypacks, penalty]
    *out, sums = pl.pallas_call(
        lambda *refs: gibbs_body(n, m, len(xpacks), len(ypacks), *refs[: len(args)], *refs[-2 * blocks - 1 :]),
        in_specs=[VMEM] * len(args) + [ANY] * len(after),
        out_specs=[VMEM] * (2 * blocks + 1),
        out_shape=[pltpu.VMEM((n, m), bf16)] * (2 * blocks) + [pltpu.VMEM((1, len(xpacks) * n), f32)],
        compiler_params=PARAMS,
        cost_estimate=pl.CostEstimate(
            flops=2 * blocks * n * m * LANES, transcendentals=blocks * n * m, bytes_accessed=blocks * n * m * 4
        ),
        name="gibbs",
    )(*args, *after)
    return [(out[2 * k], out[2 * k + 1]) for k in range(blocks)], sums


def total_of(refs):
    total = refs[0][...]
    for ref in refs[1:]:
        total = total + ref[...]
    return total


def cols_body(n, parts, packs, block_count, *refs):
    p = n // LANES
    total = total_of(refs[:parts])
    pack_refs = refs[parts : parts + packs]
    rest = refs[parts + packs :]
    blocks = [(rest[2 * k], rest[2 * k + 1]) for k in range(block_count)]
    u_ref, c_ref = refs[-2:]
    us = [flat(pack[n + 2 * p : n + 3 * p, :]) / total[:, k * n : (k + 1) * n] for k, pack in enumerate(pack_refs)]
    u_ref[...] = jnp.concatenate(us, 1)
    width = block_count // packs
    c_ref[...] = jnp.concatenate([cols_of(us, blocks[j::width]) for j in range(width)], 1)


def rows_body(m, parts, packs, block_count, *refs):
    q = m // LANES
    total = total_of(refs[:parts])
    pack_refs = refs[parts : parts + packs]
    rest = refs[parts + packs :]
    blocks = [(rest[2 * k], rest[2 * k + 1]) for k in range(block_count)]
    v_ref, r_ref = refs[-2:]
    vs = [flat(pack[m + q : m + 2 * q, :]) / total[:, k * m : (k + 1) * m] for k, pack in enumerate(pack_refs)]
    v_ref[...] = vs[0]
    r_ref[...] = jnp.concatenate([rows_of(vs, blocks[i : i + packs]) for i in range(0, block_count, packs)], 1)


def half_step(body, name, size, partials, packs, blocks, outs, after):
    args = [*partials, *packs, *[ref for block in blocks for ref in block]]
    return pl.pallas_call(
        lambda *refs: body(size, len(partials), len(packs), len(blocks), *refs[: len(args)], *refs[-2:]),
        in_specs=[VMEM] * len(args) + [ANY] * len(after),
        out_specs=[VMEM] * 2,
        out_shape=outs,
        compiler_params=PARAMS,
        name=name,
    )(*args, *after)


def table_body(n, first, count, f_ref, pack_ref, hi_ref, lo_ref, token_ref):
    filt = f_ref[...]
    t_count = filt.shape[0]
    merch_rows = lax.broadcasted_iota(jnp.int32, (MERCH_DEV, LANES), 0).astype(f32).astype(bf16)
    merch_cols = lax.broadcasted_iota(jnp.int32, (LANES, MERCH_DEV), 1).astype(f32).astype(bf16)
    one, zero = jnp.ones((MERCH_DEV, LANES), bf16), jnp.zeros((MERCH_DEV, LANES), bf16)
    size = math.gcd(count, UNROLL)

    def group(step, carry):
        start = pl.multiple_of(step * size, size)
        merch = pack_ref[pl.ds(first + start, size), :]
        days = pack_ref[pl.ds(n + first + start, size), :].astype(jnp.int32)
        amounts = pack_ref[pl.ds(2 * n + first + start, size), :]
        turned = jnp.transpose(merch).astype(bf16)
        merch = merch.astype(bf16)
        tables = []
        for i in range(size):
            day = jnp.broadcast_to(days[i : i + 1, :], (t_count, LANES))
            coef = jnp.take_along_axis(filt, day, axis=1, mode="promise_in_bounds")
            both = jnp.concatenate(split2(coef * amounts[i : i + 1, :]), 0)
            if i % 2:
                hot = jnp.where(merch_cols == jnp.broadcast_to(turned[:, i : i + 1], merch_cols.shape), one, zero)
                both = dot_rows(both, hot, ((1,), (0,)))
            else:
                hot = jnp.where(merch_rows == merch[i : i + 1, :], one, zero)
                both = dot_rows(both, hot, ((1,), (1,)))
            tables.append(both[:t_count] + both[t_count:])
        hi, lo = split2(jnp.swapaxes(jnp.stack(tables, 0), 0, 1))
        hi_ref[:, pl.ds(start, size), :] = hi
        lo_ref[:, pl.ds(start, size), :] = lo
        return carry

    lax.fori_loop(0, count // size, group, 0)
    token_ref[...] = jnp.zeros_like(token_ref)


def table_call(filt, pack, n, first, count, after):
    t_count = filt.shape[0]
    hi, lo, token = pl.pallas_call(
        lambda *refs: table_body(n, first, count, *refs[:2], *refs[-3:]),
        in_specs=[VMEM] * 2 + [ANY] * len(after),
        out_specs=[VMEM] * 3,
        out_shape=[pltpu.VMEM((t_count, count, LANES), bf16)] * 2 + [pltpu.VMEM((8, LANES), f32)],
        compiler_params=PARAMS,
        cost_estimate=pl.CostEstimate(
            flops=4 * count * t_count * LANES * LANES, transcendentals=0, bytes_accessed=count * 60000
        ),
        name="tables",
    )(filt, pack, *after)
    return (hi, lo), token


def spread_body(n, t_first, t_count, parts, packs, count, u_ref, *refs):
    p = n // LANES
    w = u_ref[...] * total_of(refs[:parts])
    pack_refs = refs[parts : parts + packs]
    pair_refs = refs[parts + packs : parts + packs + 2 * count]
    o_ref, w_ref = refs[-2:]
    w_ref[...] = w[:, :n]
    seg = jnp.concatenate([flat(pack[n + p : n + 2 * p, :]).astype(jnp.int32) for pack in pack_refs], 1)
    hot = lax.broadcasted_iota(jnp.int32, (SEG, w.shape[1]), 0) == seg
    whi, wlo = split2(jnp.where(hot, w, 0.0))
    both = jnp.concatenate([whi, wlo], 0)

    def take(part, t):
        return jnp.concatenate(
            [jnp.concatenate([pair_refs[2 * k + part][t + q] for k in range(count)], 0) for q in range(2)], 1
        )

    for t in range(t_first, t_first + t_count, 2):
        two = jnp.dot(both, take(0, t), preferred_element_type=f32)
        out = two[:SEG] + two[SEG:] + jnp.dot(whi, take(1, t), preferred_element_type=f32)
        o_ref[t - t_first] = out[:, :LANES]
        o_ref[t - t_first + 1] = out[:, LANES:]


def spread_call(n, u, partials, packs, pairs, t_first, t_count, after):
    refs = [ref for pair in pairs for ref in pair]
    args = [u, *partials, *packs, *refs]
    return pl.pallas_call(
        lambda *refs: spread_body(
            n, t_first, t_count, len(partials), len(packs), len(pairs), *refs[: len(args)], *refs[-2:]
        ),
        in_specs=[VMEM] * len(args) + [ANY] * len(after),
        out_specs=[VMEM] * 2,
        out_shape=[pltpu.VMEM((t_count, SEG, LANES), f32), jax.ShapeDtypeStruct((1, n), f32)],
        compiler_params=PARAMS,
        name="spread",
    )(*args, *after)


def move(x, axis, size, pair, step, flip):
    blocks = size // pair

    def away(b):
        return b ^ step if blocks & (blocks - 1) == 0 else (b + step) % blocks

    return lax.ppermute(
        x, axis, [(b * pair + r, away(b) * pair + (r ^ flip)) for b in range(blocks) for r in range(pair)]
    )


def gate(x, *after):
    return lax.optimization_barrier((x, *after))[0]


def per_device(
    n_cohort,
    n_cell,
    cohort_features,
    cell_features,
    cohort_region,
    cell_region,
    penalty,
    cohort_mass,
    cell_mass,
    cohort_segment,
    spend_merchant,
    spend_day,
    spend_amount,
):
    n, m = cohort_features.shape[0], cell_features.shape[0]
    t_dev = DAYS // n_cohort
    n_y, n_z = n_cohort // 2, n_cell // 2
    table = np.zeros((n_cohort, 2 * t_dev, LANES), np.float32)
    henderson = filter_table(DAYS)
    for me in range(n_cohort):
        for k, dest in enumerate((me ^ 1, me)):
            table[me, k * t_dev : (k + 1) * t_dev, :DAYS] = henderson[dest * t_dev : (dest + 1) * t_dev]

    over_y = lambda x: [move(x, "cohort", n_cohort, 2, step, 0) for step in range(1, n_y)]
    core = lambda x: move(x, "cohort", n_cohort, 2, 0, 1)
    along_z = lambda x: [x] + [move(x, "cell", n_cell, 2, step, 0) for step in range(1, n_z)]

    xpack, ypack, rpack, filt = first_call(
        cohort_features, cell_features, cohort_region, cohort_segment, cohort_mass, cell_region, cell_mass,
        jnp.asarray(table), (spend_merchant, spend_day, spend_amount),
    )
    xpacks = [xpack] + over_y(xpack)
    ypacks = [ypack, move(ypack, "cell", n_cell, 2, 0, 1)]
    pairs = {}
    unit = n // 8

    def tables(source, first, units, *after):
        for size in (units & ~1, units & 1):
            if size:
                pack = rpack if source == 0 else rpacks[source - 1]
                pairs[source, first], token = table_call(filt, pack, n, first * unit, size * unit, after)
                after, first = [token], first + size
        return after

    def others(first, units, *after):
        for source in range(1, n_y):
            after = tables(source, first, units, *after)
        return after

    after = tables(0, 0, 6, filt)
    rpacks = over_y(gate(rpack, *xpacks, *ypacks, *after))
    blocks, partial = gibbs_call(n, m, xpacks, ypacks, penalty, after)
    row_sums = pltpu.VMEM((1, len(xpacks) * n), f32)
    col_sums = pltpu.VMEM((1, len(ypacks) * m), f32)
    fills = [
        [lambda *after: tables(0, 6, 1, *after), lambda *after: tables(0, 7, 1, *after)],
        [lambda *after: others(0, 4, *after), lambda *after: others(4, 1, *after)],
        [lambda *after: others(5, 3, *after)],
    ]
    lines = along_z(partial)
    after = fills[0][0](partial)
    for iteration in range(ITERS):
        cohort_scale, column = half_step(
            cols_body, "cols", n, lines, xpacks, blocks, [row_sums, col_sums], after
        )
        sibling = core(column)
        after = fills[iteration][1](column)
        cell_scale, partial = half_step(
            rows_body, "rows", m, [column, sibling], ypacks, blocks,
            [jax.ShapeDtypeStruct((1, m), f32), row_sums], after,
        )
        lines = along_z(partial)
        after = fills[iteration + 1][0](partial)
    ordered = [pairs[key] for key in sorted(pairs)]
    away, weights = spread_call(n, cohort_scale, lines, xpacks, ordered, 0, t_dev, after)
    mine, _ = spread_call(n, cohort_scale, lines, xpacks, ordered, t_dev, t_dev, after)
    out = mine + core(away)
    return (weights.reshape(-1), cell_scale.reshape(-1), out)


def solution(mesh):
    return jax.shard_map(
        functools.partial(per_device, mesh.shape["cohort"], mesh.shape["cell"]),
        mesh=mesh,
        in_specs=(
            P("cohort", None),
            P("cell", None),
            P("cohort"),
            P("cell"),
            P(),
            P("cohort"),
            P("cell"),
            P("cohort"),
            P("cohort", "cell"),
            P("cohort", "cell"),
            P("cohort", "cell"),
        ),
        out_specs=(P("cohort"), P("cell"), P("cohort", None, "cell")),
        check_vma=False,
    )
```

```python
import functools
import math

import jax
import jax.numpy as jnp
import numpy as np
from jax import lax
from jax.experimental import pallas as pl
from jax.experimental.pallas import tpu as pltpu
from jax.sharding import PartitionSpec as P

ITERS = 2
SEG = 32
MERCH_DEV = 128
DAYS = 64
LANES = 128
UNROLL = 128

half_span = 11

f32 = jnp.float32
bf16 = jnp.bfloat16
VMEM = pl.BlockSpec(memory_space=pltpu.VMEM)
ANY = pl.BlockSpec(memory_space=pl.ANY)
HBM = pl.BlockSpec(memory_space=pltpu.HBM)
PARAMS = pltpu.CompilerParams(vmem_limit_bytes=20 * 2**20)


def filter_table(day_count):
    outer = 13.0
    coeffs = []
    for offset_days in range(-half_span, half_span + 1):
        sq = float(offset_days * offset_days)
        top = (
            315.0
            * ((outer - 1) ** 2 - sq)
            * (outer**2 - sq)
            * ((outer + 1) ** 2 - sq)
            * (3 * outer**2 - 16 - 11 * sq)
        )
        bottom = (
            8
            * outer
            * (outer**2 - 1)
            * (4 * outer**2 - 1)
            * (4 * outer**2 - 9)
            * (4 * outer**2 - 25)
        )
        coeffs.append(top / bottom)
    matrix = np.zeros((day_count, day_count))
    for row_day in range(day_count):
        for offset_days in range(-half_span, half_span + 1):
            col_day = row_day + offset_days
            if 0 <= col_day < day_count:
                matrix[row_day, col_day] = coeffs[offset_days + half_span]
        matrix[row_day] = matrix[row_day] / matrix[row_day].sum()
    return matrix


def split2(x):
    hi = x.astype(bf16)
    return hi, (x - hi.astype(f32)).astype(bf16)


def dot_rows(rows, k, dims):
    return lax.dot_general(rows, k, (dims, ((), ())), preferred_element_type=f32)


def tiles(count):
    return [slice(at, at + LANES) for at in range(0, count, LANES)]


def turn(row):
    return jnp.transpose(jnp.broadcast_to(row, (LANES, LANES)))


def cols_of(u, k_ref):
    rows, cols = k_ref.shape
    totals = [0.0] * (cols // LANES)
    for block in tiles(rows):
        scale = turn(u[:, block])
        for j, tile in enumerate(tiles(cols)):
            totals[j] = totals[j] + jnp.sum((k_ref[block, tile] * scale).reshape(-1, 8, LANES), axis=0)
    return jnp.concatenate([jnp.sum(total, axis=0, keepdims=True) for total in totals], 1)


def rows_of(v, k_ref):
    rows, cols = k_ref.shape
    out = []
    for block in tiles(rows):
        total = 0.0
        for tile in tiles(cols):
            term = k_ref[block, tile]
            total = total + (term if v is None else term * v[:, tile])
        out.append(jnp.sum(jnp.transpose(total), axis=0, keepdims=True))
    return jnp.concatenate(out, 1)


def kernel_block(x, y, row_region, col_region, penalty):
    n, m = x.shape[0], y.shape[0]
    regions = penalty.shape[0]
    inv_root = 1.0 / math.sqrt(x.shape[1])
    inner = dot_rows(x, y, ((1,), (1,)))
    row_hot = (lax.broadcasted_iota(jnp.int32, (regions, n), 0) == row_region).astype(f32).astype(bf16)
    col_hot = (lax.broadcasted_iota(jnp.int32, (regions, m), 0) == col_region).astype(f32).astype(bf16)
    phi, plo = split2(penalty)
    qhi = jnp.dot(phi, col_hot, preferred_element_type=f32).astype(bf16)
    qlo = jnp.dot(plo, col_hot, preferred_element_type=f32).astype(bf16)
    pen = dot_rows(jnp.concatenate([row_hot, row_hot], 0), jnp.concatenate([qhi, qlo], 0), ((0,), (0,)))
    return jnp.exp(inner * inv_root - pen)


def run_copies(pairs, sems):
    copies = [pltpu.make_async_copy(src, dst, sems.at[k]) for k, (src, dst) in enumerate(pairs)]
    for copy in copies:
        copy.start()
    return copies


def first_body(
    x_hbm, y_hbm, rr_hbm, seg_hbm, mass_hbm, cr_hbm, cm_hbm, f_hbm, m_hbm, d_hbm, a_hbm,
    xpack_ref, ypack_ref, rpack_ref, f_ref, xb_ref, yb_ref, rr_ref, seg_ref, cr_ref, m_ref, d_ref, sems,
):
    me = lax.axis_index("cohort")
    n, m = xb_ref.shape[0], yb_ref.shape[0]
    p, q = n // LANES, m // LANES
    copies = run_copies(
        (
            (x_hbm, xb_ref),
            (rr_hbm, rr_ref),
            (seg_hbm, seg_ref),
            (mass_hbm, xpack_ref.at[pl.ds(n + 2 * p, p), :]),
            (y_hbm, yb_ref),
            (cr_hbm, cr_ref),
            (cm_hbm, ypack_ref.at[pl.ds(m + q, q), :]),
            (m_hbm, m_ref),
            (d_hbm, d_ref),
            (a_hbm, rpack_ref.at[pl.ds(2 * n, n), :]),
            (f_hbm.at[me], f_ref),
        ),
        sems,
    )
    for copy in copies:
        copy.wait()
    xpack_ref[0:n, :] = xb_ref[...].astype(f32)
    xpack_ref[n : n + p, :] = rr_ref[...].astype(f32)
    xpack_ref[n + p : n + 2 * p, :] = seg_ref[...].astype(f32)
    ypack_ref[0:m, :] = yb_ref[...].astype(f32)
    ypack_ref[m : m + q, :] = cr_ref[...].astype(f32)
    rpack_ref[0:n, :] = m_ref[...].astype(f32)
    rpack_ref[n : 2 * n, :] = d_ref[...].astype(f32)


def first_call(x, y, rr, seg, mass, cr, cm, table, records):
    n, m = x.shape[0], y.shape[0]
    p, q = n // LANES, m // LANES
    block = lambda v: v.reshape(-1, LANES)
    i32 = jnp.int32
    out = [(n + 3 * p, LANES), (m + 2 * q, LANES), (3 * n, LANES), table.shape[1:]]
    args = (x, y, block(rr), block(seg), block(mass), block(cr), block(cm), table, *records)
    return pl.pallas_call(
        first_body,
        in_specs=[HBM] * len(args),
        out_specs=[VMEM] * len(out),
        out_shape=[pltpu.VMEM(shape, f32) for shape in out],
        scratch_shapes=[
            pltpu.VMEM(x.shape, bf16),
            pltpu.VMEM(y.shape, bf16),
            pltpu.VMEM((p, LANES), i32),
            pltpu.VMEM((p, LANES), i32),
            pltpu.VMEM((q, LANES), i32),
            pltpu.VMEM((n, LANES), i32),
            pltpu.VMEM((n, LANES), i32),
            pltpu.SemaphoreType.DMA((len(args),)),
        ],
        compiler_params=PARAMS,
        name="first",
    )(*[pltpu.with_memory_space_constraint(arg, pltpu.HBM) for arg in args])


def flat(block):
    return jnp.concatenate([block[k : k + 1, :] for k in range(block.shape[0])], 1)


def gibbs_body(n, m, packs_x, packs_y, *refs):
    xpacks, ypacks = refs[:packs_x], refs[packs_x : packs_x + packs_y]
    pen_ref, k_ref, r_ref = refs[packs_x + packs_y :]
    p, q = n // LANES, m // LANES
    pen = pen_ref[...]
    ys = [(pack[0:m, :].astype(bf16), flat(pack[m : m + q, :]).astype(jnp.int32)) for pack in ypacks]
    for i, pack in enumerate(xpacks):
        x, rr = pack[0:n, :].astype(bf16), flat(pack[n : n + p, :]).astype(jnp.int32)
        for j, (y, cr) in enumerate(ys):
            k_ref[i * n : (i + 1) * n, j * m : (j + 1) * m] = kernel_block(x, y, rr, cr, pen)
    r_ref[...] = rows_of(None, k_ref)


def gibbs_call(n, m, xpacks, ypacks, penalty, after):
    rows, cols = len(xpacks) * n, len(ypacks) * m
    args = [*xpacks, *ypacks, penalty]
    return pl.pallas_call(
        lambda *refs: gibbs_body(n, m, len(xpacks), len(ypacks), *refs[: len(args)], *refs[-2:]),
        in_specs=[VMEM] * len(args) + [ANY] * len(after),
        out_specs=[VMEM] * 2,
        out_shape=[pltpu.VMEM((rows, cols), f32), pltpu.VMEM((1, rows), f32)],
        compiler_params=PARAMS,
        cost_estimate=pl.CostEstimate(
            flops=2 * rows * cols * LANES, transcendentals=rows * cols, bytes_accessed=rows * cols * 4
        ),
        name="gibbs",
    )(*args, *after)


def total_of(refs):
    total = refs[0][...]
    for ref in refs[1:]:
        total = total + ref[...]
    return total


def cols_body(n, parts, packs, *refs):
    p = n // LANES
    total = total_of(refs[:parts])
    pack_refs = refs[parts : parts + packs]
    k_ref, u_ref, c_ref = refs[parts + packs :]
    u = jnp.concatenate([flat(pack[n + 2 * p : n + 3 * p, :]) for pack in pack_refs], 1) / total
    u_ref[...] = u
    c_ref[...] = cols_of(u, k_ref)


def rows_body(m, parts, packs, *refs):
    q = m // LANES
    total = total_of(refs[:parts])
    pack_refs = refs[parts : parts + packs]
    k_ref, v_ref, r_ref = refs[parts + packs :]
    v = jnp.concatenate([flat(pack[m + q : m + 2 * q, :]) for pack in pack_refs], 1) / total
    v_ref[...] = v[:, :m]
    r_ref[...] = rows_of(v, k_ref)


def half_step(body, name, size, partials, packs, kernel, outs, after):
    args = [*partials, *packs, kernel]
    return pl.pallas_call(
        lambda *refs: body(size, len(partials), len(packs), *refs[: len(args)], *refs[-2:]),
        in_specs=[VMEM] * len(args) + [ANY] * len(after),
        out_specs=[VMEM] * 2,
        out_shape=outs,
        compiler_params=PARAMS,
        name=name,
    )(*args, *after)


def table_body(n, first, count, f_ref, pack_ref, hi_ref, lo_ref, token_ref):
    filt = f_ref[...]
    t_count = filt.shape[0]
    merch_rows = lax.broadcasted_iota(jnp.int32, (MERCH_DEV, LANES), 0).astype(f32).astype(bf16)
    merch_cols = lax.broadcasted_iota(jnp.int32, (LANES, MERCH_DEV), 1).astype(f32).astype(bf16)
    one, zero = jnp.ones((MERCH_DEV, LANES), bf16), jnp.zeros((MERCH_DEV, LANES), bf16)
    size = math.gcd(count, UNROLL)

    def group(step, carry):
        start = pl.multiple_of(step * size, size)
        merch = pack_ref[pl.ds(first + start, size), :]
        days = pack_ref[pl.ds(n + first + start, size), :].astype(jnp.int32)
        amounts = pack_ref[pl.ds(2 * n + first + start, size), :]
        turned = jnp.transpose(merch).astype(bf16)
        merch = merch.astype(bf16)
        tables = []
        for i in range(size):
            day = jnp.broadcast_to(days[i : i + 1, :], (t_count, LANES))
            coef = jnp.take_along_axis(filt, day, axis=1, mode="promise_in_bounds")
            both = jnp.concatenate(split2(coef * amounts[i : i + 1, :]), 0)
            if i % 2:
                hot = jnp.where(merch_cols == jnp.broadcast_to(turned[:, i : i + 1], merch_cols.shape), one, zero)
                both = dot_rows(both, hot, ((1,), (0,)))
            else:
                hot = jnp.where(merch_rows == merch[i : i + 1, :], one, zero)
                both = dot_rows(both, hot, ((1,), (1,)))
            tables.append(both[:t_count] + both[t_count:])
        hi, lo = split2(jnp.swapaxes(jnp.stack(tables, 0), 0, 1))
        hi_ref[:, pl.ds(start, size), :] = hi
        lo_ref[:, pl.ds(start, size), :] = lo
        return carry

    lax.fori_loop(0, count // size, group, 0)
    token_ref[...] = jnp.zeros_like(token_ref)


def table_call(filt, pack, n, first, count, after):
    t_count = filt.shape[0]
    hi, lo, token = pl.pallas_call(
        lambda *refs: table_body(n, first, count, *refs[:2], *refs[-3:]),
        in_specs=[VMEM] * 2 + [ANY] * len(after),
        out_specs=[VMEM] * 3,
        out_shape=[pltpu.VMEM((t_count, count, LANES), bf16)] * 2 + [pltpu.VMEM((8, LANES), f32)],
        compiler_params=PARAMS,
        cost_estimate=pl.CostEstimate(
            flops=4 * count * t_count * LANES * LANES, transcendentals=0, bytes_accessed=count * 60000
        ),
        name="tables",
    )(filt, pack, *after)
    return (hi, lo), token


def spread_body(n, t_first, t_count, parts, packs, count, u_ref, *refs):
    p = n // LANES
    w = u_ref[...] * total_of(refs[:parts])
    pack_refs = refs[parts : parts + packs]
    pair_refs = refs[parts + packs : parts + packs + 2 * count]
    o_ref, w_ref = refs[-2:]
    w_ref[...] = w[:, :n]
    seg = jnp.concatenate([flat(pack[n + p : n + 2 * p, :]).astype(jnp.int32) for pack in pack_refs], 1)
    hot = lax.broadcasted_iota(jnp.int32, (SEG, w.shape[1]), 0) == seg
    whi, wlo = split2(jnp.where(hot, w, 0.0))
    both = jnp.concatenate([whi, wlo], 0)

    def take(part, t):
        return jnp.concatenate(
            [jnp.concatenate([pair_refs[2 * k + part][t + q] for k in range(count)], 0) for q in range(2)], 1
        )

    for t in range(t_first, t_first + t_count, 2):
        two = jnp.dot(both, take(0, t), preferred_element_type=f32)
        out = two[:SEG] + two[SEG:] + jnp.dot(whi, take(1, t), preferred_element_type=f32)
        o_ref[t - t_first] = out[:, :LANES]
        o_ref[t - t_first + 1] = out[:, LANES:]


def spread_call(n, u, partials, packs, pairs, t_first, t_count, after):
    refs = [ref for pair in pairs for ref in pair]
    args = [u, *partials, *packs, *refs]
    return pl.pallas_call(
        lambda *refs: spread_body(
            n, t_first, t_count, len(partials), len(packs), len(pairs), *refs[: len(args)], *refs[-2:]
        ),
        in_specs=[VMEM] * len(args) + [ANY] * len(after),
        out_specs=[VMEM] * 2,
        out_shape=[pltpu.VMEM((t_count, SEG, LANES), f32), jax.ShapeDtypeStruct((1, n), f32)],
        compiler_params=PARAMS,
        name="spread",
    )(*args, *after)


def move(x, axis, size, pair, step, flip):
    blocks = size // pair

    def away(b):
        return b ^ step if blocks & (blocks - 1) == 0 else (b + step) % blocks

    return lax.ppermute(
        x, axis, [(b * pair + r, away(b) * pair + (r ^ flip)) for b in range(blocks) for r in range(pair)]
    )


def gate(x, *after):
    return lax.optimization_barrier((x, *after))[0]


def per_device(
    n_cohort,
    n_cell,
    cohort_features,
    cell_features,
    cohort_region,
    cell_region,
    penalty,
    cohort_mass,
    cell_mass,
    cohort_segment,
    spend_merchant,
    spend_day,
    spend_amount,
):
    n, m = cohort_features.shape[0], cell_features.shape[0]
    t_dev = DAYS // n_cohort
    n_y, n_z = n_cohort // 2, n_cell // 2
    table = np.zeros((n_cohort, 2 * t_dev, LANES), np.float32)
    henderson = filter_table(DAYS)
    for me in range(n_cohort):
        for k, dest in enumerate((me ^ 1, me)):
            table[me, k * t_dev : (k + 1) * t_dev, :DAYS] = henderson[dest * t_dev : (dest + 1) * t_dev]

    over_y = lambda x: [move(x, "cohort", n_cohort, 2, step, 0) for step in range(1, n_y)]
    core = lambda x: move(x, "cohort", n_cohort, 2, 0, 1)
    along_z = lambda x: [x] + [move(x, "cell", n_cell, 2, step, 0) for step in range(1, n_z)]

    xpack, ypack, rpack, filt = first_call(
        cohort_features, cell_features, cohort_region, cohort_segment, cohort_mass, cell_region, cell_mass,
        jnp.asarray(table), (spend_merchant, spend_day, spend_amount),
    )
    xpacks = [xpack] + over_y(xpack)
    ypacks = [ypack, move(ypack, "cell", n_cell, 2, 0, 1)]
    pairs = {}
    unit = n // 8

    def tables(source, first, units, *after):
        for size in (units & ~1, units & 1):
            if size:
                pack = rpack if source == 0 else rpacks[source - 1]
                pairs[source, first], token = table_call(filt, pack, n, first * unit, size * unit, after)
                after, first = [token], first + size
        return after

    def others(first, units, *after):
        for source in range(1, n_y):
            after = tables(source, first, units, *after)
        return after

    after = tables(0, 0, 6, filt)
    rpacks = over_y(gate(rpack, *xpacks, *ypacks, *after))
    kernel, partial = gibbs_call(n, m, xpacks, ypacks, penalty, after)
    row_sums = pltpu.VMEM((1, len(xpacks) * n), f32)
    col_sums = pltpu.VMEM((1, len(ypacks) * m), f32)
    fills = [
        [lambda *after: tables(0, 6, 1, *after), lambda *after: tables(0, 7, 1, *after)],
        [lambda *after: others(0, 4, *after), lambda *after: others(4, 1, *after)],
        [lambda *after: others(5, 3, *after)],
    ]
    lines = along_z(partial)
    after = fills[0][0](partial)
    for iteration in range(ITERS):
        cohort_scale, column = half_step(
            cols_body, "cols", n, lines, xpacks, kernel, [row_sums, col_sums], after
        )
        sibling = core(column)
        after = fills[iteration][1](column)
        cell_scale, partial = half_step(
            rows_body, "rows", m, [column, sibling], ypacks, kernel,
            [jax.ShapeDtypeStruct((1, m), f32), row_sums], after,
        )
        lines = along_z(partial)
        after = fills[iteration + 1][0](partial)
    ordered = [pairs[key] for key in sorted(pairs)]
    away, weights = spread_call(n, cohort_scale, lines, xpacks, ordered, 0, t_dev, after)
    mine, _ = spread_call(n, cohort_scale, lines, xpacks, ordered, t_dev, t_dev, after)
    out = mine + core(away)
    return (weights.reshape(-1), cell_scale.reshape(-1), out)


def solution(mesh):
    return jax.shard_map(
        functools.partial(per_device, mesh.shape["cohort"], mesh.shape["cell"]),
        mesh=mesh,
        in_specs=(
            P("cohort", None),
            P("cell", None),
            P("cohort"),
            P("cell"),
            P(),
            P("cohort"),
            P("cell"),
            P("cohort"),
            P("cohort", "cell"),
            P("cohort", "cell"),
            P("cohort", "cell"),
        ),
        out_specs=(P("cohort"), P("cell"), P("cohort", None, "cell")),
        check_vma=False,
    )
```

```python
import functools
import math

import jax
import jax.numpy as jnp
import numpy as np
from jax import lax
from jax.experimental import pallas as pl
from jax.experimental.pallas import tpu as pltpu
from jax.sharding import PartitionSpec as P

ITERS = 2
SEG = 32
MERCH_DEV = 128
DAYS = 64
LANES = 128
UNROLL = 128

half_span = 11

f32 = jnp.float32
bf16 = jnp.bfloat16
VMEM = pl.BlockSpec(memory_space=pltpu.VMEM)
ANY = pl.BlockSpec(memory_space=pl.ANY)
HBM = pl.BlockSpec(memory_space=pltpu.HBM)
PARAMS = pltpu.CompilerParams(vmem_limit_bytes=20 * 2**20)


def filter_table(day_count):
    outer = 13.0
    coeffs = []
    for offset_days in range(-half_span, half_span + 1):
        sq = float(offset_days * offset_days)
        top = (
            315.0
            * ((outer - 1) ** 2 - sq)
            * (outer**2 - sq)
            * ((outer + 1) ** 2 - sq)
            * (3 * outer**2 - 16 - 11 * sq)
        )
        bottom = (
            8
            * outer
            * (outer**2 - 1)
            * (4 * outer**2 - 1)
            * (4 * outer**2 - 9)
            * (4 * outer**2 - 25)
        )
        coeffs.append(top / bottom)
    matrix = np.zeros((day_count, day_count))
    for row_day in range(day_count):
        for offset_days in range(-half_span, half_span + 1):
            col_day = row_day + offset_days
            if 0 <= col_day < day_count:
                matrix[row_day, col_day] = coeffs[offset_days + half_span]
        matrix[row_day] = matrix[row_day] / matrix[row_day].sum()
    return matrix


def split2(x):
    hi = x.astype(bf16)
    return hi, (x - hi.astype(f32)).astype(bf16)


def dot_rows(rows, k, dims):
    return lax.dot_general(rows, k, (dims, ((), ())), preferred_element_type=f32)


def tiles(count):
    return [slice(at, at + LANES) for at in range(0, count, LANES)]


def turn(row):
    return jnp.transpose(jnp.broadcast_to(row, (LANES, LANES)))


def cols_of(u, k_ref):
    rows, cols = k_ref.shape
    totals = [0.0] * (cols // LANES)
    for block in tiles(rows):
        scale = turn(u[:, block])
        for j, tile in enumerate(tiles(cols)):
            totals[j] = totals[j] + jnp.sum((k_ref[block, tile] * scale).reshape(-1, 8, LANES), axis=0)
    return jnp.concatenate([jnp.sum(total, axis=0, keepdims=True) for total in totals], 1)


def rows_of(v, k_ref):
    rows, cols = k_ref.shape
    out = []
    for block in tiles(rows):
        total = 0.0
        for tile in tiles(cols):
            term = k_ref[block, tile]
            total = total + (term if v is None else term * v[:, tile])
        out.append(jnp.sum(jnp.transpose(total), axis=0, keepdims=True))
    return jnp.concatenate(out, 1)


def kernel_block(x, y, row_region, col_region, penalty):
    n, m = x.shape[0], y.shape[0]
    regions = penalty.shape[0]
    inv_root = 1.0 / math.sqrt(x.shape[1])
    inner = dot_rows(x, y, ((1,), (1,)))
    row_hot = (lax.broadcasted_iota(jnp.int32, (regions, n), 0) == row_region).astype(f32).astype(bf16)
    col_hot = (lax.broadcasted_iota(jnp.int32, (regions, m), 0) == col_region).astype(f32).astype(bf16)
    phi, plo = split2(penalty)
    qhi = jnp.dot(phi, col_hot, preferred_element_type=f32).astype(bf16)
    qlo = jnp.dot(plo, col_hot, preferred_element_type=f32).astype(bf16)
    pen = dot_rows(jnp.concatenate([row_hot, row_hot], 0), jnp.concatenate([qhi, qlo], 0), ((0,), (0,)))
    return jnp.exp(inner * inv_root - pen)


def run_copies(pairs, sems):
    copies = [pltpu.make_async_copy(src, dst, sems.at[k]) for k, (src, dst) in enumerate(pairs)]
    for copy in copies:
        copy.start()
    return copies


def first_body(
    x_hbm, y_hbm, rr_hbm, seg_hbm, mass_hbm, cr_hbm, cm_hbm, f_hbm, m_hbm, d_hbm, a_hbm,
    xpack_ref, ypack_ref, early_ref, late_ref, f_ref, xb_ref, yb_ref, rr_ref, seg_ref, cr_ref, m_ref, d_ref, sems,
):
    me = lax.axis_index("cohort")
    n, m = xb_ref.shape[0], yb_ref.shape[0]
    p, q = n // LANES, m // LANES
    e = early_ref.shape[0] // 3
    copies = run_copies(
        (
            (x_hbm, xb_ref),
            (rr_hbm, rr_ref),
            (seg_hbm, seg_ref),
            (mass_hbm, xpack_ref.at[pl.ds(n + 2 * p, p), :]),
            (y_hbm, yb_ref),
            (cr_hbm, cr_ref),
            (cm_hbm, ypack_ref.at[pl.ds(m + q, q), :]),
            (m_hbm, m_ref),
            (d_hbm, d_ref),
            (a_hbm.at[pl.ds(0, e), :], early_ref.at[pl.ds(2 * e, e), :]),
            (a_hbm.at[pl.ds(e, n - e), :], late_ref.at[pl.ds(2 * (n - e), n - e), :]),
            (f_hbm.at[me], f_ref),
        ),
        sems,
    )
    for copy in copies:
        copy.wait()
    xpack_ref[0:n, :] = xb_ref[...].astype(f32)
    xpack_ref[n : n + p, :] = rr_ref[...].astype(f32)
    xpack_ref[n + p : n + 2 * p, :] = seg_ref[...].astype(f32)
    ypack_ref[0:m, :] = yb_ref[...].astype(f32)
    ypack_ref[m : m + q, :] = cr_ref[...].astype(f32)
    for pack, rows in ((early_ref, slice(0, e)), (late_ref, slice(e, n))):
        size = rows.stop - rows.start
        pack[0:size, :] = m_ref[rows, :].astype(f32)
        pack[size : 2 * size, :] = d_ref[rows, :].astype(f32)


def first_call(x, y, rr, seg, mass, cr, cm, table, records, early):
    n, m = x.shape[0], y.shape[0]
    p, q = n // LANES, m // LANES
    block = lambda v: v.reshape(-1, LANES)
    i32 = jnp.int32
    out = [(n + 3 * p, LANES), (m + 2 * q, LANES), (3 * early, LANES), (3 * (n - early), LANES), table.shape[1:]]
    args = (x, y, block(rr), block(seg), block(mass), block(cr), block(cm), table, *records)
    return pl.pallas_call(
        first_body,
        in_specs=[HBM] * len(args),
        out_specs=[VMEM] * len(out),
        out_shape=[pltpu.VMEM(shape, f32) for shape in out],
        scratch_shapes=[
            pltpu.VMEM(x.shape, bf16),
            pltpu.VMEM(y.shape, bf16),
            pltpu.VMEM((p, LANES), i32),
            pltpu.VMEM((p, LANES), i32),
            pltpu.VMEM((q, LANES), i32),
            pltpu.VMEM((n, LANES), i32),
            pltpu.VMEM((n, LANES), i32),
            pltpu.SemaphoreType.DMA((len(args) + 1,)),
        ],
        compiler_params=PARAMS,
        name="first",
    )(*[pltpu.with_memory_space_constraint(arg, pltpu.HBM) for arg in args])


def flat(block):
    return jnp.concatenate([block[k : k + 1, :] for k in range(block.shape[0])], 1)


def gibbs_body(n, m, packs_x, packs_y, *refs):
    xpacks, ypacks = refs[:packs_x], refs[packs_x : packs_x + packs_y]
    pen_ref, k_ref, r_ref = refs[packs_x + packs_y :]
    p, q = n // LANES, m // LANES
    pen = pen_ref[...]
    ys = [(pack[0:m, :].astype(bf16), flat(pack[m : m + q, :]).astype(jnp.int32)) for pack in ypacks]
    for i, pack in enumerate(xpacks):
        x, rr = pack[0:n, :].astype(bf16), flat(pack[n : n + p, :]).astype(jnp.int32)
        for j, (y, cr) in enumerate(ys):
            k_ref[i * n : (i + 1) * n, j * m : (j + 1) * m] = kernel_block(x, y, rr, cr, pen)
    r_ref[...] = rows_of(None, k_ref)


def gibbs_call(n, m, xpacks, ypacks, penalty, after):
    rows, cols = len(xpacks) * n, len(ypacks) * m
    args = [*xpacks, *ypacks, penalty]
    return pl.pallas_call(
        lambda *refs: gibbs_body(n, m, len(xpacks), len(ypacks), *refs[: len(args)], *refs[-2:]),
        in_specs=[VMEM] * len(args) + [ANY] * len(after),
        out_specs=[VMEM] * 2,
        out_shape=[pltpu.VMEM((rows, cols), f32), pltpu.VMEM((1, rows), f32)],
        compiler_params=PARAMS,
        cost_estimate=pl.CostEstimate(
            flops=2 * rows * cols * LANES, transcendentals=rows * cols, bytes_accessed=rows * cols * 4
        ),
        name="gibbs",
    )(*args, *after)


def total_of(refs):
    total = refs[0][...]
    for ref in refs[1:]:
        total = total + ref[...]
    return total


def cols_body(n, parts, packs, *refs):
    p = n // LANES
    total = total_of(refs[:parts])
    pack_refs = refs[parts : parts + packs]
    k_ref, u_ref, c_ref = refs[parts + packs :]
    u = jnp.concatenate([flat(pack[n + 2 * p : n + 3 * p, :]) for pack in pack_refs], 1) / total
    u_ref[...] = u
    c_ref[...] = cols_of(u, k_ref)


def rows_body(m, parts, packs, *refs):
    q = m // LANES
    total = total_of(refs[:parts])
    pack_refs = refs[parts : parts + packs]
    k_ref, v_ref, r_ref = refs[parts + packs :]
    v = jnp.concatenate([flat(pack[m + q : m + 2 * q, :]) for pack in pack_refs], 1) / total
    v_ref[...] = v[:, :m]
    r_ref[...] = rows_of(v, k_ref)


def half_step(body, name, size, partials, packs, kernel, outs, after):
    args = [*partials, *packs, kernel]
    return pl.pallas_call(
        lambda *refs: body(size, len(partials), len(packs), *refs[: len(args)], *refs[-2:]),
        in_specs=[VMEM] * len(args) + [ANY] * len(after),
        out_specs=[VMEM] * 2,
        out_shape=outs,
        compiler_params=PARAMS,
        name=name,
    )(*args, *after)


def table_body(n, first, count, f_ref, pack_ref, hi_ref, lo_ref, token_ref):
    filt = f_ref[...]
    t_count = filt.shape[0]
    merch_rows = lax.broadcasted_iota(jnp.int32, (MERCH_DEV, LANES), 0).astype(f32).astype(bf16)
    merch_cols = lax.broadcasted_iota(jnp.int32, (LANES, MERCH_DEV), 1).astype(f32).astype(bf16)
    one, zero = jnp.ones((MERCH_DEV, LANES), bf16), jnp.zeros((MERCH_DEV, LANES), bf16)
    size = math.gcd(count, UNROLL)

    def group(step, carry):
        start = pl.multiple_of(step * size, size)
        merch = pack_ref[pl.ds(first + start, size), :]
        days = pack_ref[pl.ds(n + first + start, size), :].astype(jnp.int32)
        amounts = pack_ref[pl.ds(2 * n + first + start, size), :]
        turned = jnp.transpose(merch).astype(bf16)
        merch = merch.astype(bf16)
        tables = []
        for i in range(size):
            day = jnp.broadcast_to(days[i : i + 1, :], (t_count, LANES))
            coef = jnp.take_along_axis(filt, day, axis=1, mode="promise_in_bounds")
            both = jnp.concatenate(split2(coef * amounts[i : i + 1, :]), 0)
            if i % 2:
                hot = jnp.where(merch_cols == jnp.broadcast_to(turned[:, i : i + 1], merch_cols.shape), one, zero)
                both = dot_rows(both, hot, ((1,), (0,)))
            else:
                hot = jnp.where(merch_rows == merch[i : i + 1, :], one, zero)
                both = dot_rows(both, hot, ((1,), (1,)))
            tables.append(both[:t_count] + both[t_count:])
        hi, lo = split2(jnp.swapaxes(jnp.stack(tables, 0), 0, 1))
        hi_ref[:, pl.ds(start, size), :] = hi
        lo_ref[:, pl.ds(start, size), :] = lo
        return carry

    lax.fori_loop(0, count // size, group, 0)
    token_ref[...] = jnp.zeros_like(token_ref)


def table_call(filt, pack, n, first, count, after):
    t_count = filt.shape[0]
    hi, lo, token = pl.pallas_call(
        lambda *refs: table_body(n, first, count, *refs[:2], *refs[-3:]),
        in_specs=[VMEM] * 2 + [ANY] * len(after),
        out_specs=[VMEM] * 3,
        out_shape=[pltpu.VMEM((t_count, count, LANES), bf16)] * 2 + [pltpu.VMEM((8, LANES), f32)],
        compiler_params=PARAMS,
        cost_estimate=pl.CostEstimate(
            flops=4 * count * t_count * LANES * LANES, transcendentals=0, bytes_accessed=count * 60000
        ),
        name="tables",
    )(filt, pack, *after)
    return (hi, lo), token


def spread_body(n, t_first, t_count, parts, packs, count, u_ref, *refs):
    p = n // LANES
    w = u_ref[...] * total_of(refs[:parts])
    pack_refs = refs[parts : parts + packs]
    pair_refs = refs[parts + packs : parts + packs + 2 * count]
    o_ref, w_ref = refs[-2:]
    w_ref[...] = w[:, :n]
    seg = jnp.concatenate([flat(pack[n + p : n + 2 * p, :]).astype(jnp.int32) for pack in pack_refs], 1)
    hot = lax.broadcasted_iota(jnp.int32, (SEG, w.shape[1]), 0) == seg
    whi, wlo = split2(jnp.where(hot, w, 0.0))
    both = jnp.concatenate([whi, wlo], 0)

    def take(part, t):
        return jnp.concatenate(
            [jnp.concatenate([pair_refs[2 * k + part][t + q] for k in range(count)], 0) for q in range(2)], 1
        )

    for t in range(t_first, t_first + t_count, 2):
        two = jnp.dot(both, take(0, t), preferred_element_type=f32)
        out = two[:SEG] + two[SEG:] + jnp.dot(whi, take(1, t), preferred_element_type=f32)
        o_ref[t - t_first] = out[:, :LANES]
        o_ref[t - t_first + 1] = out[:, LANES:]


def spread_call(n, u, partials, packs, pairs, t_first, t_count, after):
    refs = [ref for pair in pairs for ref in pair]
    args = [u, *partials, *packs, *refs]
    return pl.pallas_call(
        lambda *refs: spread_body(
            n, t_first, t_count, len(partials), len(packs), len(pairs), *refs[: len(args)], *refs[-2:]
        ),
        in_specs=[VMEM] * len(args) + [ANY] * len(after),
        out_specs=[VMEM] * 2,
        out_shape=[pltpu.VMEM((t_count, SEG, LANES), f32), jax.ShapeDtypeStruct((1, n), f32)],
        compiler_params=PARAMS,
        name="spread",
    )(*args, *after)


def add_body(a_ref, b_ref, o_ref):
    o_ref[...] = a_ref[...] + b_ref[...]


def add_call(a, b):
    return pl.pallas_call(
        add_body,
        in_specs=[VMEM] * 2,
        out_specs=VMEM,
        out_shape=jax.ShapeDtypeStruct(a.shape, f32),
        compiler_params=PARAMS,
        name="last",
    )(a, b)


def move(x, axis, size, pair, step, flip):
    blocks = size // pair

    def away(b):
        return b ^ step if blocks & (blocks - 1) == 0 else (b + step) % blocks

    return lax.ppermute(
        x, axis, [(b * pair + r, away(b) * pair + (r ^ flip)) for b in range(blocks) for r in range(pair)]
    )


def gate(x, *after):
    return lax.optimization_barrier((x, *after))[0]


def per_device(
    n_cohort,
    n_cell,
    cohort_features,
    cell_features,
    cohort_region,
    cell_region,
    penalty,
    cohort_mass,
    cell_mass,
    cohort_segment,
    spend_merchant,
    spend_day,
    spend_amount,
):
    n, m = cohort_features.shape[0], cell_features.shape[0]
    t_dev = DAYS // n_cohort
    n_y, n_z = n_cohort // 2, n_cell // 2
    table = np.zeros((n_cohort, 2 * t_dev, LANES), np.float32)
    henderson = filter_table(DAYS)
    for me in range(n_cohort):
        for k, dest in enumerate((me ^ 1, me)):
            table[me, k * t_dev : (k + 1) * t_dev, :DAYS] = henderson[dest * t_dev : (dest + 1) * t_dev]

    over_y = lambda x: [move(x, "cohort", n_cohort, 2, step, 0) for step in range(1, n_y)]
    core = lambda x: move(x, "cohort", n_cohort, 2, 0, 1)
    along_z = lambda x: [x] + [move(x, "cell", n_cell, 2, step, 0) for step in range(1, n_z)]

    unit = n // 8
    ahead = 4
    xpack, ypack, *own, filt = first_call(
        cohort_features, cell_features, cohort_region, cohort_segment, cohort_mass, cell_region, cell_mass,
        jnp.asarray(table), (spend_merchant, spend_day, spend_amount), ahead * unit,
    )
    xpacks = [xpack] + over_y(xpack)
    ypacks = [ypack, move(ypack, "cell", n_cell, 2, 0, 1)]
    pairs = {}

    def tables(source, first, units, *after):
        for size in (units & ~1, units & 1):
            if size:
                late = int(first >= ahead)
                pack = own[late] if source == 0 else rpacks[late][source - 1]
                pairs[source, first], token = table_call(
                    filt, pack, pack.shape[0] // 3, (first - late * ahead) * unit, size * unit, after
                )
                after, first = [token], first + size
        return after

    def others(first, units, *after):
        for source in range(1, n_y):
            after = tables(source, first, units, *after)
        return after

    after = tables(0, ahead, 2, *tables(0, 0, ahead, filt))
    rpacks = [over_y(gate(own[0], *xpacks, *ypacks, *after))]
    kernel, partial = gibbs_call(n, m, xpacks, ypacks, penalty, after)
    row_sums = pltpu.VMEM((1, len(xpacks) * n), f32)
    col_sums = pltpu.VMEM((1, len(ypacks) * m), f32)
    lines = along_z(partial)
    after = tables(0, ahead + 2, 2, partial)
    fills = [[(0, 1), (1, 3)], [(4, 1), (5, 3)]]
    for iteration in range(ITERS):
        cohort_scale, column = half_step(
            cols_body, "cols", n, lines, xpacks, kernel, [row_sums, col_sums], after
        )
        sibling = core(column)
        if iteration == 0:
            rpacks.append(over_y(gate(own[1], column)))
        after = others(*fills[iteration][0], column)
        cell_scale, partial = half_step(
            rows_body, "rows", m, [column, sibling], ypacks, kernel,
            [jax.ShapeDtypeStruct((1, m), f32), row_sums], after,
        )
        lines = along_z(partial)
        after = others(*fills[iteration][1], partial)
    ordered = [pairs[key] for key in sorted(pairs)]
    away, weights = spread_call(n, cohort_scale, lines, xpacks, ordered, 0, t_dev, after)
    mine, _ = spread_call(n, cohort_scale, lines, xpacks, ordered, t_dev, t_dev, after)
    out = add_call(mine, core(away))
    return (weights.reshape(-1), cell_scale.reshape(-1), out)


def solution(mesh):
    return jax.shard_map(
        functools.partial(per_device, mesh.shape["cohort"], mesh.shape["cell"]),
        mesh=mesh,
        in_specs=(
            P("cohort", None),
            P("cell", None),
            P("cohort"),
            P("cell"),
            P(),
            P("cohort"),
            P("cell"),
            P("cohort"),
            P("cohort", "cell"),
            P("cohort", "cell"),
            P("cohort", "cell"),
        ),
        out_specs=(P("cohort"), P("cell"), P("cohort", None, "cell")),
        check_vma=False,
    )
```

```python
import functools
import math

import jax
import jax.numpy as jnp
import numpy as np
from jax import lax
from jax.experimental import pallas as pl
from jax.experimental.pallas import tpu as pltpu
from jax.sharding import PartitionSpec as P

ITERS = 2
SEG = 32
MERCH_DEV = 128
DAYS = 64
LANES = 128
UNROLL = 128

half_span = 11

f32 = jnp.float32
bf16 = jnp.bfloat16
VMEM = pl.BlockSpec(memory_space=pltpu.VMEM)
ANY = pl.BlockSpec(memory_space=pl.ANY)
HBM = pl.BlockSpec(memory_space=pltpu.HBM)
PARAMS = pltpu.CompilerParams(vmem_limit_bytes=20 * 2**20)


def filter_table(day_count):
    outer = 13.0
    coeffs = []
    for offset_days in range(-half_span, half_span + 1):
        sq = float(offset_days * offset_days)
        top = (
            315.0
            * ((outer - 1) ** 2 - sq)
            * (outer**2 - sq)
            * ((outer + 1) ** 2 - sq)
            * (3 * outer**2 - 16 - 11 * sq)
        )
        bottom = (
            8
            * outer
            * (outer**2 - 1)
            * (4 * outer**2 - 1)
            * (4 * outer**2 - 9)
            * (4 * outer**2 - 25)
        )
        coeffs.append(top / bottom)
    matrix = np.zeros((day_count, day_count))
    for row_day in range(day_count):
        for offset_days in range(-half_span, half_span + 1):
            col_day = row_day + offset_days
            if 0 <= col_day < day_count:
                matrix[row_day, col_day] = coeffs[offset_days + half_span]
        matrix[row_day] = matrix[row_day] / matrix[row_day].sum()
    return matrix


def split2(x):
    hi = x.astype(bf16)
    return hi, (x - hi.astype(f32)).astype(bf16)


def dot_rows(rows, k, dims):
    return lax.dot_general(rows, k, (dims, ((), ())), preferred_element_type=f32)


def tiles(count):
    return [slice(at, at + LANES) for at in range(0, count, LANES)]


def turn(row):
    return jnp.transpose(jnp.broadcast_to(row, (LANES, LANES)))


def cols_of(u, k_ref):
    rows, cols = k_ref.shape
    totals = [0.0] * (cols // LANES)
    for block in tiles(rows):
        scale = turn(u[:, block])
        for j, tile in enumerate(tiles(cols)):
            totals[j] = totals[j] + jnp.sum((k_ref[block, tile] * scale).reshape(-1, 8, LANES), axis=0)
    return jnp.concatenate([jnp.sum(total, axis=0, keepdims=True) for total in totals], 1)


def rows_of(v, k_ref):
    rows, cols = k_ref.shape
    out = []
    for block in tiles(rows):
        total = 0.0
        for tile in tiles(cols):
            term = k_ref[block, tile]
            total = total + (term if v is None else term * v[:, tile])
        out.append(jnp.sum(jnp.transpose(total), axis=0, keepdims=True))
    return jnp.concatenate(out, 1)


def kernel_block(x, y, row_region, col_region, penalty):
    n, m = x.shape[0], y.shape[0]
    regions = penalty.shape[0]
    inv_root = 1.0 / math.sqrt(x.shape[1])
    inner = dot_rows(x, y, ((1,), (1,)))
    row_hot = (lax.broadcasted_iota(jnp.int32, (regions, n), 0) == row_region).astype(f32).astype(bf16)
    col_hot = (lax.broadcasted_iota(jnp.int32, (regions, m), 0) == col_region).astype(f32).astype(bf16)
    phi, plo = split2(penalty)
    qhi = jnp.dot(phi, col_hot, preferred_element_type=f32).astype(bf16)
    qlo = jnp.dot(plo, col_hot, preferred_element_type=f32).astype(bf16)
    pen = dot_rows(jnp.concatenate([row_hot, row_hot], 0), jnp.concatenate([qhi, qlo], 0), ((0,), (0,)))
    return jnp.exp(inner * inv_root - pen)


def run_copies(pairs, sems):
    copies = [pltpu.make_async_copy(src, dst, sems.at[k]) for k, (src, dst) in enumerate(pairs)]
    for copy in copies:
        copy.start()
    return copies


def packs_body(
    x_hbm, y_hbm, rr_hbm, seg_hbm, mass_hbm, cr_hbm, cm_hbm,
    xpack_ref, ypack_ref, xb_ref, yb_ref, rr_ref, seg_ref, cr_ref, sems,
):
    n, m = xb_ref.shape[0], yb_ref.shape[0]
    p, q = n // LANES, m // LANES
    copies = run_copies(
        (
            (x_hbm, xb_ref),
            (y_hbm, yb_ref),
            (rr_hbm, rr_ref),
            (seg_hbm, seg_ref),
            (mass_hbm, xpack_ref.at[pl.ds(n + 2 * p, p), :]),
            (cr_hbm, cr_ref),
            (cm_hbm, ypack_ref.at[pl.ds(m + q, q), :]),
        ),
        sems,
    )
    for copy in copies:
        copy.wait()
    xpack_ref[0:n, :] = xb_ref[...].astype(f32)
    xpack_ref[n : n + p, :] = rr_ref[...].astype(f32)
    xpack_ref[n + p : n + 2 * p, :] = seg_ref[...].astype(f32)
    ypack_ref[0:m, :] = yb_ref[...].astype(f32)
    ypack_ref[m : m + q, :] = cr_ref[...].astype(f32)


def hbm_call(body, name, args, out, scratch):
    return pl.pallas_call(
        body,
        in_specs=[HBM] * len(args),
        out_specs=[VMEM] * len(out),
        out_shape=[pltpu.VMEM(shape, f32) for shape in out],
        scratch_shapes=[*scratch, pltpu.SemaphoreType.DMA((len(args) + 1,))],
        compiler_params=PARAMS,
        name=name,
    )(*[pltpu.with_memory_space_constraint(arg, pltpu.HBM) for arg in args])


def packs_call(x, y, rr, seg, mass, cr, cm):
    n, m = x.shape[0], y.shape[0]
    p, q = n // LANES, m // LANES
    block = lambda v: v.reshape(-1, LANES)
    i32 = jnp.int32
    return hbm_call(
        packs_body,
        "packs",
        (x, y, block(rr), block(seg), block(mass), block(cr), block(cm)),
        [(n + 3 * p, LANES), (m + 2 * q, LANES)],
        [
            pltpu.VMEM(x.shape, bf16),
            pltpu.VMEM(y.shape, bf16),
            pltpu.VMEM((p, LANES), i32),
            pltpu.VMEM((p, LANES), i32),
            pltpu.VMEM((q, LANES), i32),
        ],
    )


def records_body(f_hbm, m_hbm, d_hbm, a_hbm, early_ref, late_ref, f_ref, m_ref, d_ref, sems):
    me = lax.axis_index("cohort")
    e, n = early_ref.shape[0] // 3, m_ref.shape[0]
    copies = run_copies(
        (
            (m_hbm, m_ref),
            (d_hbm, d_ref),
            (a_hbm.at[pl.ds(0, e), :], early_ref.at[pl.ds(2 * e, e), :]),
            (a_hbm.at[pl.ds(e, n - e), :], late_ref.at[pl.ds(2 * (n - e), n - e), :]),
            (f_hbm.at[me], f_ref),
        ),
        sems,
    )
    for copy in copies:
        copy.wait()
    for pack, rows in ((early_ref, slice(0, e)), (late_ref, slice(e, n))):
        size = rows.stop - rows.start
        pack[0:size, :] = m_ref[rows, :].astype(f32)
        pack[size : 2 * size, :] = d_ref[rows, :].astype(f32)


def records_call(table, merchants, days, amounts, early):
    n = merchants.shape[0]
    return hbm_call(
        records_body,
        "records",
        (table, merchants, days, amounts),
        [(3 * early, LANES), (3 * (n - early), LANES), table.shape[1:]],
        [pltpu.VMEM((n, LANES), jnp.int32), pltpu.VMEM((n, LANES), jnp.int32)],
    )


def flat(block):
    return jnp.concatenate([block[k : k + 1, :] for k in range(block.shape[0])], 1)


def gibbs_body(n, m, packs_x, packs_y, *refs):
    xpacks, ypacks = refs[:packs_x], refs[packs_x : packs_x + packs_y]
    pen_ref, k_ref, r_ref = refs[packs_x + packs_y :]
    p, q = n // LANES, m // LANES
    pen = pen_ref[...]
    ys = [(pack[0:m, :].astype(bf16), flat(pack[m : m + q, :]).astype(jnp.int32)) for pack in ypacks]
    for i, pack in enumerate(xpacks):
        x, rr = pack[0:n, :].astype(bf16), flat(pack[n : n + p, :]).astype(jnp.int32)
        for j, (y, cr) in enumerate(ys):
            k_ref[i * n : (i + 1) * n, j * m : (j + 1) * m] = kernel_block(x, y, rr, cr, pen)
    r_ref[...] = rows_of(None, k_ref)


def gibbs_call(n, m, xpacks, ypacks, penalty, after):
    rows, cols = len(xpacks) * n, len(ypacks) * m
    args = [*xpacks, *ypacks, penalty]
    return pl.pallas_call(
        lambda *refs: gibbs_body(n, m, len(xpacks), len(ypacks), *refs[: len(args)], *refs[-2:]),
        in_specs=[VMEM] * len(args) + [ANY] * len(after),
        out_specs=[VMEM] * 2,
        out_shape=[pltpu.VMEM((rows, cols), f32), pltpu.VMEM((1, rows), f32)],
        compiler_params=PARAMS,
        cost_estimate=pl.CostEstimate(
            flops=2 * rows * cols * LANES, transcendentals=rows * cols, bytes_accessed=rows * cols * 4
        ),
        name="gibbs",
    )(*args, *after)


def total_of(refs):
    total = refs[0][...]
    for ref in refs[1:]:
        total = total + ref[...]
    return total


def cols_body(n, parts, packs, *refs):
    p = n // LANES
    total = total_of(refs[:parts])
    pack_refs = refs[parts : parts + packs]
    k_ref, u_ref, c_ref = refs[parts + packs :]
    u = jnp.concatenate([flat(pack[n + 2 * p : n + 3 * p, :]) for pack in pack_refs], 1) / total
    u_ref[...] = u
    c_ref[...] = cols_of(u, k_ref)


def rows_body(m, parts, packs, *refs):
    q = m // LANES
    total = total_of(refs[:parts])
    pack_refs = refs[parts : parts + packs]
    k_ref, v_ref, r_ref = refs[parts + packs :]
    v = jnp.concatenate([flat(pack[m + q : m + 2 * q, :]) for pack in pack_refs], 1) / total
    v_ref[...] = v[:, :m]
    r_ref[...] = rows_of(v, k_ref)


def half_step(body, name, size, partials, packs, kernel, outs, after):
    args = [*partials, *packs, kernel]
    return pl.pallas_call(
        lambda *refs: body(size, len(partials), len(packs), *refs[: len(args)], *refs[-2:]),
        in_specs=[VMEM] * len(args) + [ANY] * len(after),
        out_specs=[VMEM] * 2,
        out_shape=outs,
        compiler_params=PARAMS,
        name=name,
    )(*args, *after)


def table_body(n, first, count, f_ref, pack_ref, hi_ref, lo_ref, token_ref):
    filt = f_ref[...]
    t_count = filt.shape[0]
    merch_rows = lax.broadcasted_iota(jnp.int32, (MERCH_DEV, LANES), 0).astype(f32).astype(bf16)
    merch_cols = lax.broadcasted_iota(jnp.int32, (LANES, MERCH_DEV), 1).astype(f32).astype(bf16)
    one, zero = jnp.ones((MERCH_DEV, LANES), bf16), jnp.zeros((MERCH_DEV, LANES), bf16)
    size = math.gcd(count, UNROLL)

    def group(step, carry):
        start = pl.multiple_of(step * size, size)
        merch = pack_ref[pl.ds(first + start, size), :]
        days = pack_ref[pl.ds(n + first + start, size), :].astype(jnp.int32)
        amounts = pack_ref[pl.ds(2 * n + first + start, size), :]
        turned = jnp.transpose(merch).astype(bf16)
        merch = merch.astype(bf16)
        tables = []
        for i in range(size):
            day = jnp.broadcast_to(days[i : i + 1, :], (t_count, LANES))
            coef = jnp.take_along_axis(filt, day, axis=1, mode="promise_in_bounds")
            both = jnp.concatenate(split2(coef * amounts[i : i + 1, :]), 0)
            if i % 2:
                hot = jnp.where(merch_cols == jnp.broadcast_to(turned[:, i : i + 1], merch_cols.shape), one, zero)
                both = dot_rows(both, hot, ((1,), (0,)))
            else:
                hot = jnp.where(merch_rows == merch[i : i + 1, :], one, zero)
                both = dot_rows(both, hot, ((1,), (1,)))
            tables.append(both[:t_count] + both[t_count:])
        hi, lo = split2(jnp.swapaxes(jnp.stack(tables, 0), 0, 1))
        hi_ref[:, pl.ds(start, size), :] = hi
        lo_ref[:, pl.ds(start, size), :] = lo
        return carry

    lax.fori_loop(0, count // size, group, 0)
    token_ref[...] = jnp.zeros_like(token_ref)


def table_call(filt, pack, n, first, count, after):
    t_count = filt.shape[0]
    hi, lo, token = pl.pallas_call(
        lambda *refs: table_body(n, first, count, *refs[:2], *refs[-3:]),
        in_specs=[VMEM] * 2 + [ANY] * len(after),
        out_specs=[VMEM] * 3,
        out_shape=[pltpu.VMEM((t_count, count, LANES), bf16)] * 2 + [pltpu.VMEM((8, LANES), f32)],
        compiler_params=PARAMS,
        cost_estimate=pl.CostEstimate(
            flops=4 * count * t_count * LANES * LANES, transcendentals=0, bytes_accessed=count * 60000
        ),
        name="tables",
    )(filt, pack, *after)
    return (hi, lo), token


def spread_body(n, t_first, t_count, parts, packs, count, u_ref, *refs):
    p = n // LANES
    w = u_ref[...] * total_of(refs[:parts])
    pack_refs = refs[parts : parts + packs]
    pair_refs = refs[parts + packs : parts + packs + 2 * count]
    o_ref, w_ref = refs[-2:]
    w_ref[...] = w[:, :n]
    seg = jnp.concatenate([flat(pack[n + p : n + 2 * p, :]).astype(jnp.int32) for pack in pack_refs], 1)
    hot = lax.broadcasted_iota(jnp.int32, (SEG, w.shape[1]), 0) == seg
    whi, wlo = split2(jnp.where(hot, w, 0.0))
    both = jnp.concatenate([whi, wlo], 0)

    def take(part, t):
        return jnp.concatenate(
            [jnp.concatenate([pair_refs[2 * k + part][t + q] for k in range(count)], 0) for q in range(2)], 1
        )

    for t in range(t_first, t_first + t_count, 2):
        two = jnp.dot(both, take(0, t), preferred_element_type=f32)
        out = two[:SEG] + two[SEG:] + jnp.dot(whi, take(1, t), preferred_element_type=f32)
        o_ref[t - t_first] = out[:, :LANES]
        o_ref[t - t_first + 1] = out[:, LANES:]


def spread_call(n, u, partials, packs, pairs, t_first, t_count, after):
    refs = [ref for pair in pairs for ref in pair]
    args = [u, *partials, *packs, *refs]
    return pl.pallas_call(
        lambda *refs: spread_body(
            n, t_first, t_count, len(partials), len(packs), len(pairs), *refs[: len(args)], *refs[-2:]
        ),
        in_specs=[VMEM] * len(args) + [ANY] * len(after),
        out_specs=[VMEM] * 2,
        out_shape=[pltpu.VMEM((t_count, SEG, LANES), f32), pltpu.VMEM((1, n), f32)],
        compiler_params=PARAMS,
        name="spread",
    )(*args, *after)


def last_body(a_ref, b_ref, w_ref, v_ref, o_ref, w_out, v_out):
    o_ref[...] = a_ref[...] + b_ref[...]
    w_out[...] = w_ref[...]
    v_out[...] = v_ref[...]


def last_call(a, b, w, v):
    return pl.pallas_call(
        last_body,
        in_specs=[VMEM] * 4,
        out_specs=[VMEM] * 3,
        out_shape=[jax.ShapeDtypeStruct(x.shape, f32) for x in (a, w, v)],
        compiler_params=PARAMS,
        name="last",
    )(a, b, w, v)


def move(x, axis, size, pair, step, flip):
    blocks = size // pair

    def away(b):
        return b ^ step if blocks & (blocks - 1) == 0 else (b + step) % blocks

    return lax.ppermute(
        x, axis, [(b * pair + r, away(b) * pair + (r ^ flip)) for b in range(blocks) for r in range(pair)]
    )


def gate(x, *after):
    return lax.optimization_barrier((x, *after))[0]


def per_device(
    n_cohort,
    n_cell,
    cohort_features,
    cell_features,
    cohort_region,
    cell_region,
    penalty,
    cohort_mass,
    cell_mass,
    cohort_segment,
    spend_merchant,
    spend_day,
    spend_amount,
):
    n, m = cohort_features.shape[0], cell_features.shape[0]
    t_dev = DAYS // n_cohort
    n_y, n_z = n_cohort // 2, n_cell // 2
    table = np.zeros((n_cohort, 2 * t_dev, LANES), np.float32)
    henderson = filter_table(DAYS)
    for me in range(n_cohort):
        for k, dest in enumerate((me ^ 1, me)):
            table[me, k * t_dev : (k + 1) * t_dev, :DAYS] = henderson[dest * t_dev : (dest + 1) * t_dev]

    over_y = lambda x: [move(x, "cohort", n_cohort, 2, step, 0) for step in range(1, n_y)]
    core = lambda x: move(x, "cohort", n_cohort, 2, 0, 1)
    along_z = lambda x: [x] + [move(x, "cell", n_cell, 2, step, 0) for step in range(1, n_z)]

    unit = n // 8
    ahead = 4
    xpack, ypack = packs_call(
        cohort_features, cell_features, cohort_region, cohort_segment, cohort_mass, cell_region, cell_mass
    )
    *own, filt = records_call(jnp.asarray(table), spend_merchant, spend_day, spend_amount, ahead * unit)
    xpacks = [xpack] + over_y(xpack)
    ypacks = [ypack, move(ypack, "cell", n_cell, 2, 0, 1)]
    pairs = {}

    def tables(source, first, units, *after):
        for size in (units & ~1, units & 1):
            if size:
                late = int(first >= ahead)
                pack = own[late] if source == 0 else rpacks[late][source - 1]
                pairs[source, first], token = table_call(
                    filt, pack, pack.shape[0] // 3, (first - late * ahead) * unit, size * unit, after
                )
                after, first = [token], first + size
        return after

    def others(first, units, *after):
        for source in range(1, n_y):
            after = tables(source, first, units, *after)
        return after

    after = tables(0, ahead, 2, *tables(0, 0, ahead, filt))
    rpacks = [over_y(gate(own[0], *xpacks, *ypacks, *after))]
    kernel, partial = gibbs_call(n, m, xpacks, ypacks, penalty, after)
    row_sums = pltpu.VMEM((1, len(xpacks) * n), f32)
    col_sums = pltpu.VMEM((1, len(ypacks) * m), f32)
    lines = along_z(partial)
    after = tables(0, ahead + 2, 2, partial)
    fills = [[(0, 1), (1, 3)], [(4, 1), (5, 3)]]
    for iteration in range(ITERS):
        cohort_scale, column = half_step(
            cols_body, "cols", n, lines, xpacks, kernel, [row_sums, col_sums], after
        )
        sibling = core(column)
        if iteration == 0:
            rpacks.append(over_y(gate(own[1], column)))
        after = others(*fills[iteration][0], column)
        cell_scale, partial = half_step(
            rows_body, "rows", m, [column, sibling], ypacks, kernel,
            [pltpu.VMEM((1, m), f32), row_sums], after,
        )
        lines = along_z(partial)
        after = others(*fills[iteration][1], partial)
    ordered = [pairs[key] for key in sorted(pairs)]
    away, weights = spread_call(n, cohort_scale, lines, xpacks, ordered, 0, t_dev, after)
    mine, _ = spread_call(n, cohort_scale, lines, xpacks, ordered, t_dev, t_dev, after)
    out, weights, cell_scale = last_call(mine, core(away), weights, cell_scale)
    return (weights.reshape(-1), cell_scale.reshape(-1), out)


def solution(mesh):
    return jax.shard_map(
        functools.partial(per_device, mesh.shape["cohort"], mesh.shape["cell"]),
        mesh=mesh,
        in_specs=(
            P("cohort", None),
            P("cell", None),
            P("cohort"),
            P("cell"),
            P(),
            P("cohort"),
            P("cell"),
            P("cohort"),
            P("cohort", "cell"),
            P("cohort", "cell"),
            P("cohort", "cell"),
        ),
        out_specs=(P("cohort"), P("cell"), P("cohort", None, "cell")),
        check_vma=False,
    )
```

```python
import functools
import math

import jax
import jax.numpy as jnp
import numpy as np
from jax import lax
from jax.experimental import pallas as pl
from jax.experimental.pallas import tpu as pltpu
from jax.sharding import PartitionSpec as P

ITERS = 2
SEG = 32
MERCH_DEV = 128
DAYS = 64
LANES = 128
UNROLL = 128

half_span = 11

f32 = jnp.float32
bf16 = jnp.bfloat16
VMEM = pl.BlockSpec(memory_space=pltpu.VMEM)
ANY = pl.BlockSpec(memory_space=pl.ANY)
HBM = pl.BlockSpec(memory_space=pltpu.HBM)
PARAMS = pltpu.CompilerParams(vmem_limit_bytes=20 * 2**20)


def filter_table(day_count):
    outer = 13.0
    coeffs = []
    for offset_days in range(-half_span, half_span + 1):
        sq = float(offset_days * offset_days)
        top = (
            315.0
            * ((outer - 1) ** 2 - sq)
            * (outer**2 - sq)
            * ((outer + 1) ** 2 - sq)
            * (3 * outer**2 - 16 - 11 * sq)
        )
        bottom = (
            8
            * outer
            * (outer**2 - 1)
            * (4 * outer**2 - 1)
            * (4 * outer**2 - 9)
            * (4 * outer**2 - 25)
        )
        coeffs.append(top / bottom)
    matrix = np.zeros((day_count, day_count))
    for row_day in range(day_count):
        for offset_days in range(-half_span, half_span + 1):
            col_day = row_day + offset_days
            if 0 <= col_day < day_count:
                matrix[row_day, col_day] = coeffs[offset_days + half_span]
        matrix[row_day] = matrix[row_day] / matrix[row_day].sum()
    return matrix


def split2(x):
    hi = x.astype(bf16)
    return hi, (x - hi.astype(f32)).astype(bf16)


def dot_rows(rows, k, dims):
    return lax.dot_general(rows, k, (dims, ((), ())), preferred_element_type=f32)


def tiles(count):
    return [slice(at, at + LANES) for at in range(0, count, LANES)]


def turn(row):
    return jnp.transpose(jnp.broadcast_to(row, (LANES, LANES)))


def cols_of(u, k_ref):
    rows, cols = k_ref.shape
    totals = [0.0] * (cols // LANES)
    for block in tiles(rows):
        scale = turn(u[:, block])
        for j, tile in enumerate(tiles(cols)):
            totals[j] = totals[j] + jnp.sum((k_ref[block, tile] * scale).reshape(-1, 8, LANES), axis=0)
    return jnp.concatenate([jnp.sum(total, axis=0, keepdims=True) for total in totals], 1)


def rows_of(v, k_ref):
    rows, cols = k_ref.shape
    out = []
    for block in tiles(rows):
        total = 0.0
        for tile in tiles(cols):
            term = k_ref[block, tile]
            total = total + (term if v is None else term * v[:, tile])
        out.append(jnp.sum(jnp.transpose(total), axis=0, keepdims=True))
    return jnp.concatenate(out, 1)


def kernel_block(x, y, row_region, col_region, penalty):
    n, m = x.shape[0], y.shape[0]
    regions = penalty.shape[0]
    inv_root = 1.0 / math.sqrt(x.shape[1])
    inner = dot_rows(x, y, ((1,), (1,)))
    row_hot = (lax.broadcasted_iota(jnp.int32, (regions, n), 0) == row_region).astype(f32).astype(bf16)
    col_hot = (lax.broadcasted_iota(jnp.int32, (regions, m), 0) == col_region).astype(f32).astype(bf16)
    phi, plo = split2(penalty)
    qhi = jnp.dot(phi, col_hot, preferred_element_type=f32).astype(bf16)
    qlo = jnp.dot(plo, col_hot, preferred_element_type=f32).astype(bf16)
    pen = dot_rows(jnp.concatenate([row_hot, row_hot], 0), jnp.concatenate([qhi, qlo], 0), ((0,), (0,)))
    return jnp.exp(inner * inv_root - pen)


def run_copies(pairs, sems):
    copies = [pltpu.make_async_copy(src, dst, sems.at[k]) for k, (src, dst) in enumerate(pairs)]
    for copy in copies:
        copy.start()
    return copies


def packs_body(
    x_hbm, y_hbm, rr_hbm, seg_hbm, mass_hbm, cr_hbm, cm_hbm,
    xpack_ref, ypack_ref, xb_ref, yb_ref, rr_ref, seg_ref, cr_ref, sems,
):
    n, m = xb_ref.shape[0], yb_ref.shape[0]
    p, q = n // LANES, m // LANES
    copies = run_copies(
        (
            (x_hbm, xb_ref),
            (y_hbm, yb_ref),
            (rr_hbm, rr_ref),
            (seg_hbm, seg_ref),
            (mass_hbm, xpack_ref.at[pl.ds(n + 2 * p, p), :]),
            (cr_hbm, cr_ref),
            (cm_hbm, ypack_ref.at[pl.ds(m + q, q), :]),
        ),
        sems,
    )
    for copy in copies:
        copy.wait()
    xpack_ref[0:n, :] = xb_ref[...].astype(f32)
    xpack_ref[n : n + p, :] = rr_ref[...].astype(f32)
    xpack_ref[n + p : n + 2 * p, :] = seg_ref[...].astype(f32)
    ypack_ref[0:m, :] = yb_ref[...].astype(f32)
    ypack_ref[m : m + q, :] = cr_ref[...].astype(f32)


def hbm_call(body, name, args, out, scratch):
    return pl.pallas_call(
        body,
        in_specs=[HBM] * len(args),
        out_specs=[VMEM] * len(out),
        out_shape=[pltpu.VMEM(shape, f32) for shape in out],
        scratch_shapes=[*scratch, pltpu.SemaphoreType.DMA((len(args) + 1,))],
        compiler_params=PARAMS,
        name=name,
    )(*[pltpu.with_memory_space_constraint(arg, pltpu.HBM) for arg in args])


def packs_call(x, y, rr, seg, mass, cr, cm):
    n, m = x.shape[0], y.shape[0]
    p, q = n // LANES, m // LANES
    block = lambda v: v.reshape(-1, LANES)
    i32 = jnp.int32
    return hbm_call(
        packs_body,
        "packs",
        (x, y, block(rr), block(seg), block(mass), block(cr), block(cm)),
        [(n + 3 * p, LANES), (m + 2 * q, LANES)],
        [
            pltpu.VMEM(x.shape, bf16),
            pltpu.VMEM(y.shape, bf16),
            pltpu.VMEM((p, LANES), i32),
            pltpu.VMEM((p, LANES), i32),
            pltpu.VMEM((q, LANES), i32),
        ],
    )


def records_body(f_hbm, m_hbm, d_hbm, a_hbm, early_ref, late_ref, f_ref, m_ref, d_ref, sems):
    me = lax.axis_index("cohort")
    e, n = early_ref.shape[0] // 3, m_ref.shape[0]
    copies = run_copies(
        (
            (m_hbm, m_ref),
            (d_hbm, d_ref),
            (a_hbm.at[pl.ds(0, e), :], early_ref.at[pl.ds(2 * e, e), :]),
            (a_hbm.at[pl.ds(e, n - e), :], late_ref.at[pl.ds(2 * (n - e), n - e), :]),
            (f_hbm.at[me], f_ref),
        ),
        sems,
    )
    for copy in copies:
        copy.wait()
    for pack, rows in ((early_ref, slice(0, e)), (late_ref, slice(e, n))):
        size = rows.stop - rows.start
        pack[0:size, :] = m_ref[rows, :].astype(f32)
        pack[size : 2 * size, :] = d_ref[rows, :].astype(f32)


def records_call(table, merchants, days, amounts, early):
    n = merchants.shape[0]
    return hbm_call(
        records_body,
        "records",
        (table, merchants, days, amounts),
        [(3 * early, LANES), (3 * (n - early), LANES), table.shape[1:]],
        [pltpu.VMEM((n, LANES), jnp.int32), pltpu.VMEM((n, LANES), jnp.int32)],
    )


def flat(block):
    return jnp.concatenate([block[k : k + 1, :] for k in range(block.shape[0])], 1)


def gibbs_body(n, m, packs_x, packs_y, *refs):
    xpacks, ypacks = refs[:packs_x], refs[packs_x : packs_x + packs_y]
    pen_ref, k_ref, r_ref = refs[packs_x + packs_y :]
    p, q = n // LANES, m // LANES
    pen = pen_ref[...]
    ys = [(pack[0:m, :].astype(bf16), flat(pack[m : m + q, :]).astype(jnp.int32)) for pack in ypacks]
    for i, pack in enumerate(xpacks):
        x, rr = pack[0:n, :].astype(bf16), flat(pack[n : n + p, :]).astype(jnp.int32)
        for j, (y, cr) in enumerate(ys):
            k_ref[i * n : (i + 1) * n, j * m : (j + 1) * m] = kernel_block(x, y, rr, cr, pen)
    r_ref[...] = rows_of(None, k_ref)


def gibbs_call(n, m, xpacks, ypacks, penalty, after):
    rows, cols = len(xpacks) * n, len(ypacks) * m
    args = [*xpacks, *ypacks, penalty]
    return pl.pallas_call(
        lambda *refs: gibbs_body(n, m, len(xpacks), len(ypacks), *refs[: len(args)], *refs[-2:]),
        in_specs=[VMEM] * len(args) + [ANY] * len(after),
        out_specs=[VMEM] * 2,
        out_shape=[pltpu.VMEM((rows, cols), f32), pltpu.VMEM((1, rows), f32)],
        compiler_params=PARAMS,
        cost_estimate=pl.CostEstimate(
            flops=2 * rows * cols * LANES, transcendentals=rows * cols, bytes_accessed=rows * cols * 4
        ),
        name="gibbs",
    )(*args, *after)


def total_of(refs):
    total = refs[0][...]
    for ref in refs[1:]:
        total = total + ref[...]
    return total


def cols_body(n, parts, packs, *refs):
    p = n // LANES
    total = total_of(refs[:parts])
    pack_refs = refs[parts : parts + packs]
    k_ref, u_ref, c_ref = refs[parts + packs :]
    u = jnp.concatenate([flat(pack[n + 2 * p : n + 3 * p, :]) for pack in pack_refs], 1) / total
    u_ref[...] = u
    c_ref[...] = cols_of(u, k_ref)


def rows_body(m, parts, packs, *refs):
    q = m // LANES
    total = total_of(refs[:parts])
    pack_refs = refs[parts : parts + packs]
    k_ref, v_ref, r_ref = refs[parts + packs :]
    v = jnp.concatenate([flat(pack[m + q : m + 2 * q, :]) for pack in pack_refs], 1) / total
    v_ref[...] = v[:, :m]
    r_ref[...] = rows_of(v, k_ref)


def half_step(body, name, size, partials, packs, kernel, outs, after):
    args = [*partials, *packs, kernel]
    return pl.pallas_call(
        lambda *refs: body(size, len(partials), len(packs), *refs[: len(args)], *refs[-2:]),
        in_specs=[VMEM] * len(args) + [ANY] * len(after),
        out_specs=[VMEM] * 2,
        out_shape=outs,
        compiler_params=PARAMS,
        name=name,
    )(*args, *after)


def table_body(n, first, count, f_ref, pack_ref, hi_ref, lo_ref, token_ref):
    filt = f_ref[...]
    t_count = filt.shape[0]
    merch_rows = lax.broadcasted_iota(jnp.int32, (MERCH_DEV, LANES), 0).astype(f32).astype(bf16)
    merch_cols = lax.broadcasted_iota(jnp.int32, (LANES, MERCH_DEV), 1).astype(f32).astype(bf16)
    one, zero = jnp.ones((MERCH_DEV, LANES), bf16), jnp.zeros((MERCH_DEV, LANES), bf16)
    size = math.gcd(count, UNROLL)

    def group(step, carry):
        start = pl.multiple_of(step * size, size)
        merch = pack_ref[pl.ds(first + start, size), :]
        days = pack_ref[pl.ds(n + first + start, size), :].astype(jnp.int32)
        amounts = pack_ref[pl.ds(2 * n + first + start, size), :]
        turned = jnp.transpose(merch).astype(bf16)
        merch = merch.astype(bf16)
        tables = []
        for i in range(size):
            day = jnp.broadcast_to(days[i : i + 1, :], (t_count, LANES))
            coef = jnp.take_along_axis(filt, day, axis=1, mode="promise_in_bounds")
            both = jnp.concatenate(split2(coef * amounts[i : i + 1, :]), 0)
            if i % 2:
                hot = jnp.where(merch_cols == jnp.broadcast_to(turned[:, i : i + 1], merch_cols.shape), one, zero)
                both = dot_rows(both, hot, ((1,), (0,)))
            else:
                hot = jnp.where(merch_rows == merch[i : i + 1, :], one, zero)
                both = dot_rows(both, hot, ((1,), (1,)))
            tables.append(both[:t_count] + both[t_count:])
        hi, lo = split2(jnp.swapaxes(jnp.stack(tables, 0), 0, 1))
        hi_ref[:, pl.ds(start, size), :] = hi
        lo_ref[:, pl.ds(start, size), :] = lo
        return carry

    lax.fori_loop(0, count // size, group, 0)
    token_ref[...] = jnp.zeros_like(token_ref)


def table_call(filt, pack, n, first, count, after):
    t_count = filt.shape[0]
    hi, lo, token = pl.pallas_call(
        lambda *refs: table_body(n, first, count, *refs[:2], *refs[-3:]),
        in_specs=[VMEM] * 2 + [ANY] * len(after),
        out_specs=[VMEM] * 3,
        out_shape=[pltpu.VMEM((t_count, count, LANES), bf16)] * 2 + [pltpu.VMEM((8, LANES), f32)],
        compiler_params=PARAMS,
        cost_estimate=pl.CostEstimate(
            flops=4 * count * t_count * LANES * LANES, transcendentals=0, bytes_accessed=count * 60000
        ),
        name="tables",
    )(filt, pack, *after)
    return (hi, lo), token


def spread_body(n, t_count, parts, packs, count, t_ref, u_ref, *refs):
    p = n // LANES
    w = u_ref[...] * total_of(refs[:parts])
    pack_refs = refs[parts : parts + packs]
    pair_refs = refs[parts + packs : parts + packs + 2 * count]
    o_ref, w_ref = refs[-2:]
    w_ref[...] = w[:, :n]
    seg = jnp.concatenate([flat(pack[n + p : n + 2 * p, :]).astype(jnp.int32) for pack in pack_refs], 1)
    hot = lax.broadcasted_iota(jnp.int32, (SEG, w.shape[1]), 0) == seg
    whi, wlo = split2(jnp.where(hot, w, 0.0))
    both = jnp.concatenate([whi, wlo], 0)

    def take(part, t):
        return jnp.concatenate(
            [jnp.concatenate([pair_refs[2 * k + part][t + q] for k in range(count)], 0) for q in range(2)], 1
        )

    for step in range(0, t_count, 2):
        t = t_ref[0] + step
        two = jnp.dot(both, take(0, t), preferred_element_type=f32)
        out = two[:SEG] + two[SEG:] + jnp.dot(whi, take(1, t), preferred_element_type=f32)
        o_ref[step] = out[:, :LANES]
        o_ref[step + 1] = out[:, LANES:]


def spread_call(n, u, partials, packs, pairs, t_first, t_count, after):
    refs = [ref for pair in pairs for ref in pair]
    args = [jnp.full((1,), t_first, jnp.int32), u, *partials, *packs, *refs]
    return pl.pallas_call(
        lambda *refs: spread_body(
            n, t_count, len(partials), len(packs), len(pairs), *refs[: len(args)], *refs[-2:]
        ),
        in_specs=[pl.BlockSpec(memory_space=pltpu.SMEM)] + [VMEM] * (len(args) - 1) + [ANY] * len(after),
        out_specs=[VMEM] * 2,
        out_shape=[pltpu.VMEM((t_count, SEG, LANES), f32), pltpu.VMEM((1, n), f32)],
        compiler_params=PARAMS,
        name="spread",
    )(*args, *after)


def last_body(a_ref, b_ref, w_ref, v_ref, o_ref, w_out, v_out):
    o_ref[...] = a_ref[...] + b_ref[...]
    w_out[...] = w_ref[...]
    v_out[...] = v_ref[...]


def last_call(a, b, w, v):
    return pl.pallas_call(
        last_body,
        in_specs=[VMEM] * 4,
        out_specs=[VMEM] * 3,
        out_shape=[jax.ShapeDtypeStruct(x.shape, f32) for x in (a, w, v)],
        compiler_params=PARAMS,
        name="last",
    )(a, b, w, v)


def move(x, axis, size, pair, step, flip):
    blocks = size // pair

    def away(b):
        return b ^ step if blocks & (blocks - 1) == 0 else (b + step) % blocks

    return lax.ppermute(
        x, axis, [(b * pair + r, away(b) * pair + (r ^ flip)) for b in range(blocks) for r in range(pair)]
    )


def gate(x, *after):
    return lax.optimization_barrier((x, *after))[0]


def per_device(
    n_cohort,
    n_cell,
    cohort_features,
    cell_features,
    cohort_region,
    cell_region,
    penalty,
    cohort_mass,
    cell_mass,
    cohort_segment,
    spend_merchant,
    spend_day,
    spend_amount,
):
    n, m = cohort_features.shape[0], cell_features.shape[0]
    t_dev = DAYS // n_cohort
    n_y, n_z = n_cohort // 2, n_cell // 2
    table = np.zeros((n_cohort, 2 * t_dev, LANES), np.float32)
    henderson = filter_table(DAYS)
    for me in range(n_cohort):
        for k, dest in enumerate((me ^ 1, me)):
            table[me, k * t_dev : (k + 1) * t_dev, :DAYS] = henderson[dest * t_dev : (dest + 1) * t_dev]

    over_y = lambda x: [move(x, "cohort", n_cohort, 2, step, 0) for step in range(1, n_y)]
    core = lambda x: move(x, "cohort", n_cohort, 2, 0, 1)
    along_z = lambda x: [x] + [move(x, "cell", n_cell, 2, step, 0) for step in range(1, n_z)]

    unit = n // 8
    ahead = 4
    xpack, ypack = packs_call(
        cohort_features, cell_features, cohort_region, cohort_segment, cohort_mass, cell_region, cell_mass
    )
    *own, filt = records_call(jnp.asarray(table), spend_merchant, spend_day, spend_amount, ahead * unit)
    xpacks = [xpack] + over_y(xpack)
    ypacks = [ypack, move(ypack, "cell", n_cell, 2, 0, 1)]
    pairs = {}

    def tables(source, first, units, *after):
        for size in (units & ~1, units & 1):
            if size:
                late = int(first >= ahead)
                pack = own[late] if source == 0 else rpacks[late][source - 1]
                pairs[source, first], token = table_call(
                    filt, pack, pack.shape[0] // 3, (first - late * ahead) * unit, size * unit, after
                )
                after, first = [token], first + size
        return after

    def others(first, units, *after):
        for source in range(1, n_y):
            after = tables(source, first, units, *after)
        return after

    after = tables(0, ahead, 1, *tables(0, 0, ahead, filt))
    rpacks = [over_y(gate(own[0], *xpacks, *ypacks, *after))]
    kernel, partial = gibbs_call(n, m, xpacks, ypacks, penalty, after)
    row_sums = pltpu.VMEM((1, len(xpacks) * n), f32)
    col_sums = pltpu.VMEM((1, len(ypacks) * m), f32)
    lines = along_z(partial)
    after = tables(0, ahead + 1, 3, partial)
    fills = [[(0, 1), (1, 3)], [(4, 1), (5, 3)]]
    for iteration in range(ITERS):
        cohort_scale, column = half_step(
            cols_body, "cols", n, lines, xpacks, kernel, [row_sums, col_sums], after
        )
        sibling = core(column)
        if iteration == 0:
            rpacks.append(over_y(gate(own[1], column)))
        after = others(*fills[iteration][0], column)
        cell_scale, partial = half_step(
            rows_body, "rows", m, [column, sibling], ypacks, kernel,
            [pltpu.VMEM((1, m), f32), row_sums], after,
        )
        lines = along_z(partial)
        after = others(*fills[iteration][1], partial)
    ordered = [pairs[key] for key in sorted(pairs)]
    away, weights = spread_call(n, cohort_scale, lines, xpacks, ordered, 0, t_dev, after)
    mine, _ = spread_call(n, cohort_scale, lines, xpacks, ordered, t_dev, t_dev, after)
    out, weights, cell_scale = last_call(mine, core(away), weights, cell_scale)
    return (weights.reshape(-1), cell_scale.reshape(-1), out)


def solution(mesh):
    return jax.shard_map(
        functools.partial(per_device, mesh.shape["cohort"], mesh.shape["cell"]),
        mesh=mesh,
        in_specs=(
            P("cohort", None),
            P("cell", None),
            P("cohort"),
            P("cell"),
            P(),
            P("cohort"),
            P("cell"),
            P("cohort"),
            P("cohort", "cell"),
            P("cohort", "cell"),
            P("cohort", "cell"),
        ),
        out_specs=(P("cohort"), P("cell"), P("cohort", None, "cell")),
        check_vma=False,
    )
```

```python
import functools
import math

import jax
import jax.numpy as jnp
import numpy as np
from jax import lax
from jax.experimental import pallas as pl
from jax.experimental.pallas import tpu as pltpu
from jax.sharding import PartitionSpec as P

ITERS = 2
SEG = 32
MERCH_DEV = 128
DAYS = 64
LANES = 128
UNROLL = 128
WHOLE = 192

half_span = 11

f32 = jnp.float32
bf16 = jnp.bfloat16
VMEM = pl.BlockSpec(memory_space=pltpu.VMEM)
ANY = pl.BlockSpec(memory_space=pl.ANY)
HBM = pl.BlockSpec(memory_space=pltpu.HBM)
PARAMS = pltpu.CompilerParams(vmem_limit_bytes=20 * 2**20)


def filter_table(day_count):
    outer = 13.0
    coeffs = []
    for offset_days in range(-half_span, half_span + 1):
        sq = float(offset_days * offset_days)
        top = (
            315.0
            * ((outer - 1) ** 2 - sq)
            * (outer**2 - sq)
            * ((outer + 1) ** 2 - sq)
            * (3 * outer**2 - 16 - 11 * sq)
        )
        bottom = (
            8
            * outer
            * (outer**2 - 1)
            * (4 * outer**2 - 1)
            * (4 * outer**2 - 9)
            * (4 * outer**2 - 25)
        )
        coeffs.append(top / bottom)
    matrix = np.zeros((day_count, day_count))
    for row_day in range(day_count):
        for offset_days in range(-half_span, half_span + 1):
            col_day = row_day + offset_days
            if 0 <= col_day < day_count:
                matrix[row_day, col_day] = coeffs[offset_days + half_span]
        matrix[row_day] = matrix[row_day] / matrix[row_day].sum()
    return matrix


def split2(x):
    hi = x.astype(bf16)
    return hi, (x - hi.astype(f32)).astype(bf16)


def dot_rows(rows, k, dims):
    return lax.dot_general(rows, k, (dims, ((), ())), preferred_element_type=f32)


def tiles(count):
    return [slice(at, at + LANES) for at in range(0, count, LANES)]


def turn(row):
    return jnp.transpose(jnp.broadcast_to(row, (LANES, LANES)))


def cols_of(u, k_ref):
    rows, cols = k_ref.shape
    totals = [0.0] * (cols // LANES)
    for block in tiles(rows):
        scale = turn(u[:, block])
        for j, tile in enumerate(tiles(cols)):
            totals[j] = totals[j] + jnp.sum((k_ref[block, tile] * scale).reshape(-1, 8, LANES), axis=0)
    return jnp.concatenate([jnp.sum(total, axis=0, keepdims=True) for total in totals], 1)


def rows_of(v, k_ref):
    rows, cols = k_ref.shape
    out = []
    for block in tiles(rows):
        total = 0.0
        for tile in tiles(cols):
            term = k_ref[block, tile]
            total = total + (term if v is None else term * v[:, tile])
        out.append(jnp.sum(jnp.transpose(total), axis=0, keepdims=True))
    return jnp.concatenate(out, 1)


def kernel_block(x, y, row_region, col_region, penalty):
    n, m = x.shape[0], y.shape[0]
    regions = penalty.shape[0]
    inv_root = 1.0 / math.sqrt(x.shape[1])
    inner = dot_rows(x, y, ((1,), (1,)))
    row_hot = (lax.broadcasted_iota(jnp.int32, (regions, n), 0) == row_region).astype(f32).astype(bf16)
    col_hot = (lax.broadcasted_iota(jnp.int32, (regions, m), 0) == col_region).astype(f32).astype(bf16)
    phi, plo = split2(penalty)
    qhi = jnp.dot(phi, col_hot, preferred_element_type=f32).astype(bf16)
    qlo = jnp.dot(plo, col_hot, preferred_element_type=f32).astype(bf16)
    pen = dot_rows(jnp.concatenate([row_hot, row_hot], 0), jnp.concatenate([qhi, qlo], 0), ((0,), (0,)))
    return jnp.exp(inner * inv_root - pen)


def run_copies(pairs, sems):
    copies = [pltpu.make_async_copy(src, dst, sems.at[k]) for k, (src, dst) in enumerate(pairs)]
    for copy in copies:
        copy.start()
    return copies


def packs_body(
    x_hbm, y_hbm, rr_hbm, seg_hbm, mass_hbm, cr_hbm, cm_hbm,
    xpack_ref, ypack_ref, xb_ref, yb_ref, rr_ref, seg_ref, cr_ref, sems,
):
    n, m = xb_ref.shape[0], yb_ref.shape[0]
    p, q = n // LANES, m // LANES
    copies = run_copies(
        (
            (x_hbm, xb_ref),
            (y_hbm, yb_ref),
            (rr_hbm, rr_ref),
            (seg_hbm, seg_ref),
            (mass_hbm, xpack_ref.at[pl.ds(n + 2 * p, p), :]),
            (cr_hbm, cr_ref),
            (cm_hbm, ypack_ref.at[pl.ds(m + q, q), :]),
        ),
        sems,
    )
    for copy in copies:
        copy.wait()
    xpack_ref[0:n, :] = xb_ref[...].astype(f32)
    xpack_ref[n : n + p, :] = rr_ref[...].astype(f32)
    xpack_ref[n + p : n + 2 * p, :] = seg_ref[...].astype(f32)
    ypack_ref[0:m, :] = yb_ref[...].astype(f32)
    ypack_ref[m : m + q, :] = cr_ref[...].astype(f32)


def hbm_call(body, name, args, out, scratch):
    return pl.pallas_call(
        body,
        in_specs=[HBM] * len(args),
        out_specs=[VMEM] * len(out),
        out_shape=[pltpu.VMEM(shape, f32) for shape in out],
        scratch_shapes=[*scratch, pltpu.SemaphoreType.DMA((len(args) + 1,))],
        compiler_params=PARAMS,
        name=name,
    )(*[pltpu.with_memory_space_constraint(arg, pltpu.HBM) for arg in args])


def packs_call(x, y, rr, seg, mass, cr, cm):
    n, m = x.shape[0], y.shape[0]
    p, q = n // LANES, m // LANES
    block = lambda v: v.reshape(-1, LANES)
    i32 = jnp.int32
    return hbm_call(
        packs_body,
        "packs",
        (x, y, block(rr), block(seg), block(mass), block(cr), block(cm)),
        [(n + 3 * p, LANES), (m + 2 * q, LANES)],
        [
            pltpu.VMEM(x.shape, bf16),
            pltpu.VMEM(y.shape, bf16),
            pltpu.VMEM((p, LANES), i32),
            pltpu.VMEM((p, LANES), i32),
            pltpu.VMEM((q, LANES), i32),
        ],
    )


def records_body(f_hbm, m_hbm, d_hbm, a_hbm, early_ref, late_ref, f_ref, m_ref, d_ref, sems):
    me = lax.axis_index("cohort")
    e, n = early_ref.shape[0] // 3, m_ref.shape[0]
    copies = run_copies(
        (
            (m_hbm, m_ref),
            (d_hbm, d_ref),
            (a_hbm.at[pl.ds(0, e), :], early_ref.at[pl.ds(2 * e, e), :]),
            (a_hbm.at[pl.ds(e, n - e), :], late_ref.at[pl.ds(2 * (n - e), n - e), :]),
            (f_hbm.at[me], f_ref),
        ),
        sems,
    )
    for copy in copies:
        copy.wait()
    for pack, rows in ((early_ref, slice(0, e)), (late_ref, slice(e, n))):
        size = rows.stop - rows.start
        pack[0:size, :] = m_ref[rows, :].astype(f32)
        pack[size : 2 * size, :] = d_ref[rows, :].astype(f32)


def records_call(table, merchants, days, amounts, early):
    n = merchants.shape[0]
    return hbm_call(
        records_body,
        "records",
        (table, merchants, days, amounts),
        [(3 * early, LANES), (3 * (n - early), LANES), table.shape[1:]],
        [pltpu.VMEM((n, LANES), jnp.int32), pltpu.VMEM((n, LANES), jnp.int32)],
    )


def flat(block):
    return jnp.concatenate([block[k : k + 1, :] for k in range(block.shape[0])], 1)


def gibbs_body(n, m, packs_x, packs_y, *refs):
    xpacks, ypacks = refs[:packs_x], refs[packs_x : packs_x + packs_y]
    pen_ref, k_ref, r_ref = refs[packs_x + packs_y :]
    p, q = n // LANES, m // LANES
    pen = pen_ref[...]
    ys = [(pack[0:m, :].astype(bf16), flat(pack[m : m + q, :]).astype(jnp.int32)) for pack in ypacks]
    for i, pack in enumerate(xpacks):
        x, rr = pack[0:n, :].astype(bf16), flat(pack[n : n + p, :]).astype(jnp.int32)
        for j, (y, cr) in enumerate(ys):
            k_ref[i * n : (i + 1) * n, j * m : (j + 1) * m] = kernel_block(x, y, rr, cr, pen)
    r_ref[...] = rows_of(None, k_ref)


def gibbs_call(n, m, xpacks, ypacks, penalty, after):
    rows, cols = len(xpacks) * n, len(ypacks) * m
    args = [*xpacks, *ypacks, penalty]
    return pl.pallas_call(
        lambda *refs: gibbs_body(n, m, len(xpacks), len(ypacks), *refs[: len(args)], *refs[-2:]),
        in_specs=[VMEM] * len(args) + [ANY] * len(after),
        out_specs=[VMEM] * 2,
        out_shape=[pltpu.VMEM((rows, cols), f32), pltpu.VMEM((1, rows), f32)],
        compiler_params=PARAMS,
        cost_estimate=pl.CostEstimate(
            flops=2 * rows * cols * LANES, transcendentals=rows * cols, bytes_accessed=rows * cols * 4
        ),
        name="gibbs",
    )(*args, *after)


def total_of(refs):
    total = refs[0][...]
    for ref in refs[1:]:
        total = total + ref[...]
    return total


def cols_body(n, parts, packs, *refs):
    p = n // LANES
    total = total_of(refs[:parts])
    pack_refs = refs[parts : parts + packs]
    k_ref, u_ref, c_ref = refs[parts + packs :]
    u = jnp.concatenate([flat(pack[n + 2 * p : n + 3 * p, :]) for pack in pack_refs], 1) / total
    u_ref[...] = u
    c_ref[...] = cols_of(u, k_ref)


def rows_body(m, parts, packs, *refs):
    q = m // LANES
    total = total_of(refs[:parts])
    pack_refs = refs[parts : parts + packs]
    k_ref, v_ref, r_ref = refs[parts + packs :]
    v = jnp.concatenate([flat(pack[m + q : m + 2 * q, :]) for pack in pack_refs], 1) / total
    v_ref[...] = v[:, :m]
    r_ref[...] = rows_of(v, k_ref)


def half_step(body, name, size, partials, packs, kernel, outs, after):
    args = [*partials, *packs, kernel]
    return pl.pallas_call(
        lambda *refs: body(size, len(partials), len(packs), *refs[: len(args)], *refs[-2:]),
        in_specs=[VMEM] * len(args) + [ANY] * len(after),
        out_specs=[VMEM] * 2,
        out_shape=outs,
        compiler_params=PARAMS,
        name=name,
    )(*args, *after)


def table_body(n, first, count, f_ref, pack_ref, hi_ref, lo_ref, token_ref):
    filt = f_ref[...]
    t_count = filt.shape[0]
    merch_rows = lax.broadcasted_iota(jnp.int32, (MERCH_DEV, LANES), 0).astype(f32).astype(bf16)
    merch_cols = lax.broadcasted_iota(jnp.int32, (LANES, MERCH_DEV), 1).astype(f32).astype(bf16)
    one, zero = jnp.ones((MERCH_DEV, LANES), bf16), jnp.zeros((MERCH_DEV, LANES), bf16)
    size = count if count <= WHOLE else math.gcd(count, UNROLL)

    def group(step, carry):
        start = pl.multiple_of(step * size, size)
        merch = pack_ref[pl.ds(first + start, size), :]
        days = pack_ref[pl.ds(n + first + start, size), :].astype(jnp.int32)
        amounts = pack_ref[pl.ds(2 * n + first + start, size), :]
        turned = jnp.transpose(merch).astype(bf16)
        merch = merch.astype(bf16)
        tables = []
        for i in range(size):
            day = jnp.broadcast_to(days[i : i + 1, :], (t_count, LANES))
            coef = jnp.take_along_axis(filt, day, axis=1, mode="promise_in_bounds")
            both = jnp.concatenate(split2(coef * amounts[i : i + 1, :]), 0)
            if i % 2:
                hot = jnp.where(merch_cols == jnp.broadcast_to(turned[:, i : i + 1], merch_cols.shape), one, zero)
                both = dot_rows(both, hot, ((1,), (0,)))
            else:
                hot = jnp.where(merch_rows == merch[i : i + 1, :], one, zero)
                both = dot_rows(both, hot, ((1,), (1,)))
            tables.append(both[:t_count] + both[t_count:])
        hi, lo = split2(jnp.swapaxes(jnp.stack(tables, 0), 0, 1))
        hi_ref[:, pl.ds(start, size), :] = hi
        lo_ref[:, pl.ds(start, size), :] = lo
        return carry

    lax.fori_loop(0, count // size, group, 0)
    token_ref[...] = jnp.zeros_like(token_ref)


def table_call(filt, pack, n, first, count, after):
    t_count = filt.shape[0]
    hi, lo, token = pl.pallas_call(
        lambda *refs: table_body(n, first, count, *refs[:2], *refs[-3:]),
        in_specs=[VMEM] * 2 + [ANY] * len(after),
        out_specs=[VMEM] * 3,
        out_shape=[pltpu.VMEM((t_count, count, LANES), bf16)] * 2 + [pltpu.VMEM((8, LANES), f32)],
        compiler_params=PARAMS,
        cost_estimate=pl.CostEstimate(
            flops=4 * count * t_count * LANES * LANES, transcendentals=0, bytes_accessed=count * 60000
        ),
        name="tables",
    )(filt, pack, *after)
    return (hi, lo), token


def spread_body(n, t_count, parts, packs, count, t_ref, u_ref, *refs):
    p = n // LANES
    w = u_ref[...] * total_of(refs[:parts])
    pack_refs = refs[parts : parts + packs]
    pair_refs = refs[parts + packs : parts + packs + 2 * count]
    o_ref, w_ref = refs[-2:]
    w_ref[...] = w[:, :n]
    seg = jnp.concatenate([flat(pack[n + p : n + 2 * p, :]).astype(jnp.int32) for pack in pack_refs], 1)
    hot = lax.broadcasted_iota(jnp.int32, (SEG, w.shape[1]), 0) == seg
    whi, wlo = split2(jnp.where(hot, w, 0.0))
    both = jnp.concatenate([whi, wlo], 0)

    def take(part, t):
        return jnp.concatenate(
            [jnp.concatenate([pair_refs[2 * k + part][t + q] for k in range(count)], 0) for q in range(2)], 1
        )

    for step in range(0, t_count, 2):
        t = t_ref[0] + step
        two = jnp.dot(both, take(0, t), preferred_element_type=f32)
        out = two[:SEG] + two[SEG:] + jnp.dot(whi, take(1, t), preferred_element_type=f32)
        o_ref[step] = out[:, :LANES]
        o_ref[step + 1] = out[:, LANES:]


def spread_call(n, u, partials, packs, pairs, t_first, t_count, after):
    refs = [ref for pair in pairs for ref in pair]
    args = [jnp.full((1,), t_first, jnp.int32), u, *partials, *packs, *refs]
    return pl.pallas_call(
        lambda *refs: spread_body(
            n, t_count, len(partials), len(packs), len(pairs), *refs[: len(args)], *refs[-2:]
        ),
        in_specs=[pl.BlockSpec(memory_space=pltpu.SMEM)] + [VMEM] * (len(args) - 1) + [ANY] * len(after),
        out_specs=[VMEM] * 2,
        out_shape=[pltpu.VMEM((t_count, SEG, LANES), f32), pltpu.VMEM((1, n), f32)],
        compiler_params=PARAMS,
        name="spread",
    )(*args, *after)


def last_body(a_ref, b_ref, w_ref, v_ref, o_ref, w_out, v_out):
    o_ref[...] = a_ref[...] + b_ref[...]
    w_out[...] = w_ref[...]
    v_out[...] = v_ref[...]


def last_call(a, b, w, v):
    return pl.pallas_call(
        last_body,
        in_specs=[VMEM] * 4,
        out_specs=[VMEM] * 3,
        out_shape=[jax.ShapeDtypeStruct(x.shape, f32) for x in (a, w, v)],
        compiler_params=PARAMS,
        name="last",
    )(a, b, w, v)


def move(x, axis, size, pair, step, flip):
    blocks = size // pair

    def away(b):
        return b ^ step if blocks & (blocks - 1) == 0 else (b + step) % blocks

    return lax.ppermute(
        x, axis, [(b * pair + r, away(b) * pair + (r ^ flip)) for b in range(blocks) for r in range(pair)]
    )


def gate(x, *after):
    return lax.optimization_barrier((x, *after))[0]


def per_device(
    n_cohort,
    n_cell,
    cohort_features,
    cell_features,
    cohort_region,
    cell_region,
    penalty,
    cohort_mass,
    cell_mass,
    cohort_segment,
    spend_merchant,
    spend_day,
    spend_amount,
):
    n, m = cohort_features.shape[0], cell_features.shape[0]
    t_dev = DAYS // n_cohort
    n_y, n_z = n_cohort // 2, n_cell // 2
    table = np.zeros((n_cohort, 2 * t_dev, LANES), np.float32)
    henderson = filter_table(DAYS)
    for me in range(n_cohort):
        for k, dest in enumerate((me ^ 1, me)):
            table[me, k * t_dev : (k + 1) * t_dev, :DAYS] = henderson[dest * t_dev : (dest + 1) * t_dev]

    over_y = lambda x: [move(x, "cohort", n_cohort, 2, step, 0) for step in range(1, n_y)]
    core = lambda x: move(x, "cohort", n_cohort, 2, 0, 1)
    along_z = lambda x: [x] + [move(x, "cell", n_cell, 2, step, 0) for step in range(1, n_z)]

    unit = n // 8
    ahead = 4
    xpack, ypack = packs_call(
        cohort_features, cell_features, cohort_region, cohort_segment, cohort_mass, cell_region, cell_mass
    )
    *own, filt = records_call(jnp.asarray(table), spend_merchant, spend_day, spend_amount, ahead * unit)
    xpacks = [xpack] + over_y(xpack)
    ypacks = [ypack, move(ypack, "cell", n_cell, 2, 0, 1)]
    pairs = {}

    def tables(source, first, units, *after):
        late = int(first >= ahead)
        pack = own[late] if source == 0 else rpacks[late][source - 1]
        pairs[source, first], token = table_call(
            filt, pack, pack.shape[0] // 3, (first - late * ahead) * unit, units * unit, after
        )
        return [token]

    def others(first, units, *after):
        for source in range(1, n_y):
            after = tables(source, first, units, *after)
        return after

    after = tables(0, ahead, 1, *tables(0, 0, ahead, filt))
    rpacks = [over_y(gate(own[0], *xpacks, *ypacks, *after))]
    kernel, partial = gibbs_call(n, m, xpacks, ypacks, penalty, after)
    row_sums = pltpu.VMEM((1, len(xpacks) * n), f32)
    col_sums = pltpu.VMEM((1, len(ypacks) * m), f32)
    lines = along_z(partial)
    after = tables(0, ahead + 1, 3, partial)
    fills = [[(0, 1), (1, 3)], [(4, 1), (5, 3)]]
    for iteration in range(ITERS):
        cohort_scale, column = half_step(
            cols_body, "cols", n, lines, xpacks, kernel, [row_sums, col_sums], after
        )
        sibling = core(column)
        if iteration == 0:
            rpacks.append(over_y(gate(own[1], column)))
        after = others(*fills[iteration][0], column)
        cell_scale, partial = half_step(
            rows_body, "rows", m, [column, sibling], ypacks, kernel,
            [pltpu.VMEM((1, m), f32), row_sums], after,
        )
        lines = along_z(partial)
        after = others(*fills[iteration][1], partial)
    ordered = [pairs[key] for key in sorted(pairs)]
    away, weights = spread_call(n, cohort_scale, lines, xpacks, ordered, 0, t_dev, after)
    mine, _ = spread_call(n, cohort_scale, lines, xpacks, ordered, t_dev, t_dev, after)
    out, weights, cell_scale = last_call(mine, core(away), weights, cell_scale)
    return (weights.reshape(-1), cell_scale.reshape(-1), out)


def solution(mesh):
    return jax.shard_map(
        functools.partial(per_device, mesh.shape["cohort"], mesh.shape["cell"]),
        mesh=mesh,
        in_specs=(
            P("cohort", None),
            P("cell", None),
            P("cohort"),
            P("cell"),
            P(),
            P("cohort"),
            P("cell"),
            P("cohort"),
            P("cohort", "cell"),
            P("cohort", "cell"),
            P("cohort", "cell"),
        ),
        out_specs=(P("cohort"), P("cell"), P("cohort", None, "cell")),
        check_vma=False,
    )
```

```python
import functools
import math

import jax
import jax.numpy as jnp
import numpy as np
from jax import lax
from jax.experimental import pallas as pl
from jax.experimental.pallas import tpu as pltpu
from jax.sharding import PartitionSpec as P

ITERS = 2
SEG = 32
MERCH_DEV = 128
DAYS = 64
LANES = 128
UNROLL = 128
WHOLE = 256

half_span = 11

f32 = jnp.float32
bf16 = jnp.bfloat16
VMEM = pl.BlockSpec(memory_space=pltpu.VMEM)
ANY = pl.BlockSpec(memory_space=pl.ANY)
HBM = pl.BlockSpec(memory_space=pltpu.HBM)
PARAMS = pltpu.CompilerParams(vmem_limit_bytes=20 * 2**20)


def filter_table(day_count):
    outer = 13.0
    coeffs = []
    for offset_days in range(-half_span, half_span + 1):
        sq = float(offset_days * offset_days)
        top = (
            315.0
            * ((outer - 1) ** 2 - sq)
            * (outer**2 - sq)
            * ((outer + 1) ** 2 - sq)
            * (3 * outer**2 - 16 - 11 * sq)
        )
        bottom = (
            8
            * outer
            * (outer**2 - 1)
            * (4 * outer**2 - 1)
            * (4 * outer**2 - 9)
            * (4 * outer**2 - 25)
        )
        coeffs.append(top / bottom)
    matrix = np.zeros((day_count, day_count))
    for row_day in range(day_count):
        for offset_days in range(-half_span, half_span + 1):
            col_day = row_day + offset_days
            if 0 <= col_day < day_count:
                matrix[row_day, col_day] = coeffs[offset_days + half_span]
        matrix[row_day] = matrix[row_day] / matrix[row_day].sum()
    return matrix


def split2(x):
    hi = x.astype(bf16)
    return hi, (x - hi.astype(f32)).astype(bf16)


def dot_rows(rows, k, dims):
    return lax.dot_general(rows, k, (dims, ((), ())), preferred_element_type=f32)


def tiles(count):
    return [slice(at, at + LANES) for at in range(0, count, LANES)]


def turn(row):
    return jnp.transpose(jnp.broadcast_to(row, (LANES, LANES)))


def cols_of(u, k_ref):
    rows, cols = k_ref.shape
    totals = [0.0] * (cols // LANES)
    for block in tiles(rows):
        scale = turn(u[:, block])
        for j, tile in enumerate(tiles(cols)):
            totals[j] = totals[j] + jnp.sum((k_ref[block, tile] * scale).reshape(-1, 8, LANES), axis=0)
    return jnp.concatenate([jnp.sum(total, axis=0, keepdims=True) for total in totals], 1)


def rows_of(v, k_ref):
    rows, cols = k_ref.shape
    out = []
    for block in tiles(rows):
        total = 0.0
        for tile in tiles(cols):
            term = k_ref[block, tile]
            total = total + (term if v is None else term * v[:, tile])
        out.append(jnp.sum(jnp.transpose(total), axis=0, keepdims=True))
    return jnp.concatenate(out, 1)


def kernel_block(x, y, row_region, col_region, penalty):
    n, m = x.shape[0], y.shape[0]
    regions = penalty.shape[0]
    inv_root = 1.0 / math.sqrt(x.shape[1])
    inner = dot_rows(x, y, ((1,), (1,)))
    row_hot = (lax.broadcasted_iota(jnp.int32, (regions, n), 0) == row_region).astype(f32).astype(bf16)
    col_hot = (lax.broadcasted_iota(jnp.int32, (regions, m), 0) == col_region).astype(f32).astype(bf16)
    phi, plo = split2(penalty)
    qhi = jnp.dot(phi, col_hot, preferred_element_type=f32).astype(bf16)
    qlo = jnp.dot(plo, col_hot, preferred_element_type=f32).astype(bf16)
    pen = dot_rows(jnp.concatenate([row_hot, row_hot], 0), jnp.concatenate([qhi, qlo], 0), ((0,), (0,)))
    return jnp.exp(inner * inv_root - pen)


def run_copies(pairs, sems):
    copies = [pltpu.make_async_copy(src, dst, sems.at[k]) for k, (src, dst) in enumerate(pairs)]
    for copy in copies:
        copy.start()
    return copies


def packs_body(
    x_hbm, y_hbm, rr_hbm, seg_hbm, mass_hbm, cr_hbm, cm_hbm,
    xpack_ref, ypack_ref, xb_ref, yb_ref, rr_ref, seg_ref, cr_ref, sems,
):
    n, m = xb_ref.shape[0], yb_ref.shape[0]
    p, q = n // LANES, m // LANES
    copies = run_copies(
        (
            (x_hbm, xb_ref),
            (y_hbm, yb_ref),
            (rr_hbm, rr_ref),
            (seg_hbm, seg_ref),
            (mass_hbm, xpack_ref.at[pl.ds(n + 2 * p, p), :]),
            (cr_hbm, cr_ref),
            (cm_hbm, ypack_ref.at[pl.ds(m + q, q), :]),
        ),
        sems,
    )
    for copy in copies:
        copy.wait()
    xpack_ref[0:n, :] = xb_ref[...].astype(f32)
    xpack_ref[n : n + p, :] = rr_ref[...].astype(f32)
    xpack_ref[n + p : n + 2 * p, :] = seg_ref[...].astype(f32)
    ypack_ref[0:m, :] = yb_ref[...].astype(f32)
    ypack_ref[m : m + q, :] = cr_ref[...].astype(f32)


def hbm_call(body, name, args, out, scratch):
    return pl.pallas_call(
        body,
        in_specs=[HBM] * len(args),
        out_specs=[VMEM] * len(out),
        out_shape=[pltpu.VMEM(shape, f32) for shape in out],
        scratch_shapes=[*scratch, pltpu.SemaphoreType.DMA((len(args) + 1,))],
        compiler_params=PARAMS,
        name=name,
    )(*[pltpu.with_memory_space_constraint(arg, pltpu.HBM) for arg in args])


def packs_call(x, y, rr, seg, mass, cr, cm):
    n, m = x.shape[0], y.shape[0]
    p, q = n // LANES, m // LANES
    block = lambda v: v.reshape(-1, LANES)
    i32 = jnp.int32
    return hbm_call(
        packs_body,
        "packs",
        (x, y, block(rr), block(seg), block(mass), block(cr), block(cm)),
        [(n + 3 * p, LANES), (m + 2 * q, LANES)],
        [
            pltpu.VMEM(x.shape, bf16),
            pltpu.VMEM(y.shape, bf16),
            pltpu.VMEM((p, LANES), i32),
            pltpu.VMEM((p, LANES), i32),
            pltpu.VMEM((q, LANES), i32),
        ],
    )


def records_body(f_hbm, m_hbm, d_hbm, a_hbm, early_ref, late_ref, f_ref, m_ref, d_ref, sems):
    me = lax.axis_index("cohort")
    e, n = early_ref.shape[0] // 3, m_ref.shape[0]
    copies = run_copies(
        (
            (m_hbm, m_ref),
            (d_hbm, d_ref),
            (a_hbm.at[pl.ds(0, e), :], early_ref.at[pl.ds(2 * e, e), :]),
            (a_hbm.at[pl.ds(e, n - e), :], late_ref.at[pl.ds(2 * (n - e), n - e), :]),
            (f_hbm.at[me], f_ref),
        ),
        sems,
    )
    for copy in copies:
        copy.wait()
    for pack, rows in ((early_ref, slice(0, e)), (late_ref, slice(e, n))):
        size = rows.stop - rows.start
        pack[0:size, :] = m_ref[rows, :].astype(f32)
        pack[size : 2 * size, :] = d_ref[rows, :].astype(f32)


def records_call(table, merchants, days, amounts, early):
    n = merchants.shape[0]
    return hbm_call(
        records_body,
        "records",
        (table, merchants, days, amounts),
        [(3 * early, LANES), (3 * (n - early), LANES), table.shape[1:]],
        [pltpu.VMEM((n, LANES), jnp.int32), pltpu.VMEM((n, LANES), jnp.int32)],
    )


def flat(block):
    return jnp.concatenate([block[k : k + 1, :] for k in range(block.shape[0])], 1)


def gibbs_body(n, m, packs_x, packs_y, *refs):
    xpacks, ypacks = refs[:packs_x], refs[packs_x : packs_x + packs_y]
    pen_ref, k_ref, r_ref = refs[packs_x + packs_y :]
    p, q = n // LANES, m // LANES
    pen = pen_ref[...]
    ys = [(pack[0:m, :].astype(bf16), flat(pack[m : m + q, :]).astype(jnp.int32)) for pack in ypacks]
    for i, pack in enumerate(xpacks):
        x, rr = pack[0:n, :].astype(bf16), flat(pack[n : n + p, :]).astype(jnp.int32)
        for j, (y, cr) in enumerate(ys):
            k_ref[i * n : (i + 1) * n, j * m : (j + 1) * m] = kernel_block(x, y, rr, cr, pen)
    r_ref[...] = rows_of(None, k_ref)


def gibbs_call(n, m, xpacks, ypacks, penalty, after):
    rows, cols = len(xpacks) * n, len(ypacks) * m
    args = [*xpacks, *ypacks, penalty]
    return pl.pallas_call(
        lambda *refs: gibbs_body(n, m, len(xpacks), len(ypacks), *refs[: len(args)], *refs[-2:]),
        in_specs=[VMEM] * len(args) + [ANY] * len(after),
        out_specs=[VMEM] * 2,
        out_shape=[pltpu.VMEM((rows, cols), f32), pltpu.VMEM((1, rows), f32)],
        compiler_params=PARAMS,
        cost_estimate=pl.CostEstimate(
            flops=2 * rows * cols * LANES, transcendentals=rows * cols, bytes_accessed=rows * cols * 4
        ),
        name="gibbs",
    )(*args, *after)


def total_of(refs):
    total = refs[0][...]
    for ref in refs[1:]:
        total = total + ref[...]
    return total


def cols_body(n, parts, packs, *refs):
    p = n // LANES
    total = total_of(refs[:parts])
    pack_refs = refs[parts : parts + packs]
    k_ref, u_ref, c_ref = refs[parts + packs :]
    u = jnp.concatenate([flat(pack[n + 2 * p : n + 3 * p, :]) for pack in pack_refs], 1) / total
    u_ref[...] = u
    c_ref[...] = cols_of(u, k_ref)


def rows_body(m, parts, packs, *refs):
    q = m // LANES
    total = total_of(refs[:parts])
    pack_refs = refs[parts : parts + packs]
    k_ref, v_ref, r_ref = refs[parts + packs :]
    v = jnp.concatenate([flat(pack[m + q : m + 2 * q, :]) for pack in pack_refs], 1) / total
    v_ref[...] = v[:, :m]
    r_ref[...] = rows_of(v, k_ref)


def half_step(body, name, size, partials, packs, kernel, outs, after):
    args = [*partials, *packs, kernel]
    return pl.pallas_call(
        lambda *refs: body(size, len(partials), len(packs), *refs[: len(args)], *refs[-2:]),
        in_specs=[VMEM] * len(args) + [ANY] * len(after),
        out_specs=[VMEM] * 2,
        out_shape=outs,
        compiler_params=PARAMS,
        name=name,
    )(*args, *after)


def table_body(n, first, count, f_ref, pack_ref, hi_ref, lo_ref, token_ref):
    filt = f_ref[...]
    t_count = filt.shape[0]
    merch_rows = lax.broadcasted_iota(jnp.int32, (MERCH_DEV, LANES), 0).astype(f32).astype(bf16)
    merch_cols = lax.broadcasted_iota(jnp.int32, (LANES, MERCH_DEV), 1).astype(f32).astype(bf16)
    one, zero = jnp.ones((MERCH_DEV, LANES), bf16), jnp.zeros((MERCH_DEV, LANES), bf16)
    size = count if count <= WHOLE else math.gcd(count, UNROLL)

    def group(step, carry):
        start = pl.multiple_of(step * size, size)
        merch = pack_ref[pl.ds(first + start, size), :]
        days = pack_ref[pl.ds(n + first + start, size), :].astype(jnp.int32)
        amounts = pack_ref[pl.ds(2 * n + first + start, size), :]
        turned = jnp.transpose(merch).astype(bf16)
        merch = merch.astype(bf16)
        tables = []
        for i in range(size):
            day = jnp.broadcast_to(days[i : i + 1, :], (t_count, LANES))
            coef = jnp.take_along_axis(filt, day, axis=1, mode="promise_in_bounds")
            both = jnp.concatenate(split2(coef * amounts[i : i + 1, :]), 0)
            if i % 2:
                hot = jnp.where(merch_cols == jnp.broadcast_to(turned[:, i : i + 1], merch_cols.shape), one, zero)
                both = dot_rows(both, hot, ((1,), (0,)))
            else:
                hot = jnp.where(merch_rows == merch[i : i + 1, :], one, zero)
                both = dot_rows(both, hot, ((1,), (1,)))
            tables.append(both[:t_count] + both[t_count:])
        hi, lo = split2(jnp.swapaxes(jnp.stack(tables, 0), 0, 1))
        hi_ref[:, pl.ds(start, size), :] = hi
        lo_ref[:, pl.ds(start, size), :] = lo
        return carry

    lax.fori_loop(0, count // size, group, 0)
    token_ref[...] = jnp.zeros_like(token_ref)


def table_call(filt, pack, n, first, count, after):
    t_count = filt.shape[0]
    hi, lo, token = pl.pallas_call(
        lambda *refs: table_body(n, first, count, *refs[:2], *refs[-3:]),
        in_specs=[VMEM] * 2 + [ANY] * len(after),
        out_specs=[VMEM] * 3,
        out_shape=[pltpu.VMEM((t_count, count, LANES), bf16)] * 2 + [pltpu.VMEM((8, LANES), f32)],
        compiler_params=PARAMS,
        cost_estimate=pl.CostEstimate(
            flops=4 * count * t_count * LANES * LANES, transcendentals=0, bytes_accessed=count * 60000
        ),
        name="tables",
    )(filt, pack, *after)
    return (hi, lo), token


def spread_body(n, t_count, parts, packs, count, t_ref, u_ref, *refs):
    p = n // LANES
    w = u_ref[...] * total_of(refs[:parts])
    pack_refs = refs[parts : parts + packs]
    pair_refs = refs[parts + packs : parts + packs + 2 * count]
    o_ref, w_ref = refs[-2:]
    w_ref[...] = w[:, :n]
    seg = jnp.concatenate([flat(pack[n + p : n + 2 * p, :]).astype(jnp.int32) for pack in pack_refs], 1)
    hot = lax.broadcasted_iota(jnp.int32, (SEG, w.shape[1]), 0) == seg
    whi, wlo = split2(jnp.where(hot, w, 0.0))
    both = jnp.concatenate([whi, wlo], 0)

    def take(part, t):
        return jnp.concatenate(
            [jnp.concatenate([pair_refs[2 * k + part][t + q] for k in range(count)], 0) for q in range(2)], 1
        )

    for step in range(0, t_count, 2):
        t = t_ref[0] + step
        two = jnp.dot(both, take(0, t), preferred_element_type=f32)
        out = two[:SEG] + two[SEG:] + jnp.dot(whi, take(1, t), preferred_element_type=f32)
        o_ref[step] = out[:, :LANES]
        o_ref[step + 1] = out[:, LANES:]


def spread_call(n, u, partials, packs, pairs, t_first, t_count, after):
    refs = [ref for pair in pairs for ref in pair]
    args = [jnp.full((1,), t_first, jnp.int32), u, *partials, *packs, *refs]
    return pl.pallas_call(
        lambda *refs: spread_body(
            n, t_count, len(partials), len(packs), len(pairs), *refs[: len(args)], *refs[-2:]
        ),
        in_specs=[pl.BlockSpec(memory_space=pltpu.SMEM)] + [VMEM] * (len(args) - 1) + [ANY] * len(after),
        out_specs=[VMEM] * 2,
        out_shape=[pltpu.VMEM((t_count, SEG, LANES), f32), pltpu.VMEM((1, n), f32)],
        compiler_params=PARAMS,
        name="spread",
    )(*args, *after)


def last_body(a_ref, b_ref, w_ref, v_ref, o_ref, w_out, v_out):
    o_ref[...] = a_ref[...] + b_ref[...]
    w_out[...] = w_ref[...]
    v_out[...] = v_ref[...]


def last_call(a, b, w, v):
    return pl.pallas_call(
        last_body,
        in_specs=[VMEM] * 4,
        out_specs=[VMEM] * 3,
        out_shape=[jax.ShapeDtypeStruct(x.shape, f32) for x in (a, w, v)],
        compiler_params=PARAMS,
        name="last",
    )(a, b, w, v)


def move(x, axis, size, pair, step, flip):
    blocks = size // pair

    def away(b):
        return b ^ step if blocks & (blocks - 1) == 0 else (b + step) % blocks

    return lax.ppermute(
        x, axis, [(b * pair + r, away(b) * pair + (r ^ flip)) for b in range(blocks) for r in range(pair)]
    )


def gate(x, *after):
    return lax.optimization_barrier((x, *after))[0]


def per_device(
    n_cohort,
    n_cell,
    cohort_features,
    cell_features,
    cohort_region,
    cell_region,
    penalty,
    cohort_mass,
    cell_mass,
    cohort_segment,
    spend_merchant,
    spend_day,
    spend_amount,
):
    n, m = cohort_features.shape[0], cell_features.shape[0]
    t_dev = DAYS // n_cohort
    n_y, n_z = n_cohort // 2, n_cell // 2
    table = np.zeros((n_cohort, 2 * t_dev, LANES), np.float32)
    henderson = filter_table(DAYS)
    for me in range(n_cohort):
        for k, dest in enumerate((me ^ 1, me)):
            table[me, k * t_dev : (k + 1) * t_dev, :DAYS] = henderson[dest * t_dev : (dest + 1) * t_dev]

    over_y = lambda x: [move(x, "cohort", n_cohort, 2, step, 0) for step in range(1, n_y)]
    core = lambda x: move(x, "cohort", n_cohort, 2, 0, 1)
    along_z = lambda x: [x] + [move(x, "cell", n_cell, 2, step, 0) for step in range(1, n_z)]

    unit = n // 8
    ahead = 4
    xpack, ypack = packs_call(
        cohort_features, cell_features, cohort_region, cohort_segment, cohort_mass, cell_region, cell_mass
    )
    *own, filt = records_call(jnp.asarray(table), spend_merchant, spend_day, spend_amount, ahead * unit)
    xpacks = [xpack] + over_y(xpack)
    ypacks = [ypack, move(ypack, "cell", n_cell, 2, 0, 1)]
    pairs = {}

    def tables(source, first, units, *after):
        late = int(first >= ahead)
        pack = own[late] if source == 0 else rpacks[late][source - 1]
        pairs[source, first], token = table_call(
            filt, pack, pack.shape[0] // 3, (first - late * ahead) * unit, units * unit, after
        )
        return [token]

    def others(first, units, *after):
        for source in range(1, n_y):
            after = tables(source, first, units, *after)
        return after

    after = tables(0, ahead, 1, *tables(0, 0, ahead, filt))
    rpacks = [over_y(gate(own[0], *xpacks, *ypacks, *after))]
    kernel, partial = gibbs_call(n, m, xpacks, ypacks, penalty, after)
    row_sums = pltpu.VMEM((1, len(xpacks) * n), f32)
    col_sums = pltpu.VMEM((1, len(ypacks) * m), f32)
    lines = along_z(partial)
    after = tables(0, ahead + 1, 3, partial)
    fills = [[(0, 1), (1, 3)], [(4, 1), (5, 3)]]
    for iteration in range(ITERS):
        cohort_scale, column = half_step(
            cols_body, "cols", n, lines, xpacks, kernel, [row_sums, col_sums], after
        )
        sibling = core(column)
        if iteration == 0:
            rpacks.append(over_y(gate(own[1], column)))
        after = others(*fills[iteration][0], column)
        cell_scale, partial = half_step(
            rows_body, "rows", m, [column, sibling], ypacks, kernel,
            [pltpu.VMEM((1, m), f32), row_sums], after,
        )
        lines = along_z(partial)
        after = others(*fills[iteration][1], partial)
    ordered = [pairs[key] for key in sorted(pairs)]
    away, weights = spread_call(n, cohort_scale, lines, xpacks, ordered, 0, t_dev, after)
    mine, _ = spread_call(n, cohort_scale, lines, xpacks, ordered, t_dev, t_dev, after)
    out, weights, cell_scale = last_call(mine, core(away), weights, cell_scale)
    return (weights.reshape(-1), cell_scale.reshape(-1), out)


def solution(mesh):
    return jax.shard_map(
        functools.partial(per_device, mesh.shape["cohort"], mesh.shape["cell"]),
        mesh=mesh,
        in_specs=(
            P("cohort", None),
            P("cell", None),
            P("cohort"),
            P("cell"),
            P(),
            P("cohort"),
            P("cell"),
            P("cohort"),
            P("cohort", "cell"),
            P("cohort", "cell"),
            P("cohort", "cell"),
        ),
        out_specs=(P("cohort"), P("cell"), P("cohort", None, "cell")),
        check_vma=False,
    )
```
